32 devices in a mesh: ctx: 16 (over z, y, core), fsdp: 2 (over x).
Axes of the slice: x: 2, y: 2, z: 4, core: 2. Of those that a mesh axis runs over, the one named last changes fastest.
Arguments:
- outer_gate: bfloat16 [8192, 2048], P('ctx', 'fsdp'), may hold values from -6 to 6
- inner_gate: bfloat16 [8192, 2048], P('ctx', 'fsdp'), may hold values from -6 to 6
- values: bfloat16 [8192, 2048], P('ctx', 'fsdp'), may hold values from -6 to 6
- out_weight: bfloat16 [2048, 2048], P('ctx', 'fsdp'), may hold values from -0.125 to 0.125
- skip_gain: float32 [2048], P('fsdp'), may hold values from 0.25 to 1.5
- residues: float32 [2048, 16], P('fsdp')
- decay_rates: float32 [2048, 16], P('fsdp')
- out_grad: bfloat16 [8192, 2048], P('ctx', 'fsdp'), may hold values from -6 to 6
Outputs:
- block_out: bfloat16 [8192, 2048], P('ctx', 'fsdp')
- outer_grad: bfloat16 [8192, 2048], P('ctx', 'fsdp')
- inner_grad: bfloat16 [8192, 2048], P('ctx', 'fsdp')
- value_grad: bfloat16 [8192, 2048], P('ctx', 'fsdp')
- weight_grad: float32 [2048, 2048], P('ctx', 'fsdp')
The draws below stay inside these ranges and needn't reach their ends.
All inputs are finite; a program needn't handle non-finite values.
Results may differ from the reference program's by a relative error of at most 0.011.
Values may be sent and summed in bfloat16 or wider, within the bound.
A program may use at most 192 MiB of HBM per device.

```python
import math
import jax
import jax.numpy as jnp
from jax import lax

WIDTH = 2048
FEATURES = 2048
MODES = 16
LENGTH = 8192
N_FSDP = 2


def mode_pair(key):
    folded = jax.random.fold_in(key, 11)
    pick_key, slow_key, fast_key, spread_key = jax.random.split(folded, 4)
    slow_share = 0.5
    chosen = jax.random.uniform(pick_key, (WIDTH, MODES), jnp.float32) < slow_share
    slow_rates = jnp.exp(jax.random.uniform(slow_key, (WIDTH, MODES), jnp.float32, minval=math.log(0.2 / LENGTH), maxval=math.log(2.0 / LENGTH)))
    fast_rates = jnp.exp(jax.random.uniform(fast_key, (WIDTH, MODES), jnp.float32, minval=math.log(1.0 / 50.0), maxval=math.log(1.0 / 30.0)))
    all_rates = jnp.where(chosen, slow_rates, fast_rates)
    spread = jnp.clip(jax.random.normal(spread_key, (WIDTH, MODES), jnp.float32), -3.0, 3.0)
    residue = spread * jnp.sqrt(2.0 * all_rates / MODES)
    return (all_rates, residue)


def draw_decay_rates(key, part):
    return mode_pair(key)[0]


def draw_residues(key, part):
    return mode_pair(key)[1]


def block_scale(rng, extent, shards, least, high):
    level, own = 1.0, jax.random.fold_in(rng, 6)
    for axis_at, blocks in shards:
        steps = jnp.exp(jax.random.uniform(jax.random.fold_in(own, axis_at), (blocks,), jnp.float32, least / len(shards), high / len(shards)))
        level = level * jnp.repeat(steps, extent[axis_at] // blocks).reshape([-1 if axis == axis_at else 1 for axis in range(len(extent))])
    return level


def noise(stream_key, extent, deviation, most, shards=(), kind=jnp.bfloat16):
    factor_of = block_scale(stream_key, extent, shards, -0.22, 0.18) if shards else 1.0
    array = jax.random.normal(stream_key, extent, jnp.float32) * deviation * factor_of
    return jnp.minimum(jnp.maximum(array, -most), most).astype(kind)


def setup_inputs(seed: int = 0) -> dict:
    keys = jax.random.split(jax.random.key(seed), 9)
    outer_gate = noise(keys[0], (LENGTH, WIDTH), 1.0, 6.0, ((0, 16), (1, 2)))
    inner_gate = noise(keys[1], (LENGTH, WIDTH), 1.0, 6.0, ((0, 16), (1, 2)))
    values = noise(keys[2], (LENGTH, WIDTH), 1.0, 6.0, ((0, 16), (1, 2)))
    out_weight = noise(keys[3], (WIDTH, FEATURES), WIDTH ** -0.5, 0.125, ((0, 16), (1, 2)))
    skip_gain = jnp.clip(0.25 + 1.25 * jax.random.uniform(keys[4], (WIDTH,), jnp.float32) ** block_scale(keys[4], (WIDTH,), ((0, 2),), -0.2, 0.2), 0.25, 1.5)
    residues = draw_residues(jax.random.fold_in(keys[8], 71), 0)
    decay_rates = draw_decay_rates(jax.random.fold_in(keys[8], 71), 0)
    out_grad = noise(keys[7], (LENGTH, FEATURES), 1.0, 6.0, ((0, 16), (1, 2)))
    return dict(outer_gate=outer_gate, inner_gate=inner_gate, values=values, out_weight=out_weight, skip_gain=skip_gain, residues=residues, decay_rates=decay_rates, out_grad=out_grad)


def mode_tables(residues, decay_rates, row_count):
    block_rows = min(64, row_count)
    lag_steps = jnp.arange(block_rows, dtype=jnp.float32)
    lag_index = jnp.arange(block_rows)[:, None] - jnp.arange(block_rows)[None, :]
    kernel = lax.optimization_barrier(jnp.sum(residues[:, :, None] * jnp.exp(-decay_rates[:, :, None] * lag_steps[None, None, :]), axis=1))
    picked = kernel[:, jnp.clip(lag_index, 0, block_rows - 1)]
    toeplitz = jnp.where((lag_index >= 0)[None], picked, jnp.zeros_like(picked))
    rise_table = jnp.exp(-decay_rates[None] * (lag_steps[:, None, None] + 1.0))
    tail_table = jnp.exp(-decay_rates[None] * (block_rows - 1.0 - lag_steps)[:, None, None])
    return (block_rows, toeplitz, rise_table, tail_table)

def local_forward(inputs, decay_rates, tables):
    block_rows, toeplitz, rise_table, tail_table = tables
    blocks = inputs.shape[0] // block_rows
    shaped = inputs.reshape(blocks, block_rows, inputs.shape[1])
    inner_part = jnp.einsum('cts,nsc->ntc', toeplitz, shaped, precision=lax.Precision.HIGHEST)
    end_terms = jnp.einsum('nsc,scr->ncr', shaped, tail_table, precision=lax.Precision.HIGHEST)
    step_decay = jnp.exp(-decay_rates * block_rows)

    def advance(running, end_term):
        return (step_decay * running + end_term, running)
    end_state, befores = lax.scan(advance, jnp.zeros(decay_rates.shape, jnp.float32), end_terms)
    return (inner_part, befores, end_state)

def finish_forward(inner_part, befores, incoming, residues, decay_rates, tables):
    block_rows, toeplitz, rise_table, tail_table = tables
    blocks = inner_part.shape[0]
    offsets = block_rows * jnp.arange(blocks, dtype=jnp.float32)
    powers = jnp.exp(-decay_rates[None] * offsets[:, None, None])
    states = befores + powers * incoming[None]
    cross_part = jnp.einsum('tcr,ncr->ntc', rise_table * residues[None], states, precision=lax.Precision.HIGHEST)
    total = inner_part + cross_part
    return total.reshape(blocks * block_rows, total.shape[2])

def local_backward(grads, decay_rates, tables):
    block_rows, toeplitz, rise_table, tail_table = tables
    blocks = grads.shape[0] // block_rows
    shaped = grads.reshape(blocks, block_rows, grads.shape[1])
    inner_part = jnp.einsum('cts,ntc->nsc', toeplitz, shaped, precision=lax.Precision.HIGHEST)
    start_terms = jnp.einsum('ntc,tcr->ncr', shaped, rise_table, precision=lax.Precision.HIGHEST)
    step_decay = jnp.exp(-decay_rates * block_rows)

    def retreat(running, start_term):
        return (step_decay * running + start_term, running)
    start_state, afters = lax.scan(retreat, jnp.zeros(decay_rates.shape, jnp.float32), start_terms, reverse=True)
    return (inner_part, afters, start_state)

def finish_backward(inner_part, afters, outgoing, residues, decay_rates, tables):
    block_rows, toeplitz, rise_table, tail_table = tables
    blocks = inner_part.shape[0]
    offsets = block_rows * (blocks - 1.0 - jnp.arange(blocks, dtype=jnp.float32))
    powers = jnp.exp(-decay_rates[None] * offsets[:, None, None])
    states = afters + powers * outgoing[None]
    cross_part = jnp.einsum('scr,ncr->nsc', tail_table * residues[None], states, precision=lax.Precision.HIGHEST)
    total = inner_part + cross_part
    return total.reshape(blocks * block_rows, total.shape[2])

def reference(outer_gate, inner_gate, values, out_weight, skip_gain, residues, decay_rates, out_grad):
    row_count = outer_gate.shape[0]
    tables = mode_tables(residues, decay_rates, row_count)
    zero_state = jnp.zeros(decay_rates.shape, jnp.float32)
    gated = inner_gate.astype(jnp.float32) * values.astype(jnp.float32)
    inner_part, befores, end_state = local_forward(gated, decay_rates, tables)
    filtered = finish_forward(inner_part, befores, zero_state, residues, decay_rates, tables) + skip_gain[None] * gated
    modulated = (outer_gate.astype(jnp.float32) * filtered).astype(jnp.bfloat16)
    block_out = jnp.dot(modulated, out_weight, preferred_element_type=jnp.float32).astype(jnp.bfloat16)
    block_cols = FEATURES // N_FSDP
    modulated_grad = jnp.zeros(modulated.shape, jnp.float32)
    for member in range(N_FSDP):
        first_col = member * block_cols
        partial_term = jnp.dot(out_grad[:, first_col:first_col + block_cols], out_weight[:, first_col:first_col + block_cols].T, preferred_element_type=jnp.float32)
        rounded = lax.optimization_barrier(partial_term.astype(jnp.bfloat16))
        modulated_grad = modulated_grad + rounded.astype(jnp.float32)
    outer_grad = (modulated_grad * filtered).astype(jnp.bfloat16)
    filtered_grad = modulated_grad * outer_gate.astype(jnp.float32)
    inner_back, afters, start_state = local_backward(filtered_grad, decay_rates, tables)
    gated_grad = finish_backward(inner_back, afters, zero_state, residues, decay_rates, tables) + skip_gain[None] * filtered_grad
    inner_grad = (gated_grad * values.astype(jnp.float32)).astype(jnp.bfloat16)
    value_grad = (gated_grad * inner_gate.astype(jnp.float32)).astype(jnp.bfloat16)
    weight_grad = jnp.dot(modulated.T, out_grad, preferred_element_type=jnp.float32) * (1.0 / math.sqrt(LENGTH))
    return (block_out, outer_grad, inner_grad, value_grad, weight_grad)
```

```python
import functools
import math

import jax
import jax.numpy as jnp
from jax import lax
from jax.experimental import pallas as pl
from jax.experimental.pallas import tpu as pltpu
from jax.sharding import PartitionSpec as P

F32 = jnp.float32
BF16 = jnp.bfloat16
LANES = 128
SEGS = 8
VMEM_BYTES = 62 * 2**20


def rows_at(i, steps):
    return pl.ds(i, SEGS, stride=steps)


def spread(row):
    return jnp.broadcast_to(row, (SEGS, LANES))


def segment_states(u_scr, decay_ref, pre_ref, end_ref, reverse):
    modes = decay_ref.shape[0]
    steps = u_scr.shape[0] // SEGS
    a = [spread(jnp.exp(-decay_ref[r : r + 1, :])) for r in range(modes)]

    def step(k, states):
        i = steps - 1 - k if reverse else k
        u = u_scr[rows_at(i, steps), :]
        return tuple(a[r] * states[r] + u for r in range(modes))

    zero = jnp.zeros((SEGS, LANES), F32)
    states = lax.fori_loop(0, steps, step, (zero,) * modes, unroll=4)
    seg = lax.broadcasted_iota(jnp.int32, (SEGS, LANES), 0)

    def moved(x, by):
        if reverse:
            return jnp.where(seg < SEGS - by, pltpu.roll(x, SEGS - by, 0), 0.0)
        return jnp.where(seg >= by, pltpu.roll(x, by, 0), 0.0)

    last = 0 if reverse else SEGS - 1
    for r in range(modes):
        rate = spread(decay_ref[r : r + 1, :])
        x = states[r]
        for by in (1, 2, 4):
            x = x + jnp.exp(-rate * float(steps * by)) * moved(x, by)
        end_ref[r : r + 1, :] = x[last : last + 1, :]
        pre_ref[r] = moved(x, 1)


def full_scan(u_scr, y_scr, decay_ref, res_ref, pre_ref, incoming_ref, reverse):
    modes = decay_ref.shape[0]
    rows = u_scr.shape[0]
    steps = rows // SEGS
    seg = lax.broadcasted_iota(jnp.int32, (SEGS, LANES), 0)
    ahead = ((SEGS - 1 - seg if reverse else seg) * steps).astype(F32)
    a = []
    first = []
    for r in range(modes):
        rate = spread(decay_ref[r : r + 1, :])
        a.append(jnp.exp(-rate))
        first.append(pre_ref[r] + jnp.exp(-rate * ahead) * incoming_ref[r : r + 1, :])
    res = [spread(res_ref[r : r + 1, :]) for r in range(modes)]

    def step(k, states):
        i = steps - 1 - k if reverse else k
        u = u_scr[rows_at(i, steps), :]
        states = tuple(a[r] * states[r] + u for r in range(modes))
        terms = [res[r] * states[r] for r in range(modes)]
        while len(terms) > 1:
            terms = [p + q for p, q in zip(terms[::2], terms[1::2])]
        y_scr[rows_at(i, steps), :] = terms[0]
        return states

    lax.fori_loop(0, steps, step, tuple(first), unroll=2)


def forward_ends(inner_ref, values_ref, decay_ref, pre_ref, end_ref, u_scr):
    u_scr[...] = inner_ref[...].astype(F32) * values_ref[...].astype(F32)
    segment_states(u_scr, decay_ref, pre_ref, end_ref, False)


def forward_finish(
    inner_ref, values_ref, outer_ref, decay_ref, res_ref, skip_ref, pre_ref, incoming_ref,
    filtered_ref, modulated_ref, u_scr, y_scr,
):
    u_scr[...] = inner_ref[...].astype(F32) * values_ref[...].astype(F32)
    full_scan(u_scr, y_scr, decay_ref, res_ref, pre_ref, incoming_ref, False)
    filtered = y_scr[...] + skip_ref[...] * u_scr[...]
    filtered_ref[...] = filtered
    modulated_ref[...] = (outer_ref[...].astype(F32) * filtered).astype(BF16)


def backward_ends(own_ref, other_ref, outer_ref, decay_ref, pre_ref, end_ref, u_scr):
    grad = own_ref[...].astype(F32) + other_ref[...].astype(F32)
    u_scr[...] = grad * outer_ref[...].astype(F32)
    segment_states(u_scr, decay_ref, pre_ref, end_ref, True)


def backward_finish(
    own_ref, other_ref, outer_ref, inner_ref, values_ref, filtered_ref, decay_ref, res_ref, skip_ref,
    pre_ref, incoming_ref, outer_grad_ref, inner_grad_ref, value_grad_ref, u_scr, y_scr,
):
    grad = own_ref[...].astype(F32) + other_ref[...].astype(F32)
    u_scr[...] = grad * outer_ref[...].astype(F32)
    outer_grad_ref[...] = (grad * filtered_ref[...]).astype(BF16)
    full_scan(u_scr, y_scr, decay_ref, res_ref, pre_ref, incoming_ref, True)
    gated_grad = y_scr[...] + skip_ref[...] * u_scr[...]
    inner_grad_ref[...] = (gated_grad * values_ref[...].astype(F32)).astype(BF16)
    value_grad_ref[...] = (gated_grad * inner_ref[...].astype(F32)).astype(BF16)


def by_lanes(kernel, operands, outs, rows, scans):
    channels = operands[0].shape[-1]

    def spec(x):
        lead = x.shape[:-1]
        return pl.BlockSpec(lead + (LANES,), lambda c, n=len(lead): (0,) * n + (c,))

    work = rows * channels * (24000 if scans > 1 else 16000)
    moved = sum(math.prod(x.shape) * x.dtype.itemsize for x in list(operands) + list(outs))
    return pl.pallas_call(
        kernel,
        grid=(channels // LANES,),
        out_shape=outs,
        in_specs=[spec(x) for x in operands],
        out_specs=[spec(x) for x in outs],
        scratch_shapes=[pltpu.VMEM((rows, LANES), F32)] * scans,
        cost_estimate=pl.CostEstimate(flops=work, bytes_accessed=moved, transcendentals=0),
        name=kernel.__name__,
    )(*operands)


def prefix_kernel(reverse, rows, end_ref, decay_ref, out_ref, sent, got, send_sem, recv_sem):
    me, n = lax.axis_index("ctx"), lax.axis_size("ctx")
    hops = [1 << k for k in range(sent.shape[0])]
    barrier = pltpu.get_barrier_semaphore()
    for hop in hops:
        for peer in (lax.rem(me + hop, n), lax.rem(me + n - hop, n)):
            pl.semaphore_signal(
                barrier, inc=1, device_id={"ctx": peer}, device_id_type=pl.DeviceIdType.MESH
            )
    pl.semaphore_wait(barrier, 2 * len(hops))
    decay = decay_ref[...]
    upto = end_ref[...]
    before = jnp.zeros_like(upto)
    for k, hop in enumerate(hops):
        sent[k] = upto.astype(BF16)
        copy = pltpu.make_async_remote_copy(
            src_ref=sent.at[k],
            dst_ref=got.at[k],
            send_sem=send_sem.at[k],
            recv_sem=recv_sem.at[k],
            device_id={"ctx": lax.rem(me + (n - hop if reverse else hop), n)},
            device_id_type=pl.DeviceIdType.MESH,
        )
        copy.start()
        near = jnp.exp(-decay * float(rows * (hop - 1)))
        far = jnp.exp(-decay * float(rows * hop))
        copy.wait()
        inside = (me + hop < n) if reverse else (me >= hop)
        term = got[k].astype(F32) * jnp.where(inside, 1.0, 0.0)
        before = before + near * term
        upto = upto + far * term
    out_ref[...] = before


def prefix(end, decay, rows, reverse):
    hops = max(1, (lax.axis_size("ctx") - 1).bit_length())
    whole = pl.BlockSpec(memory_space=pltpu.VMEM)
    return pl.pallas_call(
        functools.partial(prefix_kernel, reverse, rows),
        out_shape=jax.ShapeDtypeStruct(end.shape, F32),
        in_specs=[whole, whole],
        out_specs=whole,
        scratch_shapes=[
            pltpu.VMEM((hops,) + end.shape, BF16),
            pltpu.VMEM((hops,) + end.shape, BF16),
            pltpu.SemaphoreType.DMA((hops,)),
            pltpu.SemaphoreType.DMA((hops,)),
        ],
        compiler_params=pltpu.CompilerParams(
            collective_id=2 if reverse else 1, has_side_effects=True
        ),
        cost_estimate=pl.CostEstimate(flops=18 * 10**9, bytes_accessed=0, transcendentals=0),
        name="prefix_back" if reverse else "prefix_ahead",
    )(end, decay)


def shards(outer_gate, inner_gate, values, out_weight, skip_gain, residues, decay_rates, out_grad):
    rows, channels = values.shape
    modes = decay_rates.shape[1]
    ctx, fsdp = lax.axis_size("ctx"), lax.axis_size("fsdp")
    at = lax.axis_index("fsdp")
    swap = [(0, 1), (1, 0)]
    shape = jax.ShapeDtypeStruct
    panel = lax.all_gather(out_weight, "ctx", axis=0, tiled=True)
    decay = decay_rates.T
    res = residues.T
    skip = skip_gain[None]
    state_outs = [shape((modes, SEGS, channels), F32), shape((modes, channels), F32)]
    pre, end = by_lanes(forward_ends, (inner_gate, values, decay), state_outs, rows, 1)
    incoming = prefix(end, decay, rows, False)
    filtered, modulated = by_lanes(
        forward_finish,
        (inner_gate, values, outer_gate, decay, res, skip, pre, incoming),
        [shape((rows, channels), F32), shape((rows, channels), BF16)],
        rows,
        2,
    )
    if fsdp == 2:
        other = lax.ppermute(modulated, "fsdp", swap)
        first = jnp.where(at == 0, modulated, other)
        second = jnp.where(at == 0, other, modulated)
        gathered = jnp.concatenate([first, second], axis=1)
        mine = lax.dynamic_slice_in_dim(panel, at * channels, channels, 0)
        theirs = lax.dynamic_slice_in_dim(panel, (1 - at) * channels, channels, 0)
        for_them = jnp.dot(out_grad, theirs.T, preferred_element_type=F32).astype(BF16)
        from_them = lax.ppermute(for_them, "fsdp", swap)
        own = jnp.dot(out_grad, mine.T, preferred_element_type=F32).astype(BF16)
    else:
        gathered = lax.all_gather(modulated, "fsdp", axis=1, tiled=True)
        partial = jnp.dot(out_grad, panel.T, preferred_element_type=F32).astype(BF16)
        own = lax.psum_scatter(partial, "fsdp", scatter_dimension=1, tiled=True)
        from_them = jnp.zeros_like(own)
    grad_rows = lax.dot_general(
        gathered, out_grad, (((0,), (0,)), ((), ())), preferred_element_type=F32
    ).astype(BF16)
    weight_grad = lax.psum_scatter(grad_rows, "ctx", scatter_dimension=0, tiled=True)
    block_out = jnp.dot(gathered, panel, preferred_element_type=F32).astype(BF16)
    pre, end = by_lanes(
        backward_ends, (own, from_them, outer_gate, decay), state_outs, rows, 1
    )
    incoming = prefix(end, decay, rows, True)
    outer_grad, inner_grad, value_grad = by_lanes(
        backward_finish,
        (own, from_them, outer_gate, inner_gate, values, filtered, decay, res, skip, pre, incoming),
        [shape((rows, channels), BF16)] * 3,
        rows,
        2,
    )
    weight_grad, value_grad = lax.optimization_barrier((weight_grad, value_grad))
    weight_grad = weight_grad.astype(F32) * (1.0 / math.sqrt(rows * ctx))
    return (block_out, outer_grad, inner_grad, value_grad, weight_grad)


TAPS = 16
GRAN = 16
PER = LANES // GRAN
WIDE = TAPS * GRAN
SUB = 2
PIECES = 4
MESH = pl.DeviceIdType.MESH
ORDER = ((1, True), (0, True), (1, False), (0, False))


def regroup(v):
    lane = lax.broadcasted_iota(jnp.int32, v[0].shape, 1) // GRAN
    v = list(v)
    for m in (1, 2, 4):
        low = (lane & m) == 0
        for i in range(PER):
            if i & m:
                continue
            p, q = v[i], v[i + m]
            v[i] = jnp.where(low, p, pltpu.roll(q, GRAN * m, 1))
            v[i + m] = jnp.where(low, pltpu.roll(p, LANES - GRAN * m, 1), q)
    return v


def row_at(k, s, steps, reverse):
    return TAPS * (steps - 1 - k) + TAPS - 1 - s if reverse else TAPS * k + s


def regroup_filters(decay_ref, res_ref, skip_ref, par_ref, gen_ref):
    row = lax.broadcasted_iota(jnp.int32, (SEGS, LANES), 0)
    lag = lax.broadcasted_iota(jnp.int32, (TAPS, LANES), 0)
    lags = lag.astype(F32)

    def block(b, _):
        cols = pl.ds(pl.multiple_of(b * LANES, LANES), LANES)
        kern = jnp.where(lag == 0, jnp.broadcast_to(skip_ref[:, cols], (TAPS, LANES)), 0.0)
        for r in range(TAPS):
            kern = kern + res_ref[r : r + 1, cols] * jnp.exp(-decay_ref[r : r + 1, cols] * lags)
        gen_ref[...] = kern
        for half in range(2):
            v = []
            for s in range(half * PER, (half + 1) * PER):
                rate = jnp.broadcast_to(decay_ref[s : s + 1, cols], (SEGS, LANES))
                res = jnp.broadcast_to(res_ref[s : s + 1, cols], (SEGS, LANES))
                tap = jnp.broadcast_to(gen_ref[s : s + 1, :], (SEGS, LANES))
                v.append(jnp.where(row == 0, rate, jnp.where(row == 1, res, tap)))
            for h, out in enumerate(regroup(v)):
                par_ref[b * PER + h, :, half * LANES : (half + 1) * LANES] = out
        return 0

    lax.fori_loop(0, decay_ref.shape[1] // LANES, block, 0)


def build_tables(par_ref, rate_ref, taps_ref, tail_ref, rise_ref, toep_ref, first, groups):
    shape = (GRAN, WIDE)
    diagonal = lax.broadcasted_iota(jnp.int32, shape, 1) % GRAN == lax.broadcasted_iota(jnp.int32, shape, 0)
    lag = lax.broadcasted_iota(jnp.int32, (TAPS, WIDE), 0)
    lags = lag.astype(F32)
    at = lax.broadcasted_iota(jnp.int32, (TAPS, WIDE), 1) // GRAN

    def group(g, _):
        rate = par_ref[g, 0:1, :]
        res = par_ref[g, 1:2, :]
        kern = jnp.broadcast_to(par_ref[g, 2:3, :], (TAPS, WIDE))
        rate_ref[pl.ds(g, 1), :] = rate
        taps_ref[0] = jnp.exp(-rate * (TAPS - 1 - lags))
        taps_ref[1] = res * jnp.exp(-rate * (lags + 1))
        taps_ref[2] = jnp.where(at >= lag, pltpu.roll(kern, 0, 1, stride=GRAN, stride_axis=0), 0.0)
        for i, out in enumerate((tail_ref, rise_ref, toep_ref)):
            for s in range(TAPS):
                line = jnp.broadcast_to(taps_ref[i, s : s + 1, :], shape)
                out[g, s * GRAN : (s + 1) * GRAN, :] = jnp.where(diagonal, line, 0.0).astype(BF16)
        return 0

    lax.fori_loop(first, first + groups, group, 0)


def moved(x, by, reverse):
    seg = lax.broadcasted_iota(jnp.int32, x.shape, 0)
    if reverse:
        return jnp.where(seg < SEGS - by, pltpu.roll(x, SEGS - by, 0), 0.0)
    return jnp.where(seg >= by, pltpu.roll(x, by, 0), 0.0)


def chunks_in(u_ref, z_ref, reverse):
    blocks, rows, _ = u_ref.shape
    stride = rows // SEGS
    steps = stride // TAPS

    def block(b, _):
        for half in range(2):
            for k in range(0, steps, 2):
                pair = [
                    regroup(
                        [
                            u_ref[b, pl.ds(row_at(n, half * PER + j, steps, reverse), SEGS, stride=stride), :]
                            for j in range(PER)
                        ]
                    )
                    for n in (k, k + 1)
                ]
                for h in range(PER):
                    z_ref[b * PER + h, k * SEGS : (k + 2) * SEGS, half * LANES : (half + 1) * LANES] = (
                        jnp.concatenate([pair[0][h], pair[1][h]], axis=0).astype(BF16)
                    )
        return 0

    lax.fori_loop(0, blocks, block, 0)


def chunk_ends(z_ref, tail_ref, rate_ref, e_ref, pre_ref, end_ref, reverse):
    groups, chunks, _ = z_ref.shape
    steps = chunks // SEGS
    last = 0 if reverse else SEGS - 1

    def group(g, _):
        e = jnp.dot(z_ref[g], tail_ref[g], preferred_element_type=F32)
        e_ref[g] = e
        rate = jnp.broadcast_to(rate_ref[pl.ds(g, 1), :], (SEGS, WIDE))
        a = jnp.exp(-rate * float(TAPS))
        x = e[0:SEGS]
        for k in range(1, steps):
            x = a * x + e[k * SEGS : (k + 1) * SEGS]
        for by in (1, 2, 4):
            x = x + jnp.exp(-rate * float(TAPS * steps * by)) * moved(x, by, reverse)
        end_ref[pl.ds(g, 1), :] = x[last : last + 1, :]
        pre_ref[g] = moved(x, 1, reverse)
        return 0

    lax.fori_loop(0, groups, group, 0, unroll=8)


def chunk_finish(z_ref, toep_ref, rise_ref, rate_ref, e_ref, pre_ref, inc_ref, y_ref, reverse):
    groups, chunks, _ = z_ref.shape
    steps = chunks // SEGS
    stride = y_ref.shape[1] // SEGS
    seg = lax.broadcasted_iota(jnp.int32, (SEGS, WIDE), 0)
    ahead = ((SEGS - 1 - seg if reverse else seg) * (TAPS * steps)).astype(F32)

    def group(g, _):
        rate = jnp.broadcast_to(rate_ref[pl.ds(g, 1), :], (SEGS, WIDE))
        a = jnp.exp(-rate * float(TAPS))
        x = pre_ref[g] + jnp.exp(-rate * ahead) * inc_ref[pl.ds(g, 1), :]
        states = [x]
        for k in range(steps - 1):
            x = a * x + e_ref[g, k * SEGS : (k + 1) * SEGS]
            states.append(x)
        s = jnp.concatenate(states, axis=0).astype(BF16)
        y = jnp.dot(z_ref[g], toep_ref[g], preferred_element_type=F32)
        e_ref[g] = y + lax.dot_general(s, rise_ref[g], (((1,), (1,)), ((), ())), preferred_element_type=F32)
        return 0

    lax.fori_loop(0, groups, group, 0, unroll=8)

    def block(b, _):
        for half in range(2):
            for k in range(steps):
                v = regroup(
                    [
                        e_ref[b * PER + h, k * SEGS : (k + 1) * SEGS, half * LANES : (half + 1) * LANES]
                        for h in range(PER)
                    ]
                )
                for j in range(PER):
                    y_ref[b, pl.ds(row_at(k, half * PER + j, steps, reverse), SEGS, stride=stride), :] = v[j]
        return 0

    lax.fori_loop(0, groups // PER, block, 0)


def fused_scratch(rows, channels):
    blocks, groups = channels // LANES, channels // GRAN
    chunks = rows // TAPS
    part = channels // 8
    dma = pltpu.SemaphoreType.DMA
    v = pltpu.VMEM
    return dict(
        tail=v((groups, WIDE, WIDE), BF16),
        rise=v((groups, WIDE, WIDE), BF16),
        toep=v((groups, WIDE, WIDE), BF16),
        par=v((groups, SEGS, WIDE), F32),
        rate=v((groups, WIDE), F32),
        taps=v((3, TAPS, WIDE), F32),
        gen=v((TAPS, LANES), F32),
        inner=v((rows, channels), BF16),
        values=v((rows, channels), BF16),
        outer=v((rows, channels), BF16),
        og=v((2, rows, channels), BF16),
        w=v((2, 8, part, channels), BF16),
        u=v((blocks, rows, LANES), F32),
        y=v((blocks, rows, LANES), F32),
        z=v((groups, chunks, WIDE), BF16),
        e=v((groups, chunks, WIDE), F32),
        pre=v((groups, SEGS, WIDE), F32),
        end=v((groups, WIDE), F32),
        before=v((groups, WIDE), F32),
        inc=v((groups, WIDE), F32),
        near=v((2, 4, groups, WIDE), BF16),
        total=v((2, groups, WIDE), BF16),
        far=v((2, 4, groups, WIDE), BF16),
        mod=v((rows, channels), BF16),
        modt=v((channels, rows), BF16),
        bs=v((PIECES, rows, channels // PIECES), BF16),
        br=v((PIECES, rows, channels // PIECES), BF16),
        bo=v((rows, channels), BF16),
        part=v((2, 8, part, channels), BF16),
        rc=v((4, 2, part, channels), BF16),
        ys=v((4, part, channels), BF16),
        ry=v((4, part, channels), BF16),
        zs=v((4, part, channels), BF16),
        rz=v((4, part, channels), BF16),
        rb=v((2, part, channels), BF16),
        wx=v((part, channels), BF16),
        wo=v((part, channels), F32),
        load=dma((5,)),
        store=dma((PIECES + 4,)),
        og_s=dma((PIECES,)),
        og_r=dma((PIECES,)),
        wx_s=dma((SUB,)),
        w_r=dma((2, 8, SUB)),
        up_s=dma((4, SUB)),
        down_s=dma((4, SUB)),
        y_s=dma((4, SUB)),
        c_s=dma((4, SUB)),
        cy_s=dma((4, SUB)),
        near_s=dma((2, 4)),
        near_r=dma((2, 4)),
        far_s=dma((2, 4)),
        far_r=dma((2, 4)),
        b_s=dma((PIECES,)),
        b_r=dma((PIECES,)),
        rc_s=dma((4, 2)),
        rc_r=dma((4, 2)),
        ry_s=dma((4, SUB)),
        ry_r=dma((4, SUB)),
        rz_s=dma((4, SUB)),
        rz_r=dma((4, SUB)),
        rb_r=dma((2, SUB)),
        fx_s=dma((SUB,)),
        fx_r=dma((SUB,)),
    )


def fused_kernel(names, length, *refs):
    decay, res, skip, outer_in, inner_in, values_in, weight_in, grad_in = refs[:8]
    block_out, outer_out, inner_out, value_out, weight_out = refs[8:13]
    s = dict(zip(names, refs[13:]))
    rows, channels = inner_in.shape
    part = weight_in.shape[0]
    blocks = channels // LANES
    groups = channels // GRAN
    fine = part // SUB
    i, x = lax.axis_index("ctx"), lax.axis_index("fsdp")
    z, y, c = i // 4, (i // 2) % 2, i % 2
    zm = jnp.where(x == 0, z, 3 - z)
    q = i % 4

    def ctx_at(z, y, c):
        return z * 4 + y * 2 + c

    up_to = ctx_at(z + 1 - 2 * x, y, c)
    down_to = ctx_at(z - 1 + 2 * x, y, c)
    y_to = ctx_at(z, 1 - y, c)
    c_to = ctx_at(z, y, 1 - c)

    def remote(src, dst, send, recv, ctx, fsdp=x):
        return pltpu.make_async_remote_copy(
            src_ref=src, dst_ref=dst, send_sem=send, recv_sem=recv,
            device_id={"ctx": ctx, "fsdp": fsdp}, device_id_type=MESH,
        )

    def when(cond):
        return pl.when(cond)

    loads = [
        pltpu.make_async_copy(inner_in, s["inner"], s["load"].at[0]),
        pltpu.make_async_copy(values_in, s["values"], s["load"].at[1]),
        pltpu.make_async_copy(outer_in, s["outer"], s["load"].at[2]),
        pltpu.make_async_copy(grad_in, s["og"].at[x], s["load"].at[3]),
    ]
    for copy in loads:
        copy.start()
    jown = (z % 2) * 4 + q
    source = zm < 2
    keep_w = pltpu.make_async_copy(weight_in, s["w"].at[x, jown], s["load"].at[4])
    when(source)(keep_w.start)
    s["far"][...] = jnp.zeros_like(s["far"])

    barrier = pltpu.get_barrier_semaphore()
    peers = [(ctx_at(z, (q + t) % 4 // 2, (q + t) % 2), x) for t in (1, 2, 3)]
    peers += [(ctx_at((z + t) % 4, y, c), x) for t in (1, 2, 3)] + [(i, 1 - x)]
    for ctx, fsdp in peers:
        pl.semaphore_signal(barrier, inc=1, device_id={"ctx": ctx, "fsdp": fsdp}, device_id_type=MESH)
    pl.semaphore_wait(barrier, len(peers))

    def fine_rows(t):
        return pl.ds(t * fine, fine)

    def spot(sidx, yy, cc):
        return jnp.where(x == 0, sidx, 1 - sidx) * 4 + yy * 2 + cc

    def side(own):
        return x if own else 1 - x

    def w_cross(t):
        return remote(
            weight_in.at[fine_rows(t)], s["w"].at[x, jown, fine_rows(t)], s["wx_s"].at[t],
            s["w_r"].at[x, jown, t], i, 1 - x,
        )

    def w_sends(src, g, j, k, t, up, down):
        dst = s["w"].at[g, j, fine_rows(t)]
        recv = s["w_r"].at[g, j, t]
        return [
            (up, remote(src, dst, s["up_s"].at[k, t], recv, up_to)),
            (down, remote(src, dst, s["down_s"].at[k, t], recv, down_to)),
            (None, remote(src, dst, s["y_s"].at[k, t], recv, y_to)),
            (None, remote(src, dst, s["c_s"].at[k, t], recv, c_to)),
        ]

    def each(sends, act):
        for cond, copy in sends:
            if cond is None:
                getattr(copy, act)()
            elif cond is not False:
                when(cond)(getattr(copy, act))

    def own_sends(t):
        return w_sends(weight_in.at[fine_rows(t)], x, jown, 1 - zm, t, None, zm == 1)

    def line_sends(k, t):
        sidx, own = ORDER[k]
        j, g = spot(sidx, y, c), side(own)
        src = s["w"].at[g, j, fine_rows(t)]
        if sidx == 0:
            up, down = zm < 3, False
        elif own:
            up, down = zm == 2, False
        else:
            up, down = (zm == 1) | (zm == 2), zm == 1
        return w_sends(src, g, j, k, t, up, down)

    def w_wait(g, j, t):
        dst = s["w"].at[g, j, fine_rows(t)]
        remote(dst, dst, s["wx_s"].at[t], s["w_r"].at[g, j, t], c_to).wait_recv()

    def pump_line(k, t):
        sidx, own = ORDER[k]

        def go():
            w_wait(side(own), spot(sidx, y, c), t)
            each(line_sends(k, t), "start")

        if own:
            when(zm != sidx)(go)
        else:
            go()

    def y_pass(k, t):
        sidx, own = ORDER[k]
        g, j = side(own), spot(sidx, 1 - y, c)
        at = s["w"].at[g, j, fine_rows(t)]
        return remote(at, at, s["cy_s"].at[k, t], s["w_r"].at[g, j, t], c_to)

    def pump_y(k, t):
        sidx, own = ORDER[k]
        w_wait(side(own), spot(sidx, 1 - y, c), t)
        y_pass(k, t).start()

    def w_rest():
        for k, (sidx, own) in enumerate(ORDER):
            for t in range(SUB):
                for yy in (0, 1):
                    w_wait(side(own), spot(sidx, yy, 1 - c), t)
        when(source)(keep_w.wait)

    def w_drain():
        def cross():
            for t in range(SUB):
                w_cross(t).wait_send()

        def owned():
            for t in range(SUB):
                each(own_sends(t), "wait_send")

        when(zm >= 2)(cross)
        when(source)(owned)
        for k, (sidx, own) in enumerate(ORDER):
            for t in range(SUB):
                if own:
                    when(zm != sidx)(functools.partial(each, line_sends(k, t), "wait_send"))
                else:
                    each(line_sends(k, t), "wait_send")
                y_pass(k, t).wait_send()

    def start_cross():
        for t in range(SUB):
            w_cross(t).start()

    def start_owned():
        for t in range(SUB):
            each(own_sends(t), "start")

    when(zm >= 2)(start_cross)
    when(source)(start_owned)

    slab = rows // PIECES

    def og_copy(n):
        return remote(
            grad_in.at[pl.ds(n * slab, slab)], s["og"].at[x, pl.ds(n * slab, slab)],
            s["og_s"].at[n], s["og_r"].at[n], i, 1 - x,
        )

    for n in range(PIECES):
        og_copy(n).start()

    pumps = [(pump_line, k, t) for k in range(4) for t in range(SUB)]
    lagged = [(pump_y, k, t) for k in range(4) for t in range(SUB)]
    order = []
    for n in range(len(pumps) + 1):
        if n < len(pumps):
            order.append(pumps[n])
        if n >= 1:
            order.append(lagged[n - 1])
    todo = iter(order)

    def pump(n):
        for _ in range(n):
            step = next(todo, None)
            if step is not None:
                step[0](*step[1:])

    def rate():
        return s["rate"][...]

    def near_copy(d, t):
        to = (q + t) % 4
        at = s["near"].at[d, q]
        return remote(at, at, s["near_s"].at[d, t], s["near_r"].at[d, q], ctx_at(z, to // 2, to % 2))

    def near_wait(d, t):
        frm = (q + t) % 4
        at = s["near"].at[d, frm]
        remote(at, at, s["near_s"].at[d, t], s["near_r"].at[d, frm], c_to).wait_recv()

    def far_copy(d, t):
        to = z + t if d == 0 else z - t
        at = s["far"].at[d, z]
        return remote(s["total"].at[d], at, s["far_s"].at[d, t], s["far_r"].at[d, z], ctx_at(to, y, c))

    def far_sends(d, act):
        for t in (1, 2, 3):
            cond = z + t < 4 if d == 0 else z - t >= 0
            when(cond)(getattr(far_copy(d, t), act))

    def near_start(d):
        s["near"][d, q] = s["end"][...].astype(BF16)
        for t in (1, 2, 3):
            near_copy(d, t).start()

    def near_finish(d):
        for t in (1, 2, 3):
            near_wait(d, t)
        total = jnp.zeros((groups, WIDE), F32)
        before = jnp.zeros((groups, WIDE), F32)
        mine = q if d == 0 else 3 - q
        for k in range(4):
            rank = k if d == 0 else 3 - k
            term = s["near"][d, k].astype(F32)
            total = total + jnp.exp(-rate() * float(rows * (3 - rank))) * term
            gap = mine - rank
            weight = jnp.exp(-rate() * (rows * jnp.maximum(gap - 1, 0)).astype(F32))
            before = before + jnp.where(gap > 0, weight, 0.0) * term
        s["before"][...] = before
        s["total"][d] = total.astype(BF16)
        far_sends(d, "start")

    def far_finish(d):
        for t in (1, 2, 3):
            frm = z - t if d == 0 else z + t
            at = s["far"].at[d, frm]
            copy = remote(at, at, s["far_s"].at[d, t], s["far_r"].at[d, frm], c_to)
            when(z - t >= 0 if d == 0 else z + t < 4)(copy.wait_recv)
        into = jnp.zeros((groups, WIDE), F32)
        for k in range(4):
            gap = z - k if d == 0 else k - z
            weight = jnp.exp(-rate() * (4 * rows * jnp.maximum(gap - 1, 0)).astype(F32))
            into = into + jnp.where(gap > 0, weight, 0.0) * s["far"][d, k].astype(F32)
        mine = q if d == 0 else 3 - q
        s["inc"][...] = s["before"][...] + jnp.exp(-rate() * (rows * mine).astype(F32)) * into

    def lanes(b):
        return pl.ds(pl.multiple_of(b * LANES, LANES), LANES)

    regroup_filters(decay, res, skip, s["par"], s["gen"])
    tables = functools.partial(
        build_tables, s["par"], s["rate"], s["taps"], s["tail"], s["rise"], s["toep"]
    )
    tables(0, groups // 2)
    pump(2)
    tables(groups // 2, groups // 2)
    pump(2)
    loads[0].wait()
    loads[1].wait()

    def gated(b, _):
        s["u"][b] = s["inner"][:, lanes(b)].astype(F32) * s["values"][:, lanes(b)].astype(F32)
        return 0

    lax.fori_loop(0, blocks, gated, 0)
    chunks_in(s["u"], s["z"], False)
    pump(2)
    chunk_ends(s["z"], s["tail"], s["rate"], s["e"], s["pre"], s["end"], False)
    near_start(0)
    pump(2)
    near_finish(0)
    pump(2)
    far_finish(0)
    chunk_finish(s["z"], s["toep"], s["rise"], s["rate"], s["e"], s["pre"], s["inc"], s["y"], False)
    loads[2].wait()
    loads[3].wait()

    def modulate(b, _):
        m = (s["outer"][:, lanes(b)].astype(F32) * s["y"][b]).astype(BF16)
        s["mod"][:, lanes(b)] = m
        s["modt"][pl.ds(pl.multiple_of(b * LANES, LANES), LANES), :] = m.T
        return 0

    lax.fori_loop(0, blocks, modulate, 0)

    def wg_terms(k):
        sidx, own = ORDER[k]
        g, first = side(own), spot(sidx, 0, 0)
        height = 4 * part
        lhs = pl.ds(pl.multiple_of(first * part, height), height)

        def tile(n, _):
            cols = pl.ds(pl.multiple_of(n * 256, 256), 256)
            t = jnp.dot(s["modt"][lhs, :], s["og"][g, :, cols], preferred_element_type=F32)
            s["part"][g, pl.ds(first, 4), :, cols] = t.astype(BF16).reshape(4, part, 256)
            return 0

        lax.fori_loop(0, channels // 256, tile, 0)
        for yy in (0, 1):
            rc_copy(k, yy).start()

    def rc_copy(k, yy):
        sidx, own = ORDER[k]
        return remote(
            s["part"].at[side(own), spot(sidx, yy, 1 - c)], s["rc"].at[k, yy],
            s["rc_s"].at[k, yy], s["rc_r"].at[k, yy], c_to,
        )

    def ry_copy(k, t):
        return remote(
            s["ys"].at[k, fine_rows(t)], s["ry"].at[k, fine_rows(t)],
            s["ry_s"].at[k, t], s["ry_r"].at[k, t], y_to,
        )

    def wg_y(k):
        sidx, own = ORDER[k]
        rc_copy(k, 0).wait_recv()
        rc_copy(k, 1).wait_recv()
        for t in range(SUB):
            r = fine_rows(t)
            term = s["part"][side(own), spot(sidx, 1 - y, c), r].astype(F32) + s["rc"][k, 1 - y, r].astype(F32)
            s["ys"][k, r] = term.astype(BF16)
            ry_copy(k, t).start()

    def rz_copy(k, t, back=False):
        r = fine_rows(t)
        if back:
            return remote(s["zs"].at[k, r], s["rb"].at[k // 2, r], s["rz_s"].at[k, t], s["rb_r"].at[k // 2, t], up_to)
        return remote(s["zs"].at[k, r], s["rz"].at[k, r], s["rz_s"].at[k, t], s["rz_r"].at[k, t], down_to)

    def fx_copy(k, t):
        r = fine_rows(t)
        return remote(s["zs"].at[k, r], s["wx"].at[r], s["rz_s"].at[k, t], s["fx_r"].at[t], i, 1 - x)

    scale = 1.0 / math.sqrt(length)

    def z_sends(k, t):
        sidx, own = ORDER[k]
        sends = [(zm > sidx, rz_copy(k, t))]
        if sidx == 1:
            sends.append((zm == 0, rz_copy(k, t, True)))
        if not own:
            sends.append((zm == sidx, fx_copy(k, t)))
        return sends

    def wg_z(k):
        sidx, own = ORDER[k]
        g, j = side(own), spot(sidx, y, c)
        for t in range(SUB):
            r = fine_rows(t)
            ry_copy(k, t).wait_recv()
            acc = s["part"][g, j, r].astype(F32) + s["rc"][k, y, r].astype(F32) + s["ry"][k, r].astype(F32)
            s["acc"][...] = acc

            def add_down(k=k, t=t, r=r):
                rz_copy(k, t).wait_recv()
                s["acc"][...] += s["rz"][k, r].astype(F32)

            def add_back(k=k, t=t, r=r):
                rz_copy(k, t, True).wait_recv()
                s["acc"][...] += s["rb"][k // 2, r].astype(F32)

            if sidx == 0:
                when(zm < 3)(add_down)
            else:
                when((zm == 1) | (zm == 2))(add_down)
                when(zm == 1)(add_back)

            def keep(r=r):
                s["wo"][r] = s["acc"][...] * scale

            def stage(k=k, r=r):
                s["zs"][k, r] = s["acc"][...].astype(BF16)

            if own:
                when(zm == sidx)(keep)
                when(zm != sidx)(stage)
            else:
                stage()
            each(z_sends(k, t), "start")

    def wg_last():
        def take():
            for t in range(SUB):
                fx_copy(2, t).wait_recv()
                s["wo"][fine_rows(t)] = s["wx"][fine_rows(t)].astype(F32) * scale

        when(zm >= 2)(take)
        stores[-1].start()

    def wg_drain():
        for k in range(4):
            for yy in (0, 1):
                rc_copy(k, yy).wait_send()
            for t in range(SUB):
                ry_copy(k, t).wait_send()
                each(z_sends(k, t), "wait_send")

    width = channels // PIECES

    def piece(n):
        return pl.ds(n * width, width)

    stores = [
        pltpu.make_async_copy(s["bo"].at[:, piece(n)], block_out.at[:, piece(n)], s["store"].at[n])
        for n in range(PIECES)
    ] + [
        pltpu.make_async_copy(s["outer"], outer_out, s["store"].at[PIECES]),
        pltpu.make_async_copy(s["inner"], inner_out, s["store"].at[PIECES + 1]),
        pltpu.make_async_copy(s["values"], value_out, s["store"].at[PIECES + 2]),
        pltpu.make_async_copy(s["wo"], weight_out, s["store"].at[PIECES + 3]),
    ]

    def b_copy(n):
        return remote(s["bs"].at[n], s["br"].at[n], s["b_s"].at[n], s["b_r"].at[n], i, 1 - x)

    def projected(g, n):
        return jnp.dot(
            s["mod"][...], s["w"][g, :, :, piece(n)].reshape(channels, width), preferred_element_type=F32
        )

    wg_terms(0)
    pump(2)
    wg_terms(1)
    pump(100)
    w_rest()
    for n in range(PIECES):
        s["bs"][n] = projected(1 - x, n).astype(BF16)
        b_copy(n).start()
    for n in range(PIECES):
        og_copy(n).wait_recv()
    wg_y(0)
    wg_y(1)
    wg_terms(2)
    wg_terms(3)

    def gradient(p, _):
        cols = pl.ds(pl.multiple_of(p * 2 * LANES, 2 * LANES), 2 * LANES)
        grad = None
        for g in range(2):
            w = s["w"][g, pl.ds(p * (2 * LANES // part), 2 * LANES // part)].reshape(2 * LANES, channels)
            t = lax.dot_general(s["og"][g], w, (((1,), (1,)), ((), ())), preferred_element_type=F32)
            grad = t if grad is None else grad + t
        gate = s["outer"][:, cols].astype(F32)
        filtered_grad = grad * gate
        s["outer"][:, cols] = (
            grad * jnp.concatenate([s["y"][2 * p], s["y"][2 * p + 1]], axis=1)
        ).astype(BF16)
        s["u"][2 * p] = filtered_grad[:, :LANES]
        s["u"][2 * p + 1] = filtered_grad[:, LANES:]
        return 0

    lax.fori_loop(0, blocks // 2, gradient, 0)
    stores[PIECES].start()
    wg_y(2)
    wg_y(3)
    chunks_in(s["u"], s["z"], True)
    chunk_ends(s["z"], s["tail"], s["rate"], s["e"], s["pre"], s["end"], True)
    near_start(1)
    wg_z(0)
    wg_z(1)
    near_finish(1)
    for n in range(PIECES):
        s["bo"][:, piece(n)] = projected(x, n).astype(BF16)
    far_finish(1)
    chunk_finish(s["z"], s["toep"], s["rise"], s["rate"], s["e"], s["pre"], s["inc"], s["u"], True)

    def grads(b, _):
        gg = s["u"][b]
        gate, value = s["inner"][:, lanes(b)].astype(F32), s["values"][:, lanes(b)].astype(F32)
        s["inner"][:, lanes(b)] = (gg * value).astype(BF16)
        s["values"][:, lanes(b)] = (gg * gate).astype(BF16)
        return 0

    lax.fori_loop(0, blocks, grads, 0)
    stores[PIECES + 1].start()
    stores[PIECES + 2].start()
    wg_z(2)
    wg_z(3)
    for n in range(PIECES):
        b_copy(n).wait_recv()
        s["bo"][:, piece(n)] = (s["bo"][:, piece(n)].astype(F32) + s["br"][n].astype(F32)).astype(BF16)
        stores[n].start()
    wg_last()

    w_drain()
    wg_drain()
    for n in range(PIECES):
        og_copy(n).wait_send()
        b_copy(n).wait_send()
    for d in (0, 1):
        for t in (1, 2, 3):
            near_copy(d, t).wait_send()
        far_sends(d, "wait_send")
    for copy in stores:
        copy.wait()


def fused(outer_gate, inner_gate, values, out_weight, skip_gain, residues, decay_rates, out_grad):
    rows, channels = values.shape
    ctx = lax.axis_size("ctx")
    scratch = fused_scratch(rows, channels)
    scratch["acc"] = pltpu.VMEM((channels // 8 // SUB, channels), F32)
    shape = jax.ShapeDtypeStruct
    small = pl.BlockSpec(memory_space=pltpu.VMEM)
    large = pl.BlockSpec(memory_space=pl.ANY)
    tile = shape((rows, channels), BF16)
    return pl.pallas_call(
        functools.partial(fused_kernel, tuple(scratch), rows * ctx),
        out_shape=[tile] * 4 + [shape(out_weight.shape, F32)],
        in_specs=[small] * 3 + [large] * 5,
        out_specs=[large] * 5,
        scratch_shapes=list(scratch.values()),
        compiler_params=pltpu.CompilerParams(
            collective_id=3, has_side_effects=True, vmem_limit_bytes=VMEM_BYTES
        ),
        cost_estimate=pl.CostEstimate(flops=6 * 2**30, bytes_accessed=10 * 2**20, transcendentals=0),
        name="fused",
    )(decay_rates.T, residues.T, skip_gain[None], outer_gate, inner_gate, values, out_weight, out_grad)


def solution(mesh):
    tile = P("ctx", "fsdp")
    small = dict(mesh.shape) == {"ctx": 16, "fsdp": 2}
    return jax.shard_map(
        fused if small else shards,
        mesh=mesh,
        in_specs=(tile, tile, tile, tile, P("fsdp"), P("fsdp", None), P("fsdp", None), tile),
        out_specs=(tile,) * 5,
        check_vma=False,
    )
```

```python
import functools
import math

import jax
import jax.numpy as jnp
from jax import lax
from jax.experimental import pallas as pl
from jax.experimental.pallas import tpu as pltpu
from jax.sharding import PartitionSpec as P

F32 = jnp.float32
BF16 = jnp.bfloat16
LANES = 128
SEGS = 8
VMEM_BYTES = 62 * 2**20


def rows_at(i, steps):
    return pl.ds(i, SEGS, stride=steps)


def spread(row):
    return jnp.broadcast_to(row, (SEGS, LANES))


def segment_states(u_scr, decay_ref, pre_ref, end_ref, reverse):
    modes = decay_ref.shape[0]
    steps = u_scr.shape[0] // SEGS
    a = [spread(jnp.exp(-decay_ref[r : r + 1, :])) for r in range(modes)]

    def step(k, states):
        i = steps - 1 - k if reverse else k
        u = u_scr[rows_at(i, steps), :]
        return tuple(a[r] * states[r] + u for r in range(modes))

    zero = jnp.zeros((SEGS, LANES), F32)
    states = lax.fori_loop(0, steps, step, (zero,) * modes, unroll=4)
    seg = lax.broadcasted_iota(jnp.int32, (SEGS, LANES), 0)

    def moved(x, by):
        if reverse:
            return jnp.where(seg < SEGS - by, pltpu.roll(x, SEGS - by, 0), 0.0)
        return jnp.where(seg >= by, pltpu.roll(x, by, 0), 0.0)

    last = 0 if reverse else SEGS - 1
    for r in range(modes):
        rate = spread(decay_ref[r : r + 1, :])
        x = states[r]
        for by in (1, 2, 4):
            x = x + jnp.exp(-rate * float(steps * by)) * moved(x, by)
        end_ref[r : r + 1, :] = x[last : last + 1, :]
        pre_ref[r] = moved(x, 1)


def full_scan(u_scr, y_scr, decay_ref, res_ref, pre_ref, incoming_ref, reverse):
    modes = decay_ref.shape[0]
    rows = u_scr.shape[0]
    steps = rows // SEGS
    seg = lax.broadcasted_iota(jnp.int32, (SEGS, LANES), 0)
    ahead = ((SEGS - 1 - seg if reverse else seg) * steps).astype(F32)
    a = []
    first = []
    for r in range(modes):
        rate = spread(decay_ref[r : r + 1, :])
        a.append(jnp.exp(-rate))
        first.append(pre_ref[r] + jnp.exp(-rate * ahead) * incoming_ref[r : r + 1, :])
    res = [spread(res_ref[r : r + 1, :]) for r in range(modes)]

    def step(k, states):
        i = steps - 1 - k if reverse else k
        u = u_scr[rows_at(i, steps), :]
        states = tuple(a[r] * states[r] + u for r in range(modes))
        terms = [res[r] * states[r] for r in range(modes)]
        while len(terms) > 1:
            terms = [p + q for p, q in zip(terms[::2], terms[1::2])]
        y_scr[rows_at(i, steps), :] = terms[0]
        return states

    lax.fori_loop(0, steps, step, tuple(first), unroll=2)


def forward_ends(inner_ref, values_ref, decay_ref, pre_ref, end_ref, u_scr):
    u_scr[...] = inner_ref[...].astype(F32) * values_ref[...].astype(F32)
    segment_states(u_scr, decay_ref, pre_ref, end_ref, False)


def forward_finish(
    inner_ref, values_ref, outer_ref, decay_ref, res_ref, skip_ref, pre_ref, incoming_ref,
    filtered_ref, modulated_ref, u_scr, y_scr,
):
    u_scr[...] = inner_ref[...].astype(F32) * values_ref[...].astype(F32)
    full_scan(u_scr, y_scr, decay_ref, res_ref, pre_ref, incoming_ref, False)
    filtered = y_scr[...] + skip_ref[...] * u_scr[...]
    filtered_ref[...] = filtered
    modulated_ref[...] = (outer_ref[...].astype(F32) * filtered).astype(BF16)


def backward_ends(own_ref, other_ref, outer_ref, decay_ref, pre_ref, end_ref, u_scr):
    grad = own_ref[...].astype(F32) + other_ref[...].astype(F32)
    u_scr[...] = grad * outer_ref[...].astype(F32)
    segment_states(u_scr, decay_ref, pre_ref, end_ref, True)


def backward_finish(
    own_ref, other_ref, outer_ref, inner_ref, values_ref, filtered_ref, decay_ref, res_ref, skip_ref,
    pre_ref, incoming_ref, outer_grad_ref, inner_grad_ref, value_grad_ref, u_scr, y_scr,
):
    grad = own_ref[...].astype(F32) + other_ref[...].astype(F32)
    u_scr[...] = grad * outer_ref[...].astype(F32)
    outer_grad_ref[...] = (grad * filtered_ref[...]).astype(BF16)
    full_scan(u_scr, y_scr, decay_ref, res_ref, pre_ref, incoming_ref, True)
    gated_grad = y_scr[...] + skip_ref[...] * u_scr[...]
    inner_grad_ref[...] = (gated_grad * values_ref[...].astype(F32)).astype(BF16)
    value_grad_ref[...] = (gated_grad * inner_ref[...].astype(F32)).astype(BF16)


def by_lanes(kernel, operands, outs, rows, scans):
    channels = operands[0].shape[-1]

    def spec(x):
        lead = x.shape[:-1]
        return pl.BlockSpec(lead + (LANES,), lambda c, n=len(lead): (0,) * n + (c,))

    work = rows * channels * (24000 if scans > 1 else 16000)
    moved = sum(math.prod(x.shape) * x.dtype.itemsize for x in list(operands) + list(outs))
    return pl.pallas_call(
        kernel,
        grid=(channels // LANES,),
        out_shape=outs,
        in_specs=[spec(x) for x in operands],
        out_specs=[spec(x) for x in outs],
        scratch_shapes=[pltpu.VMEM((rows, LANES), F32)] * scans,
        cost_estimate=pl.CostEstimate(flops=work, bytes_accessed=moved, transcendentals=0),
        name=kernel.__name__,
    )(*operands)


def prefix_kernel(reverse, rows, end_ref, decay_ref, out_ref, sent, got, send_sem, recv_sem):
    me, n = lax.axis_index("ctx"), lax.axis_size("ctx")
    hops = [1 << k for k in range(sent.shape[0])]
    barrier = pltpu.get_barrier_semaphore()
    for hop in hops:
        for peer in (lax.rem(me + hop, n), lax.rem(me + n - hop, n)):
            pl.semaphore_signal(
                barrier, inc=1, device_id={"ctx": peer}, device_id_type=pl.DeviceIdType.MESH
            )
    pl.semaphore_wait(barrier, 2 * len(hops))
    decay = decay_ref[...]
    upto = end_ref[...]
    before = jnp.zeros_like(upto)
    for k, hop in enumerate(hops):
        sent[k] = upto.astype(BF16)
        copy = pltpu.make_async_remote_copy(
            src_ref=sent.at[k],
            dst_ref=got.at[k],
            send_sem=send_sem.at[k],
            recv_sem=recv_sem.at[k],
            device_id={"ctx": lax.rem(me + (n - hop if reverse else hop), n)},
            device_id_type=pl.DeviceIdType.MESH,
        )
        copy.start()
        near = jnp.exp(-decay * float(rows * (hop - 1)))
        far = jnp.exp(-decay * float(rows * hop))
        copy.wait()
        inside = (me + hop < n) if reverse else (me >= hop)
        term = got[k].astype(F32) * jnp.where(inside, 1.0, 0.0)
        before = before + near * term
        upto = upto + far * term
    out_ref[...] = before


def prefix(end, decay, rows, reverse):
    hops = max(1, (lax.axis_size("ctx") - 1).bit_length())
    whole = pl.BlockSpec(memory_space=pltpu.VMEM)
    return pl.pallas_call(
        functools.partial(prefix_kernel, reverse, rows),
        out_shape=jax.ShapeDtypeStruct(end.shape, F32),
        in_specs=[whole, whole],
        out_specs=whole,
        scratch_shapes=[
            pltpu.VMEM((hops,) + end.shape, BF16),
            pltpu.VMEM((hops,) + end.shape, BF16),
            pltpu.SemaphoreType.DMA((hops,)),
            pltpu.SemaphoreType.DMA((hops,)),
        ],
        compiler_params=pltpu.CompilerParams(
            collective_id=2 if reverse else 1, has_side_effects=True
        ),
        cost_estimate=pl.CostEstimate(flops=18 * 10**9, bytes_accessed=0, transcendentals=0),
        name="prefix_back" if reverse else "prefix_ahead",
    )(end, decay)


def shards(outer_gate, inner_gate, values, out_weight, skip_gain, residues, decay_rates, out_grad):
    rows, channels = values.shape
    modes = decay_rates.shape[1]
    ctx, fsdp = lax.axis_size("ctx"), lax.axis_size("fsdp")
    at = lax.axis_index("fsdp")
    swap = [(0, 1), (1, 0)]
    shape = jax.ShapeDtypeStruct
    panel = lax.all_gather(out_weight, "ctx", axis=0, tiled=True)
    decay = decay_rates.T
    res = residues.T
    skip = skip_gain[None]
    state_outs = [shape((modes, SEGS, channels), F32), shape((modes, channels), F32)]
    pre, end = by_lanes(forward_ends, (inner_gate, values, decay), state_outs, rows, 1)
    incoming = prefix(end, decay, rows, False)
    filtered, modulated = by_lanes(
        forward_finish,
        (inner_gate, values, outer_gate, decay, res, skip, pre, incoming),
        [shape((rows, channels), F32), shape((rows, channels), BF16)],
        rows,
        2,
    )
    if fsdp == 2:
        other = lax.ppermute(modulated, "fsdp", swap)
        first = jnp.where(at == 0, modulated, other)
        second = jnp.where(at == 0, other, modulated)
        gathered = jnp.concatenate([first, second], axis=1)
        mine = lax.dynamic_slice_in_dim(panel, at * channels, channels, 0)
        theirs = lax.dynamic_slice_in_dim(panel, (1 - at) * channels, channels, 0)
        for_them = jnp.dot(out_grad, theirs.T, preferred_element_type=F32).astype(BF16)
        from_them = lax.ppermute(for_them, "fsdp", swap)
        own = jnp.dot(out_grad, mine.T, preferred_element_type=F32).astype(BF16)
    else:
        gathered = lax.all_gather(modulated, "fsdp", axis=1, tiled=True)
        partial = jnp.dot(out_grad, panel.T, preferred_element_type=F32).astype(BF16)
        own = lax.psum_scatter(partial, "fsdp", scatter_dimension=1, tiled=True)
        from_them = jnp.zeros_like(own)
    grad_rows = lax.dot_general(
        gathered, out_grad, (((0,), (0,)), ((), ())), preferred_element_type=F32
    ).astype(BF16)
    weight_grad = lax.psum_scatter(grad_rows, "ctx", scatter_dimension=0, tiled=True)
    block_out = jnp.dot(gathered, panel, preferred_element_type=F32).astype(BF16)
    pre, end = by_lanes(
        backward_ends, (own, from_them, outer_gate, decay), state_outs, rows, 1
    )
    incoming = prefix(end, decay, rows, True)
    outer_grad, inner_grad, value_grad = by_lanes(
        backward_finish,
        (own, from_them, outer_gate, inner_gate, values, filtered, decay, res, skip, pre, incoming),
        [shape((rows, channels), BF16)] * 3,
        rows,
        2,
    )
    weight_grad, value_grad = lax.optimization_barrier((weight_grad, value_grad))
    weight_grad = weight_grad.astype(F32) * (1.0 / math.sqrt(rows * ctx))
    return (block_out, outer_grad, inner_grad, value_grad, weight_grad)


TAPS = 16
GRAN = 16
PER = LANES // GRAN
WIDE = TAPS * GRAN
SUB = 2
PIECES = 4
GATHER = (
    "L0 L1 L2 L3 L4 L5 Y0 Y1 L6 L7 Y2 Y3 Y4 Y5 Y6 Y7",
    "L0 L1 L2 Y0 L3 Y1 L4 L5 L6 Y2 L7 Y3 Y4 Y5 Y6 Y7",
    "L0 L1 L2 Y0 L3 Y1 L4 Y2 L5 Y3 L6 L7 Y4 Y5 Y6 Y7",
)
REDUCE = (
    (0, 1, 4, 5, 2, 3, 6, 7),
    (0, 1, 2, 3, 4, 5, 6, 7),
    (0, 1, 2, 3, 4, 5, 6, 7),
    (0, 1, 2, 3, 4, 5, 6, 7),
)
MESH = pl.DeviceIdType.MESH
ORDER = ((1, True), (0, True), (1, False), (0, False))


def regroup(v):
    lane = lax.broadcasted_iota(jnp.int32, v[0].shape, 1) // GRAN
    v = list(v)
    for m in (1, 2, 4):
        low = (lane & m) == 0
        for i in range(PER):
            if i & m:
                continue
            p, q = v[i], v[i + m]
            v[i] = jnp.where(low, p, pltpu.roll(q, GRAN * m, 1))
            v[i + m] = jnp.where(low, pltpu.roll(p, LANES - GRAN * m, 1), q)
    return v


def row_at(k, s, steps, reverse):
    return TAPS * (steps - 1 - k) + TAPS - 1 - s if reverse else TAPS * k + s


def regroup_filters(decay_ref, res_ref, skip_ref, par_ref, gen_ref):
    row = lax.broadcasted_iota(jnp.int32, (SEGS, LANES), 0)
    lag = lax.broadcasted_iota(jnp.int32, (TAPS, LANES), 0)
    lags = lag.astype(F32)

    def block(b, _):
        cols = pl.ds(pl.multiple_of(b * LANES, LANES), LANES)
        kern = jnp.where(lag == 0, jnp.broadcast_to(skip_ref[:, cols], (TAPS, LANES)), 0.0)
        for r in range(TAPS):
            kern = kern + res_ref[r : r + 1, cols] * jnp.exp(-decay_ref[r : r + 1, cols] * lags)
        gen_ref[...] = kern
        for half in range(2):
            v = []
            for s in range(half * PER, (half + 1) * PER):
                rate = jnp.broadcast_to(decay_ref[s : s + 1, cols], (SEGS, LANES))
                res = jnp.broadcast_to(res_ref[s : s + 1, cols], (SEGS, LANES))
                tap = jnp.broadcast_to(gen_ref[s : s + 1, :], (SEGS, LANES))
                v.append(jnp.where(row == 0, rate, jnp.where(row == 1, res, tap)))
            for h, out in enumerate(regroup(v)):
                par_ref[b * PER + h, :, half * LANES : (half + 1) * LANES] = out
        return 0

    lax.fori_loop(0, decay_ref.shape[1] // LANES, block, 0)


def build_tables(par_ref, rate_ref, taps_ref, outs, first, groups):
    shape = (GRAN, WIDE)
    diagonal = lax.broadcasted_iota(jnp.int32, shape, 1) % GRAN == lax.broadcasted_iota(jnp.int32, shape, 0)
    lag = lax.broadcasted_iota(jnp.int32, (TAPS, WIDE), 0)
    lags = lag.astype(F32)
    at = lax.broadcasted_iota(jnp.int32, (TAPS, WIDE), 1) // GRAN

    def group(n, _):
        for d in range(4):
            g = first + 4 * n + d
            rate = par_ref[g, 0:1, :]
            for i in outs:
                if i == 0:
                    rate_ref[pl.ds(g, 1), :] = rate
                    taps_ref[d, i] = jnp.exp(-rate * (TAPS - 1 - lags))
                elif i == 1:
                    taps_ref[d, i] = par_ref[g, 1:2, :] * jnp.exp(-rate * (lags + 1))
                else:
                    kern = jnp.broadcast_to(par_ref[g, 2:3, :], (TAPS, WIDE))
                    taps_ref[d, i] = jnp.where(at >= lag, pltpu.roll(kern, 0, 1, stride=GRAN, stride_axis=0), 0.0)
        for d in range(4):
            g = first + 4 * n + d
            for i, out in outs.items():
                for s in range(TAPS):
                    line = jnp.broadcast_to(taps_ref[d, i, s : s + 1, :], shape)
                    out[g, s * GRAN : (s + 1) * GRAN, :] = jnp.where(diagonal, line, 0.0).astype(BF16)
        return 0

    lax.fori_loop(0, groups // 4, group, 0)


def moved(x, by, reverse):
    seg = lax.broadcasted_iota(jnp.int32, x.shape, 0)
    if reverse:
        return jnp.where(seg < SEGS - by, pltpu.roll(x, SEGS - by, 0), 0.0)
    return jnp.where(seg >= by, pltpu.roll(x, by, 0), 0.0)


def conv_in(u_ref, z_ref, tail_ref, rate_ref, e_ref, pre_ref, end_ref, reverse):
    blocks, rows, _ = u_ref.shape
    stride = rows // SEGS
    steps = stride // TAPS
    last = 0 if reverse else SEGS - 1

    def split(b):
        for half in range(2):
            for k in range(0, steps, 2):
                pair = [
                    regroup(
                        [
                            u_ref[b, pl.ds(row_at(n, half * PER + j, steps, reverse), SEGS, stride=stride), :]
                            for j in range(PER)
                        ]
                    )
                    for n in (k, k + 1)
                ]
                for h in range(PER):
                    z_ref[b * PER + h, k * SEGS : (k + 2) * SEGS, half * LANES : (half + 1) * LANES] = (
                        jnp.concatenate([pair[0][h], pair[1][h]], axis=0).astype(BF16)
                    )

    def ends(b):
        for h in range(PER):
            g = b * PER + h
            e = jnp.dot(z_ref[g], tail_ref[g], preferred_element_type=F32)
            e_ref[g] = e
            rate = jnp.broadcast_to(rate_ref[pl.ds(g, 1), :], (SEGS, WIDE))
            a = jnp.exp(-rate * float(TAPS))
            x = e[0:SEGS]
            for k in range(1, steps):
                x = a * x + e[k * SEGS : (k + 1) * SEGS]
            for by in (1, 2, 4):
                x = x + jnp.exp(-rate * float(TAPS * steps * by)) * moved(x, by, reverse)
            end_ref[pl.ds(g, 1), :] = x[last : last + 1, :]
            pre_ref[g] = moved(x, 1, reverse)

    return pipelined(split, ends, blocks)


def pipelined(first, second, blocks):
    def body(b, _):
        second(b - 1)
        first(b)
        return 0

    def run(lo, hi):
        if lo == 0:
            first(0)
        lax.fori_loop(max(lo, 1), hi, body, 0)
        if hi == blocks:
            second(blocks - 1)

    return run


def conv_out(z_ref, toep_ref, rise_ref, rate_ref, e_ref, pre_ref, inc_ref, y_ref, reverse):
    groups, chunks, _ = z_ref.shape
    steps = chunks // SEGS
    stride = y_ref.shape[1] // SEGS

    def finish(b):
        seg = lax.broadcasted_iota(jnp.int32, (SEGS, WIDE), 0)
        ahead = ((SEGS - 1 - seg if reverse else seg) * (TAPS * steps)).astype(F32)
        for h in range(PER):
            g = b * PER + h
            rate = jnp.broadcast_to(rate_ref[pl.ds(g, 1), :], (SEGS, WIDE))
            a = jnp.exp(-rate * float(TAPS))
            x = pre_ref[g] + jnp.exp(-rate * ahead) * inc_ref[pl.ds(g, 1), :]
            states = [x]
            for k in range(steps - 1):
                x = a * x + e_ref[g, k * SEGS : (k + 1) * SEGS]
                states.append(x)
            s = jnp.concatenate(states, axis=0).astype(BF16)
            y = jnp.dot(z_ref[g], toep_ref[g], preferred_element_type=F32)
            e_ref[g] = y + lax.dot_general(s, rise_ref[g], (((1,), (1,)), ((), ())), preferred_element_type=F32)

    def merge(b):
        for half in range(2):
            for k in range(steps):
                v = regroup(
                    [
                        e_ref[b * PER + h, k * SEGS : (k + 1) * SEGS, half * LANES : (half + 1) * LANES]
                        for h in range(PER)
                    ]
                )
                for j in range(PER):
                    y_ref[b, pl.ds(row_at(k, half * PER + j, steps, reverse), SEGS, stride=stride), :] = v[j]

    return pipelined(finish, merge, groups // PER)


def fused_scratch(rows, channels):
    blocks, groups = channels // LANES, channels // GRAN
    chunks = rows // TAPS
    part = channels // 8
    dma = pltpu.SemaphoreType.DMA
    v = pltpu.VMEM
    return dict(
        tail=v((groups, WIDE, WIDE), BF16),
        rise=v((groups, WIDE, WIDE), BF16),
        toep=v((groups, WIDE, WIDE), BF16),
        par=v((groups, SEGS, WIDE), F32),
        rate=v((groups, WIDE), F32),
        taps=v((4, 3, TAPS, WIDE), F32),
        gen=v((TAPS, LANES), F32),
        inner=v((rows, channels), BF16),
        values=v((rows, channels), BF16),
        outer=v((rows, channels), BF16),
        og=v((2, rows, channels), BF16),
        w=v((2, 8, part, channels), BF16),
        u=v((blocks, rows, LANES), F32),
        y=v((blocks, rows, LANES), F32),
        z=v((groups, chunks, WIDE), BF16),
        e=v((groups, chunks, WIDE), F32),
        pre=v((groups, SEGS, WIDE), F32),
        end=v((groups, WIDE), F32),
        before=v((groups, WIDE), F32),
        inc=v((groups, WIDE), F32),
        near=v((2, 4, groups, WIDE), BF16),
        total=v((2, groups, WIDE), BF16),
        far=v((2, 4, groups, WIDE), BF16),
        mod=v((rows, channels), BF16),
        modt=v((channels, rows), BF16),
        bs=v((PIECES, rows, channels // PIECES), BF16),
        br=v((PIECES, rows, channels // PIECES), BF16),
        bo=v((rows, channels), BF16),
        part=v((2, 8, part, channels), BF16),
        rc=v((4, 2, part, channels), BF16),
        ys=v((4, part, channels), BF16),
        ry=v((4, part, channels), BF16),
        zs=v((4, part, channels), BF16),
        rz=v((4, part, channels), BF16),
        rb=v((2, part, channels), BF16),
        wx=v((part, channels), BF16),
        wo=v((part, channels), F32),
        load=dma((5,)),
        store=dma((PIECES + 4,)),
        og_s=dma((PIECES,)),
        og_r=dma((PIECES,)),
        wx_s=dma((SUB,)),
        w_r=dma((2, 8, SUB)),
        up_s=dma((4, SUB)),
        down_s=dma((4, SUB)),
        y_s=dma((4, SUB)),
        c_s=dma((4, SUB)),
        cy_s=dma((4, SUB)),
        near_s=dma((2, 4)),
        near_r=dma((2, 4)),
        far_s=dma((2, 4)),
        far_r=dma((2, 4)),
        b_s=dma((PIECES,)),
        b_r=dma((PIECES,)),
        rc_s=dma((4, 2)),
        rc_r=dma((4, 2)),
        ry_s=dma((4, SUB)),
        ry_r=dma((4, SUB)),
        rz_s=dma((4, SUB)),
        rz_r=dma((4, SUB)),
        rb_r=dma((2, SUB)),
        fx_s=dma((SUB,)),
        fx_r=dma((SUB,)),
    )


def fused_kernel(names, length, *refs):
    decay, res, skip, outer_in, inner_in, values_in, weight_in, grad_in = refs[:8]
    block_out, outer_out, inner_out, value_out, weight_out = refs[8:13]
    s = dict(zip(names, refs[13:]))
    rows, channels = inner_in.shape
    part = weight_in.shape[0]
    blocks = channels // LANES
    groups = channels // GRAN
    fine = part // SUB
    i, x = lax.axis_index("ctx"), lax.axis_index("fsdp")
    z, y, c = i // 4, (i // 2) % 2, i % 2
    zm = jnp.where(x == 0, z, 3 - z)
    q = i % 4

    def ctx_at(z, y, c):
        return z * 4 + y * 2 + c

    up_to = ctx_at(z + 1 - 2 * x, y, c)
    down_to = ctx_at(z - 1 + 2 * x, y, c)
    y_to = ctx_at(z, 1 - y, c)
    c_to = ctx_at(z, y, 1 - c)

    def remote(src, dst, send, recv, ctx, fsdp=x):
        return pltpu.make_async_remote_copy(
            src_ref=src, dst_ref=dst, send_sem=send, recv_sem=recv,
            device_id={"ctx": ctx, "fsdp": fsdp}, device_id_type=MESH,
        )

    def when(cond):
        return pl.when(cond)

    loads = [
        pltpu.make_async_copy(inner_in, s["inner"], s["load"].at[0]),
        pltpu.make_async_copy(values_in, s["values"], s["load"].at[1]),
        pltpu.make_async_copy(outer_in, s["outer"], s["load"].at[2]),
        pltpu.make_async_copy(grad_in, s["og"].at[x], s["load"].at[3]),
    ]
    for copy in loads:
        copy.start()
    jown = (z % 2) * 4 + q
    source = zm < 2
    keep_w = pltpu.make_async_copy(weight_in, s["w"].at[x, jown], s["load"].at[4])
    when(source)(keep_w.start)
    s["far"][...] = jnp.zeros_like(s["far"])

    barrier = pltpu.get_barrier_semaphore()
    peers = [(ctx_at(z, (q + t) % 4 // 2, (q + t) % 2), x) for t in (1, 2, 3)]
    peers += [(ctx_at((z + t) % 4, y, c), x) for t in (1, 2, 3)] + [(i, 1 - x)]
    for ctx, fsdp in peers:
        pl.semaphore_signal(barrier, inc=1, device_id={"ctx": ctx, "fsdp": fsdp}, device_id_type=MESH)
    pl.semaphore_wait(barrier, len(peers))

    def fine_rows(t):
        return pl.ds(t * fine, fine)

    def spot(sidx, yy, cc):
        return jnp.where(x == 0, sidx, 1 - sidx) * 4 + yy * 2 + cc

    def side(own):
        return x if own else 1 - x

    def w_cross(t):
        return remote(
            weight_in.at[fine_rows(t)], s["w"].at[x, jown, fine_rows(t)], s["wx_s"].at[t],
            s["w_r"].at[x, jown, t], i, 1 - x,
        )

    def w_sends(src, g, j, k, t, up, down):
        dst = s["w"].at[g, j, fine_rows(t)]
        recv = s["w_r"].at[g, j, t]
        return [
            (up, remote(src, dst, s["up_s"].at[k, t], recv, up_to)),
            (down, remote(src, dst, s["down_s"].at[k, t], recv, down_to)),
            (None, remote(src, dst, s["y_s"].at[k, t], recv, y_to)),
            (None, remote(src, dst, s["c_s"].at[k, t], recv, c_to)),
        ]

    def each(sends, act):
        for cond, copy in sends:
            if cond is None:
                getattr(copy, act)()
            elif cond is not False:
                when(cond)(getattr(copy, act))

    def place(p):
        low = zm == 0
        sidx = jnp.where(low, p // 2, 1 - p % 2)
        own = jnp.where(low, p % 2 == 0, p < 2)
        return sidx, jnp.where(own, x, 1 - x)

    def own_sends(t):
        return w_sends(weight_in.at[fine_rows(t)], x, jown, 0, t, None, zm == 1)

    def line_sends(p, t):
        sidx, g = place(p)
        j = spot(sidx, y, c)
        src = s["w"].at[g, j, fine_rows(t)]
        up = ((sidx == 0) & (zm < 3)) | ((sidx == 1) & (zm >= 1) & (zm < 3))
        return w_sends(src, g, j, p, t, up, (sidx == 1) & (zm == 1))

    def w_wait(g, j, t):
        dst = s["w"].at[g, j, fine_rows(t)]
        remote(dst, dst, s["wx_s"].at[t], s["w_r"].at[g, j, t], c_to).wait_recv()

    def pump_line(p, t):
        def go():
            sidx, g = place(p)
            w_wait(g, spot(sidx, y, c), t)
            each(line_sends(p, t), "start")

        if p == 0:
            when(zm >= 2)(go)
        else:
            go()

    def y_pass(p, t):
        sidx, g = place(p)
        j = spot(sidx, 1 - y, c)
        at = s["w"].at[g, j, fine_rows(t)]
        return remote(at, at, s["cy_s"].at[p, t], s["w_r"].at[g, j, t], c_to)

    def pump_y(p, t):
        sidx, g = place(p)
        w_wait(g, spot(sidx, 1 - y, c), t)
        y_pass(p, t).start()

    def w_rest():
        for sidx, own in ORDER:
            for t in range(SUB):
                for yy in (0, 1):
                    w_wait(side(own), spot(sidx, yy, 1 - c), t)
        when(source)(keep_w.wait)

    def w_drain():
        def cross():
            for t in range(SUB):
                w_cross(t).wait_send()

        def owned():
            for t in range(SUB):
                each(own_sends(t), "wait_send")

        when(zm >= 2)(cross)
        when(source)(owned)
        for p in range(4):
            for t in range(SUB):
                if p == 0:
                    when(zm >= 2)(functools.partial(each, line_sends(p, t), "wait_send"))
                else:
                    each(line_sends(p, t), "wait_send")
                y_pass(p, t).wait_send()

    def start_cross():
        for t in range(SUB):
            w_cross(t).start()

    def start_owned():
        for t in range(SUB):
            each(own_sends(t), "start")

    when(zm >= 2)(start_cross)
    when(source)(start_owned)

    slab = rows // PIECES

    def og_copy(n):
        return remote(
            grad_in.at[pl.ds(n * slab, slab)], s["og"].at[x, pl.ds(n * slab, slab)],
            s["og_s"].at[n], s["og_r"].at[n], i, 1 - x,
        )

    for n in range(PIECES):
        og_copy(n).start()

    def listed(text):
        return [
            (pump_line if at[0] == "L" else pump_y, int(at[1:]) // SUB, int(at[1:]) % SUB)
            for at in text.split()
        ]

    classes = (source, zm == 2, zm == 3)
    orders = [listed(text) for text in GATHER]
    done = [0] * len(classes)

    def pump(*counts):
        for n, cond in enumerate(classes):
            steps = orders[n][done[n] : counts[n]]
            done[n] = max(done[n], counts[n])

            def go(steps=steps):
                for act, p, t in steps:
                    act(p, t)

            if steps:
                when(cond)(go)

    def rate():
        return s["rate"][...]

    def near_copy(d, t):
        to = (q + t) % 4
        at = s["near"].at[d, q]
        return remote(at, at, s["near_s"].at[d, t], s["near_r"].at[d, q], ctx_at(z, to // 2, to % 2))

    def near_wait(d, t):
        frm = (q + t) % 4
        at = s["near"].at[d, frm]
        remote(at, at, s["near_s"].at[d, t], s["near_r"].at[d, frm], c_to).wait_recv()

    def far_copy(d, t):
        to = z + t if d == 0 else z - t
        at = s["far"].at[d, z]
        return remote(s["total"].at[d], at, s["far_s"].at[d, t], s["far_r"].at[d, z], ctx_at(to, y, c))

    def far_sends(d, act):
        for t in (1, 2, 3):
            cond = z + t < 4 if d == 0 else z - t >= 0
            when(cond)(getattr(far_copy(d, t), act))

    def near_start(d):
        s["near"][d, q] = s["end"][...].astype(BF16)
        for t in (1, 2, 3):
            near_copy(d, t).start()

    def near_finish(d):
        for t in (1, 2, 3):
            near_wait(d, t)
        total = jnp.zeros((groups, WIDE), F32)
        before = jnp.zeros((groups, WIDE), F32)
        mine = q if d == 0 else 3 - q
        for k in range(4):
            rank = k if d == 0 else 3 - k
            term = s["near"][d, k].astype(F32)
            total = total + jnp.exp(-rate() * float(rows * (3 - rank))) * term
            gap = mine - rank
            weight = jnp.exp(-rate() * (rows * jnp.maximum(gap - 1, 0)).astype(F32))
            before = before + jnp.where(gap > 0, weight, 0.0) * term
        s["before"][...] = before
        s["total"][d] = total.astype(BF16)
        far_sends(d, "start")

    def far_finish(d):
        for t in (1, 2, 3):
            frm = z - t if d == 0 else z + t
            at = s["far"].at[d, frm]
            copy = remote(at, at, s["far_s"].at[d, t], s["far_r"].at[d, frm], c_to)
            when(z - t >= 0 if d == 0 else z + t < 4)(copy.wait_recv)
        into = jnp.zeros((groups, WIDE), F32)
        for k in range(4):
            gap = z - k if d == 0 else k - z
            weight = jnp.exp(-rate() * (4 * rows * jnp.maximum(gap - 1, 0)).astype(F32))
            into = into + jnp.where(gap > 0, weight, 0.0) * s["far"][d, k].astype(F32)
        mine = q if d == 0 else 3 - q
        s["inc"][...] = s["before"][...] + jnp.exp(-rate() * (rows * mine).astype(F32)) * into

    def lanes(b):
        return pl.ds(pl.multiple_of(b * LANES, LANES), LANES)

    build = functools.partial(build_tables, s["par"], s["rate"], s["taps"])
    later = {1: s["rise"], 2: s["toep"]}
    regroup_filters(decay, res, skip, s["par"], s["gen"])
    loads[0].wait()
    loads[1].wait()

    def gated(b, _):
        s["u"][b] = s["inner"][:, lanes(b)].astype(F32) * s["values"][:, lanes(b)].astype(F32)
        return 0

    lax.fori_loop(0, blocks, gated, 0)
    build({0: s["tail"]}, 0, groups)
    states = (s["rate"], s["e"], s["pre"])
    ahead = conv_in(s["u"], s["z"], s["tail"], *states, s["end"], False)
    ahead(0, blocks // 2)
    pump(4, 1, 0)
    ahead(blocks // 2, blocks)
    near_start(0)
    pump(8, 2, 0)
    build({1: s["rise"]}, 0, groups)
    build({2: s["toep"]}, 0, groups)
    pump(8, 4, 1)
    near_finish(0)
    pump(10, 6, 2)
    far_finish(0)
    pump(12, 8, 5)
    onward = conv_out(s["z"], s["toep"], s["rise"], *states, s["inc"], s["y"], False)
    onward(0, blocks // 2)
    pump(14, 10, 7)
    onward(blocks // 2, blocks)
    pump(15, 12, 9)
    loads[2].wait()
    loads[3].wait()

    def modulate(b, _):
        m = (s["outer"][:, lanes(b)].astype(F32) * s["y"][b]).astype(BF16)
        s["mod"][:, lanes(b)] = m
        s["modt"][pl.ds(pl.multiple_of(b * LANES, LANES), LANES), :] = m.T
        return 0

    lax.fori_loop(0, blocks, modulate, 0)

    def wg_terms(k):
        sidx, own = ORDER[k]
        g, first = side(own), spot(sidx, 0, 0)
        height = 4 * part
        lhs = pl.ds(pl.multiple_of(first * part, height), height)

        def tile(n, _):
            cols = pl.ds(pl.multiple_of(n * 256, 256), 256)
            t = jnp.dot(s["modt"][lhs, :], s["og"][g, :, cols], preferred_element_type=F32)
            s["part"][g, pl.ds(first, 4), :, cols] = t.astype(BF16).reshape(4, part, 256)
            return 0

        lax.fori_loop(0, channels // 256, tile, 0)
        for yy in (0, 1):
            rc_copy(k, yy).start()

    def rc_copy(k, yy):
        sidx, own = ORDER[k]
        return remote(
            s["part"].at[side(own), spot(sidx, yy, 1 - c)], s["rc"].at[k, yy],
            s["rc_s"].at[k, yy], s["rc_r"].at[k, yy], c_to,
        )

    def ry_copy(k, t):
        return remote(
            s["ys"].at[k, fine_rows(t)], s["ry"].at[k, fine_rows(t)],
            s["ry_s"].at[k, t], s["ry_r"].at[k, t], y_to,
        )

    def wg_y(k):
        sidx, own = ORDER[k]
        rc_copy(k, 0).wait_recv()
        rc_copy(k, 1).wait_recv()
        for t in range(SUB):
            r = fine_rows(t)
            term = s["part"][side(own), spot(sidx, 1 - y, c), r].astype(F32) + s["rc"][k, 1 - y, r].astype(F32)
            s["ys"][k, r] = term.astype(BF16)
            ry_copy(k, t).start()

    def rz_copy(k, t, back=False):
        r = fine_rows(t)
        if back:
            return remote(s["zs"].at[k, r], s["rb"].at[k // 2, r], s["rz_s"].at[k, t], s["rb_r"].at[k // 2, t], up_to)
        return remote(s["zs"].at[k, r], s["rz"].at[k, r], s["rz_s"].at[k, t], s["rz_r"].at[k, t], down_to)

    def fx_copy(k, t):
        r = fine_rows(t)
        return remote(s["zs"].at[k, r], s["wx"].at[r], s["rz_s"].at[k, t], s["fx_r"].at[t], i, 1 - x)

    scale = 1.0 / math.sqrt(length)

    def z_sends(k, t):
        sidx, own = ORDER[k]
        sends = [(zm > sidx, rz_copy(k, t))]
        if sidx == 1:
            sends.append((zm == 0, rz_copy(k, t, True)))
        if not own:
            sends.append((zm == sidx, fx_copy(k, t)))
        return sends

    def wg_z(k, t):
        sidx, own = ORDER[k]
        g, j = side(own), spot(sidx, y, c)
        r = fine_rows(t)
        ry_copy(k, t).wait_recv()
        s["acc"][...] = (
            s["part"][g, j, r].astype(F32) + s["rc"][k, y, r].astype(F32) + s["ry"][k, r].astype(F32)
        )

        def add_down():
            rz_copy(k, t).wait_recv()
            s["acc"][...] += s["rz"][k, r].astype(F32)

        def add_back():
            rz_copy(k, t, True).wait_recv()
            s["acc"][...] += s["rb"][k // 2, r].astype(F32)

        if sidx == 0:
            when(zm < 3)(add_down)
        else:
            when((zm == 1) | (zm == 2))(add_down)
            when(zm == 1)(add_back)

        def keep():
            s["wo"][r] = s["acc"][...] * scale

        def stage():
            s["zs"][k, r] = s["acc"][...].astype(BF16)

        if own:
            when(zm == sidx)(keep)
            when(zm != sidx)(stage)
        else:
            stage()
        each(z_sends(k, t), "start")

    def wg_last():
        def take():
            for t in range(SUB):
                fx_copy(2, t).wait_recv()
                s["wo"][fine_rows(t)] = s["wx"][fine_rows(t)].astype(F32) * scale

        when(zm >= 2)(take)
        stores[-1].start()

    def wg_drain():
        for k in range(4):
            for yy in (0, 1):
                rc_copy(k, yy).wait_send()
            for t in range(SUB):
                ry_copy(k, t).wait_send()
                each(z_sends(k, t), "wait_send")

    width = channels // PIECES

    def piece(n):
        return pl.ds(n * width, width)

    stores = [
        pltpu.make_async_copy(s["bo"].at[:, piece(n)], block_out.at[:, piece(n)], s["store"].at[n])
        for n in range(PIECES)
    ] + [
        pltpu.make_async_copy(s["outer"], outer_out, s["store"].at[PIECES]),
        pltpu.make_async_copy(s["inner"], inner_out, s["store"].at[PIECES + 1]),
        pltpu.make_async_copy(s["values"], value_out, s["store"].at[PIECES + 2]),
        pltpu.make_async_copy(s["wo"], weight_out, s["store"].at[PIECES + 3]),
    ]

    def b_copy(n):
        return remote(s["bs"].at[n], s["br"].at[n], s["b_s"].at[n], s["b_r"].at[n], i, 1 - x)

    def projected(g, n):
        return jnp.dot(
            s["mod"][...], s["w"][g, :, :, piece(n)].reshape(channels, width), preferred_element_type=F32
        )

    wg_terms(0)
    pump(16, 13, 11)
    wg_terms(1)
    pump(16, 14, 12)
    wg_y(0)
    for n in range(PIECES):
        og_copy(n).wait_recv()
    wg_terms(2)
    pump(16, 15, 13)
    wg_y(1)
    wg_terms(3)
    pump(16, 16, 16)
    w_rest()
    wg_y(2)
    turns = [0] * 4

    def reduce(*counts):
        for n in range(4):
            steps = REDUCE[n][turns[n] : counts[n]]
            turns[n] = max(turns[n], counts[n])

            def go(steps=steps):
                for at in steps:
                    wg_z(at // SUB, at % SUB)

            if steps:
                when(zm == n)(go)

    reduce(1, 0, 0, 1)

    def gradient(p, _):
        cols = pl.ds(pl.multiple_of(p * 2 * LANES, 2 * LANES), 2 * LANES)
        grad = None
        for g in range(2):
            w = s["w"][g, pl.ds(p * (2 * LANES // part), 2 * LANES // part)].reshape(2 * LANES, channels)
            t = lax.dot_general(s["og"][g], w, (((1,), (1,)), ((), ())), preferred_element_type=F32)
            grad = t if grad is None else grad + t
        gate = s["outer"][:, cols].astype(F32)
        filtered_grad = grad * gate
        s["outer"][:, cols] = (
            grad * jnp.concatenate([s["y"][2 * p], s["y"][2 * p + 1]], axis=1)
        ).astype(BF16)
        s["u"][2 * p] = filtered_grad[:, :LANES]
        s["u"][2 * p + 1] = filtered_grad[:, LANES:]
        return 0

    lax.fori_loop(0, blocks // 2, gradient, 0)
    stores[PIECES].start()
    back = conv_in(s["u"], s["z"], s["tail"], *states, s["end"], True)
    back(0, blocks)
    near_start(1)
    wg_y(3)
    reduce(2, 0, 1, 2)
    for n in range(PIECES):
        s["bs"][n] = projected(1 - x, n).astype(BF16)
        b_copy(n).start()
    reduce(2, 0, 2, 4)
    near_finish(1)
    for n in range(PIECES):
        s["bo"][:, piece(n)] = projected(x, n).astype(BF16)
    reduce(4, 2, 4, 5)
    far_finish(1)
    reduce(4, 3, 5, 6)
    home = conv_out(s["z"], s["toep"], s["rise"], *states, s["inc"], s["u"], True)
    home(0, blocks // 2)
    reduce(4, 4, 6, 7)
    home(blocks // 2, blocks)
    reduce(5, 5, 7, 8)

    def grads(b, _):
        gg = s["u"][b]
        gate, value = s["inner"][:, lanes(b)].astype(F32), s["values"][:, lanes(b)].astype(F32)
        s["inner"][:, lanes(b)] = (gg * value).astype(BF16)
        s["values"][:, lanes(b)] = (gg * gate).astype(BF16)
        return 0

    lax.fori_loop(0, blocks, grads, 0)
    stores[PIECES + 1].start()
    stores[PIECES + 2].start()
    reduce(8, 8, 8, 8)
    for n in range(PIECES):
        b_copy(n).wait_recv()
        s["bo"][:, piece(n)] = (s["bo"][:, piece(n)].astype(F32) + s["br"][n].astype(F32)).astype(BF16)
        stores[n].start()
    wg_last()

    w_drain()
    wg_drain()
    for n in range(PIECES):
        og_copy(n).wait_send()
        b_copy(n).wait_send()
    for d in (0, 1):
        for t in (1, 2, 3):
            near_copy(d, t).wait_send()
        far_sends(d, "wait_send")
    for copy in stores:
        copy.wait()


def fused(outer_gate, inner_gate, values, out_weight, skip_gain, residues, decay_rates, out_grad):
    rows, channels = values.shape
    ctx = lax.axis_size("ctx")
    scratch = fused_scratch(rows, channels)
    scratch["acc"] = pltpu.VMEM((channels // 8 // SUB, channels), F32)
    shape = jax.ShapeDtypeStruct
    small = pl.BlockSpec(memory_space=pltpu.VMEM)
    large = pl.BlockSpec(memory_space=pl.ANY)
    tile = shape((rows, channels), BF16)
    return pl.pallas_call(
        functools.partial(fused_kernel, tuple(scratch), rows * ctx),
        out_shape=[tile] * 4 + [shape(out_weight.shape, F32)],
        in_specs=[small] * 3 + [large] * 5,
        out_specs=[large] * 5,
        scratch_shapes=list(scratch.values()),
        compiler_params=pltpu.CompilerParams(
            collective_id=3, has_side_effects=True, vmem_limit_bytes=VMEM_BYTES
        ),
        cost_estimate=pl.CostEstimate(flops=6 * 2**30, bytes_accessed=10 * 2**20, transcendentals=0),
        name="fused",
    )(decay_rates.T, residues.T, skip_gain[None], outer_gate, inner_gate, values, out_weight, out_grad)


def solution(mesh):
    tile = P("ctx", "fsdp")
    small = dict(mesh.shape) == {"ctx": 16, "fsdp": 2}
    return jax.shard_map(
        fused if small else shards,
        mesh=mesh,
        in_specs=(tile, tile, tile, tile, P("fsdp"), P("fsdp", None), P("fsdp", None), tile),
        out_specs=(tile,) * 5,
        check_vma=False,
    )
```

```python
import functools
import math

import jax
import jax.numpy as jnp
from jax import lax
from jax.experimental import pallas as pl
from jax.experimental.pallas import tpu as pltpu
from jax.sharding import PartitionSpec as P

F32 = jnp.float32
BF16 = jnp.bfloat16
LANES = 128
SEGS = 8
VMEM_BYTES = 62 * 2**20


def rows_at(i, steps):
    return pl.ds(i, SEGS, stride=steps)


def spread(row):
    return jnp.broadcast_to(row, (SEGS, LANES))


def segment_states(u_scr, decay_ref, pre_ref, end_ref, reverse):
    modes = decay_ref.shape[0]
    steps = u_scr.shape[0] // SEGS
    a = [spread(jnp.exp(-decay_ref[r : r + 1, :])) for r in range(modes)]

    def step(k, states):
        i = steps - 1 - k if reverse else k
        u = u_scr[rows_at(i, steps), :]
        return tuple(a[r] * states[r] + u for r in range(modes))

    zero = jnp.zeros((SEGS, LANES), F32)
    states = lax.fori_loop(0, steps, step, (zero,) * modes, unroll=4)
    seg = lax.broadcasted_iota(jnp.int32, (SEGS, LANES), 0)

    def moved(x, by):
        if reverse:
            return jnp.where(seg < SEGS - by, pltpu.roll(x, SEGS - by, 0), 0.0)
        return jnp.where(seg >= by, pltpu.roll(x, by, 0), 0.0)

    last = 0 if reverse else SEGS - 1
    for r in range(modes):
        rate = spread(decay_ref[r : r + 1, :])
        x = states[r]
        for by in (1, 2, 4):
            x = x + jnp.exp(-rate * float(steps * by)) * moved(x, by)
        end_ref[r : r + 1, :] = x[last : last + 1, :]
        pre_ref[r] = moved(x, 1)


def full_scan(u_scr, y_scr, decay_ref, res_ref, pre_ref, incoming_ref, reverse):
    modes = decay_ref.shape[0]
    rows = u_scr.shape[0]
    steps = rows // SEGS
    seg = lax.broadcasted_iota(jnp.int32, (SEGS, LANES), 0)
    ahead = ((SEGS - 1 - seg if reverse else seg) * steps).astype(F32)
    a = []
    first = []
    for r in range(modes):
        rate = spread(decay_ref[r : r + 1, :])
        a.append(jnp.exp(-rate))
        first.append(pre_ref[r] + jnp.exp(-rate * ahead) * incoming_ref[r : r + 1, :])
    res = [spread(res_ref[r : r + 1, :]) for r in range(modes)]

    def step(k, states):
        i = steps - 1 - k if reverse else k
        u = u_scr[rows_at(i, steps), :]
        states = tuple(a[r] * states[r] + u for r in range(modes))
        terms = [res[r] * states[r] for r in range(modes)]
        while len(terms) > 1:
            terms = [p + q for p, q in zip(terms[::2], terms[1::2])]
        y_scr[rows_at(i, steps), :] = terms[0]
        return states

    lax.fori_loop(0, steps, step, tuple(first), unroll=2)


def forward_ends(inner_ref, values_ref, decay_ref, pre_ref, end_ref, u_scr):
    u_scr[...] = inner_ref[...].astype(F32) * values_ref[...].astype(F32)
    segment_states(u_scr, decay_ref, pre_ref, end_ref, False)


def forward_finish(
    inner_ref, values_ref, outer_ref, decay_ref, res_ref, skip_ref, pre_ref, incoming_ref,
    filtered_ref, modulated_ref, u_scr, y_scr,
):
    u_scr[...] = inner_ref[...].astype(F32) * values_ref[...].astype(F32)
    full_scan(u_scr, y_scr, decay_ref, res_ref, pre_ref, incoming_ref, False)
    filtered = y_scr[...] + skip_ref[...] * u_scr[...]
    filtered_ref[...] = filtered
    modulated_ref[...] = (outer_ref[...].astype(F32) * filtered).astype(BF16)


def backward_ends(own_ref, other_ref, outer_ref, decay_ref, pre_ref, end_ref, u_scr):
    grad = own_ref[...].astype(F32) + other_ref[...].astype(F32)
    u_scr[...] = grad * outer_ref[...].astype(F32)
    segment_states(u_scr, decay_ref, pre_ref, end_ref, True)


def backward_finish(
    own_ref, other_ref, outer_ref, inner_ref, values_ref, filtered_ref, decay_ref, res_ref, skip_ref,
    pre_ref, incoming_ref, outer_grad_ref, inner_grad_ref, value_grad_ref, u_scr, y_scr,
):
    grad = own_ref[...].astype(F32) + other_ref[...].astype(F32)
    u_scr[...] = grad * outer_ref[...].astype(F32)
    outer_grad_ref[...] = (grad * filtered_ref[...]).astype(BF16)
    full_scan(u_scr, y_scr, decay_ref, res_ref, pre_ref, incoming_ref, True)
    gated_grad = y_scr[...] + skip_ref[...] * u_scr[...]
    inner_grad_ref[...] = (gated_grad * values_ref[...].astype(F32)).astype(BF16)
    value_grad_ref[...] = (gated_grad * inner_ref[...].astype(F32)).astype(BF16)


def by_lanes(kernel, operands, outs, rows, scans):
    channels = operands[0].shape[-1]

    def spec(x):
        lead = x.shape[:-1]
        return pl.BlockSpec(lead + (LANES,), lambda c, n=len(lead): (0,) * n + (c,))

    work = rows * channels * (24000 if scans > 1 else 16000)
    moved = sum(math.prod(x.shape) * x.dtype.itemsize for x in list(operands) + list(outs))
    return pl.pallas_call(
        kernel,
        grid=(channels // LANES,),
        out_shape=outs,
        in_specs=[spec(x) for x in operands],
        out_specs=[spec(x) for x in outs],
        scratch_shapes=[pltpu.VMEM((rows, LANES), F32)] * scans,
        cost_estimate=pl.CostEstimate(flops=work, bytes_accessed=moved, transcendentals=0),
        name=kernel.__name__,
    )(*operands)


def prefix_kernel(reverse, rows, end_ref, decay_ref, out_ref, sent, got, send_sem, recv_sem):
    me, n = lax.axis_index("ctx"), lax.axis_size("ctx")
    hops = [1 << k for k in range(sent.shape[0])]
    barrier = pltpu.get_barrier_semaphore()
    for hop in hops:
        for peer in (lax.rem(me + hop, n), lax.rem(me + n - hop, n)):
            pl.semaphore_signal(
                barrier, inc=1, device_id={"ctx": peer}, device_id_type=pl.DeviceIdType.MESH
            )
    pl.semaphore_wait(barrier, 2 * len(hops))
    decay = decay_ref[...]
    upto = end_ref[...]
    before = jnp.zeros_like(upto)
    for k, hop in enumerate(hops):
        sent[k] = upto.astype(BF16)
        copy = pltpu.make_async_remote_copy(
            src_ref=sent.at[k],
            dst_ref=got.at[k],
            send_sem=send_sem.at[k],
            recv_sem=recv_sem.at[k],
            device_id={"ctx": lax.rem(me + (n - hop if reverse else hop), n)},
            device_id_type=pl.DeviceIdType.MESH,
        )
        copy.start()
        near = jnp.exp(-decay * float(rows * (hop - 1)))
        far = jnp.exp(-decay * float(rows * hop))
        copy.wait()
        inside = (me + hop < n) if reverse else (me >= hop)
        term = got[k].astype(F32) * jnp.where(inside, 1.0, 0.0)
        before = before + near * term
        upto = upto + far * term
    out_ref[...] = before


def prefix(end, decay, rows, reverse):
    hops = max(1, (lax.axis_size("ctx") - 1).bit_length())
    whole = pl.BlockSpec(memory_space=pltpu.VMEM)
    return pl.pallas_call(
        functools.partial(prefix_kernel, reverse, rows),
        out_shape=jax.ShapeDtypeStruct(end.shape, F32),
        in_specs=[whole, whole],
        out_specs=whole,
        scratch_shapes=[
            pltpu.VMEM((hops,) + end.shape, BF16),
            pltpu.VMEM((hops,) + end.shape, BF16),
            pltpu.SemaphoreType.DMA((hops,)),
            pltpu.SemaphoreType.DMA((hops,)),
        ],
        compiler_params=pltpu.CompilerParams(
            collective_id=2 if reverse else 1, has_side_effects=True
        ),
        cost_estimate=pl.CostEstimate(flops=18 * 10**9, bytes_accessed=0, transcendentals=0),
        name="prefix_back" if reverse else "prefix_ahead",
    )(end, decay)


def shards(outer_gate, inner_gate, values, out_weight, skip_gain, residues, decay_rates, out_grad):
    rows, channels = values.shape
    modes = decay_rates.shape[1]
    ctx, fsdp = lax.axis_size("ctx"), lax.axis_size("fsdp")
    at = lax.axis_index("fsdp")
    swap = [(0, 1), (1, 0)]
    shape = jax.ShapeDtypeStruct
    panel = lax.all_gather(out_weight, "ctx", axis=0, tiled=True)
    decay = decay_rates.T
    res = residues.T
    skip = skip_gain[None]
    state_outs = [shape((modes, SEGS, channels), F32), shape((modes, channels), F32)]
    pre, end = by_lanes(forward_ends, (inner_gate, values, decay), state_outs, rows, 1)
    incoming = prefix(end, decay, rows, False)
    filtered, modulated = by_lanes(
        forward_finish,
        (inner_gate, values, outer_gate, decay, res, skip, pre, incoming),
        [shape((rows, channels), F32), shape((rows, channels), BF16)],
        rows,
        2,
    )
    if fsdp == 2:
        other = lax.ppermute(modulated, "fsdp", swap)
        first = jnp.where(at == 0, modulated, other)
        second = jnp.where(at == 0, other, modulated)
        gathered = jnp.concatenate([first, second], axis=1)
        mine = lax.dynamic_slice_in_dim(panel, at * channels, channels, 0)
        theirs = lax.dynamic_slice_in_dim(panel, (1 - at) * channels, channels, 0)
        for_them = jnp.dot(out_grad, theirs.T, preferred_element_type=F32).astype(BF16)
        from_them = lax.ppermute(for_them, "fsdp", swap)
        own = jnp.dot(out_grad, mine.T, preferred_element_type=F32).astype(BF16)
    else:
        gathered = lax.all_gather(modulated, "fsdp", axis=1, tiled=True)
        partial = jnp.dot(out_grad, panel.T, preferred_element_type=F32).astype(BF16)
        own = lax.psum_scatter(partial, "fsdp", scatter_dimension=1, tiled=True)
        from_them = jnp.zeros_like(own)
    grad_rows = lax.dot_general(
        gathered, out_grad, (((0,), (0,)), ((), ())), preferred_element_type=F32
    ).astype(BF16)
    weight_grad = lax.psum_scatter(grad_rows, "ctx", scatter_dimension=0, tiled=True)
    block_out = jnp.dot(gathered, panel, preferred_element_type=F32).astype(BF16)
    pre, end = by_lanes(
        backward_ends, (own, from_them, outer_gate, decay), state_outs, rows, 1
    )
    incoming = prefix(end, decay, rows, True)
    outer_grad, inner_grad, value_grad = by_lanes(
        backward_finish,
        (own, from_them, outer_gate, inner_gate, values, filtered, decay, res, skip, pre, incoming),
        [shape((rows, channels), BF16)] * 3,
        rows,
        2,
    )
    weight_grad, value_grad = lax.optimization_barrier((weight_grad, value_grad))
    weight_grad = weight_grad.astype(F32) * (1.0 / math.sqrt(rows * ctx))
    return (block_out, outer_grad, inner_grad, value_grad, weight_grad)


TAPS = 16
GRAN = 16
PER = LANES // GRAN
WIDE = TAPS * GRAN
SUB = 2
PIECES = 4
GATHER = (
    (0, 1, 2, 3, 4, 5, 8, 9, 6, 7, 10, 11, 12, 13, 14, 15),
    (0, 1, 2, 8, 3, 9, 4, 5, 6, 10, 7, 11, 12, 13, 14, 15),
    (0, 1, 2, 3, 8, 9, 4, 10, 5, 11, 6, 7, 12, 13, 14, 15),
)
REDUCE = (
    (0, 1, 4, 5, 2, 3, 6, 7),
    (2, 3, 4, 5, 6, 7, 0, 1),
    (2, 3, 4, 5, 6, 7, 0, 1),
    (2, 3, 4, 5, 6, 7),
)
MESH = pl.DeviceIdType.MESH
ORDER = ((1, True), (0, True), (1, False), (0, False))


def regroup(v):
    lane = lax.broadcasted_iota(jnp.int32, v[0].shape, 1) // GRAN
    v = list(v)
    for m in (1, 2, 4):
        low = (lane & m) == 0
        for i in range(PER):
            if i & m:
                continue
            p, q = v[i], v[i + m]
            v[i] = jnp.where(low, p, pltpu.roll(q, GRAN * m, 1))
            v[i + m] = jnp.where(low, pltpu.roll(p, LANES - GRAN * m, 1), q)
    return v


def row_at(k, s, steps, reverse):
    return TAPS * (steps - 1 - k) + TAPS - 1 - s if reverse else TAPS * k + s


def regroup_filters(decay_ref, res_ref, skip_ref, par_ref, gen_ref):
    row = lax.broadcasted_iota(jnp.int32, (SEGS, LANES), 0)
    lag = lax.broadcasted_iota(jnp.int32, (TAPS, LANES), 0)
    lags = lag.astype(F32)

    def block(b, _):
        cols = pl.ds(pl.multiple_of(b * LANES, LANES), LANES)
        kern = jnp.where(lag == 0, jnp.broadcast_to(skip_ref[:, cols], (TAPS, LANES)), 0.0)
        for r in range(TAPS):
            kern = kern + res_ref[r : r + 1, cols] * jnp.exp(-decay_ref[r : r + 1, cols] * lags)
        gen_ref[...] = kern
        for half in range(2):
            v = []
            for s in range(half * PER, (half + 1) * PER):
                rate = jnp.broadcast_to(decay_ref[s : s + 1, cols], (SEGS, LANES))
                res = jnp.broadcast_to(res_ref[s : s + 1, cols], (SEGS, LANES))
                tap = jnp.broadcast_to(gen_ref[s : s + 1, :], (SEGS, LANES))
                v.append(jnp.where(row == 0, rate, jnp.where(row == 1, res, tap)))
            for h, out in enumerate(regroup(v)):
                par_ref[b * PER + h, :, half * LANES : (half + 1) * LANES] = out
        return 0

    lax.fori_loop(0, decay_ref.shape[1] // LANES, block, 0)


def build_tables(par_ref, rate_ref, taps_ref, outs, first, groups):
    shape = (GRAN, WIDE)
    diagonal = lax.broadcasted_iota(jnp.int32, shape, 1) % GRAN == lax.broadcasted_iota(jnp.int32, shape, 0)
    lag = lax.broadcasted_iota(jnp.int32, (TAPS, WIDE), 0)
    lags = lag.astype(F32)
    at = lax.broadcasted_iota(jnp.int32, (TAPS, WIDE), 1) // GRAN

    def group(n, _):
        for d in range(4):
            g = first + 4 * n + d
            rate = par_ref[g, 0:1, :]
            for i in outs:
                if i == 0:
                    rate_ref[pl.ds(g, 1), :] = rate
                    taps_ref[d, i] = jnp.exp(-rate * (TAPS - 1 - lags))
                elif i == 1:
                    taps_ref[d, i] = par_ref[g, 1:2, :] * jnp.exp(-rate * (lags + 1))
                else:
                    kern = jnp.broadcast_to(par_ref[g, 2:3, :], (TAPS, WIDE))
                    taps_ref[d, i] = jnp.where(at >= lag, pltpu.roll(kern, 0, 1, stride=GRAN, stride_axis=0), 0.0)
        for d in range(4):
            g = first + 4 * n + d
            for i, out in outs.items():
                for s in range(TAPS):
                    line = jnp.broadcast_to(taps_ref[d, i, s : s + 1, :], shape)
                    out[g, s * GRAN : (s + 1) * GRAN, :] = jnp.where(diagonal, line, 0.0).astype(BF16)
        return 0

    lax.fori_loop(0, groups // 4, group, 0)


def moved(x, by, reverse):
    seg = lax.broadcasted_iota(jnp.int32, x.shape, 0)
    if reverse:
        return jnp.where(seg < SEGS - by, pltpu.roll(x, SEGS - by, 0), 0.0)
    return jnp.where(seg >= by, pltpu.roll(x, by, 0), 0.0)


def conv_in(u_ref, z_ref, tail_ref, rate_ref, e_ref, pre_ref, end_ref, reverse):
    blocks, rows, _ = u_ref.shape
    stride = rows // SEGS
    steps = stride // TAPS
    last = 0 if reverse else SEGS - 1

    def split(b):
        for half in range(2):
            for k in range(0, steps, 2):
                pair = [
                    regroup(
                        [
                            u_ref[b, pl.ds(row_at(n, half * PER + j, steps, reverse), SEGS, stride=stride), :]
                            for j in range(PER)
                        ]
                    )
                    for n in (k, k + 1)
                ]
                for h in range(PER):
                    z_ref[b * PER + h, k * SEGS : (k + 2) * SEGS, half * LANES : (half + 1) * LANES] = (
                        jnp.concatenate([pair[0][h], pair[1][h]], axis=0).astype(BF16)
                    )

    def ends(b):
        for h in range(PER):
            g = b * PER + h
            e = jnp.dot(z_ref[g], tail_ref[g], preferred_element_type=F32)
            e_ref[g] = e
            rate = jnp.broadcast_to(rate_ref[pl.ds(g, 1), :], (SEGS, WIDE))
            a = jnp.exp(-rate * float(TAPS))
            x = e[0:SEGS]
            for k in range(1, steps):
                x = a * x + e[k * SEGS : (k + 1) * SEGS]
            for by in (1, 2, 4):
                x = x + jnp.exp(-rate * float(TAPS * steps * by)) * moved(x, by, reverse)
            end_ref[pl.ds(g, 1), :] = x[last : last + 1, :]
            pre_ref[g] = moved(x, 1, reverse)

    return pipelined(split, ends, blocks)


def pipelined(first, second, blocks):
    def body(b, _):
        second(b - 1)
        first(b)
        return 0

    def run(lo, hi):
        if lo == 0:
            first(0)
        lax.fori_loop(max(lo, 1), hi, body, 0)
        if hi == blocks:
            second(blocks - 1)

    return run


def conv_out(z_ref, toep_ref, rise_ref, rate_ref, e_ref, pre_ref, inc_ref, y_ref, reverse):
    groups, chunks, _ = z_ref.shape
    steps = chunks // SEGS
    stride = y_ref.shape[1] // SEGS

    def finish(b):
        seg = lax.broadcasted_iota(jnp.int32, (SEGS, WIDE), 0)
        ahead = ((SEGS - 1 - seg if reverse else seg) * (TAPS * steps)).astype(F32)
        for h in range(PER):
            g = b * PER + h
            rate = jnp.broadcast_to(rate_ref[pl.ds(g, 1), :], (SEGS, WIDE))
            a = jnp.exp(-rate * float(TAPS))
            x = pre_ref[g] + jnp.exp(-rate * ahead) * inc_ref[pl.ds(g, 1), :]
            states = [x]
            for k in range(steps - 1):
                x = a * x + e_ref[g, k * SEGS : (k + 1) * SEGS]
                states.append(x)
            s = jnp.concatenate(states, axis=0).astype(BF16)
            y = jnp.dot(z_ref[g], toep_ref[g], preferred_element_type=F32)
            e_ref[g] = y + lax.dot_general(s, rise_ref[g], (((1,), (1,)), ((), ())), preferred_element_type=F32)

    def merge(b):
        for half in range(2):
            for k in range(steps):
                v = regroup(
                    [
                        e_ref[b * PER + h, k * SEGS : (k + 1) * SEGS, half * LANES : (half + 1) * LANES]
                        for h in range(PER)
                    ]
                )
                for j in range(PER):
                    y_ref[b, pl.ds(row_at(k, half * PER + j, steps, reverse), SEGS, stride=stride), :] = v[j]

    return pipelined(finish, merge, groups // PER)


def fused_scratch(rows, channels):
    blocks, groups = channels // LANES, channels // GRAN
    chunks = rows // TAPS
    part = channels // 8
    dma = pltpu.SemaphoreType.DMA
    v = pltpu.VMEM
    return dict(
        tail=v((groups, WIDE, WIDE), BF16),
        rise=v((groups, WIDE, WIDE), BF16),
        toep=v((groups, WIDE, WIDE), BF16),
        par=v((groups, SEGS, WIDE), F32),
        rate=v((groups, WIDE), F32),
        taps=v((4, 3, TAPS, WIDE), F32),
        gen=v((TAPS, LANES), F32),
        inner=v((rows, channels), BF16),
        values=v((rows, channels), BF16),
        outer=v((rows, channels), BF16),
        og=v((2, rows, channels), BF16),
        w=v((2, 8, part, channels), BF16),
        u=v((blocks, rows, LANES), F32),
        y=v((blocks, rows, LANES), F32),
        z=v((groups, chunks, WIDE), BF16),
        e=v((groups, chunks, WIDE), F32),
        pre=v((groups, SEGS, WIDE), F32),
        end=v((groups, WIDE), F32),
        before=v((groups, WIDE), F32),
        inc=v((groups, WIDE), F32),
        near=v((2, 4, groups, WIDE), BF16),
        total=v((2, groups, WIDE), BF16),
        far=v((2, 4, groups, WIDE), BF16),
        mod=v((rows, channels), BF16),
        modt=v((channels, rows), BF16),
        bs=v((PIECES, rows, channels // PIECES), BF16),
        br=v((PIECES, rows, channels // PIECES), BF16),
        bo=v((rows, channels), BF16),
        part=v((2, 8, part, channels), BF16),
        rc=v((4, 2, part, channels), BF16),
        ys=v((4, part, channels), BF16),
        ry=v((4, part, channels), BF16),
        zs=v((4, part, channels), BF16),
        rz=v((4, part, channels), BF16),
        rb=v((2, part, channels), BF16),
        ro=v((part, channels), BF16),
        wx=v((part, channels), BF16),
        wo=v((part, channels), F32),
        load=dma((5,)),
        store=dma((PIECES + 4,)),
        og_s=dma((PIECES,)),
        og_r=dma((PIECES,)),
        wx_s=dma((SUB,)),
        w_r=dma((2, 8, SUB)),
        up_s=dma((4, SUB)),
        down_s=dma((4, SUB)),
        y_s=dma((4, SUB)),
        c_s=dma((4, SUB)),
        cy_s=dma((4, SUB)),
        near_s=dma((2, 4)),
        near_r=dma((2, 4)),
        far_s=dma((2, 4)),
        far_r=dma((2, 4)),
        b_s=dma((PIECES,)),
        b_r=dma((PIECES,)),
        rc_s=dma((4, 2)),
        rc_r=dma((4, 2)),
        ry_s=dma((4, SUB)),
        ry_r=dma((4, SUB)),
        rz_s=dma((4, SUB)),
        rz_r=dma((4, SUB)),
        rb_r=dma((2, SUB)),
        ro_r=dma((SUB,)),
        fx_s=dma((SUB,)),
        fx_r=dma((SUB,)),
    )


def fused_kernel(names, length, *refs):
    decay, res, skip, outer_in, inner_in, values_in, weight_in, grad_in = refs[:8]
    block_out, outer_out, inner_out, value_out, weight_out = refs[8:13]
    s = dict(zip(names, refs[13:]))
    rows, channels = inner_in.shape
    part = weight_in.shape[0]
    blocks = channels // LANES
    groups = channels // GRAN
    fine = part // SUB
    i, x = lax.axis_index("ctx"), lax.axis_index("fsdp")
    z, y, c = i // 4, (i // 2) % 2, i % 2
    zm = jnp.where(x == 0, z, 3 - z)
    q = i % 4

    def ctx_at(z, y, c):
        return z * 4 + y * 2 + c

    up_to = ctx_at(z + 1 - 2 * x, y, c)
    down_to = ctx_at(z - 1 + 2 * x, y, c)
    y_to = ctx_at(z, 1 - y, c)
    c_to = ctx_at(z, y, 1 - c)

    def remote(src, dst, send, recv, ctx, fsdp=x):
        return pltpu.make_async_remote_copy(
            src_ref=src, dst_ref=dst, send_sem=send, recv_sem=recv,
            device_id={"ctx": ctx, "fsdp": fsdp}, device_id_type=MESH,
        )

    def when(cond):
        return pl.when(cond)

    loads = [
        pltpu.make_async_copy(inner_in, s["inner"], s["load"].at[0]),
        pltpu.make_async_copy(values_in, s["values"], s["load"].at[1]),
        pltpu.make_async_copy(outer_in, s["outer"], s["load"].at[2]),
        pltpu.make_async_copy(grad_in, s["og"].at[x], s["load"].at[3]),
    ]
    for copy in loads:
        copy.start()
    jown = (z % 2) * 4 + q
    source = zm < 2
    keep_w = pltpu.make_async_copy(weight_in, s["w"].at[x, jown], s["load"].at[4])
    when(source)(keep_w.start)
    s["far"][...] = jnp.zeros_like(s["far"])

    barrier = pltpu.get_barrier_semaphore()
    peers = [(ctx_at(z, (q + t) % 4 // 2, (q + t) % 2), x) for t in (1, 2, 3)]
    peers += [(ctx_at((z + t) % 4, y, c), x) for t in (1, 2, 3)] + [(i, 1 - x)]
    for ctx, fsdp in peers:
        pl.semaphore_signal(barrier, inc=1, device_id={"ctx": ctx, "fsdp": fsdp}, device_id_type=MESH)
    pl.semaphore_wait(barrier, len(peers))

    def fine_rows(t):
        return pl.ds(t * fine, fine)

    def spot(sidx, yy, cc):
        return jnp.where(x == 0, sidx, 1 - sidx) * 4 + yy * 2 + cc

    def side(own):
        return x if own else 1 - x

    def w_cross(t):
        return remote(
            weight_in.at[fine_rows(t)], s["w"].at[x, jown, fine_rows(t)], s["wx_s"].at[t],
            s["w_r"].at[x, jown, t], i, 1 - x,
        )

    def w_sends(src, g, j, k, t, up, down):
        dst = s["w"].at[g, j, fine_rows(t)]
        recv = s["w_r"].at[g, j, t]
        return [
            (up, remote(src, dst, s["up_s"].at[k, t], recv, up_to)),
            (down, remote(src, dst, s["down_s"].at[k, t], recv, down_to)),
            (None, remote(src, dst, s["y_s"].at[k, t], recv, y_to)),
            (None, remote(src, dst, s["c_s"].at[k, t], recv, c_to)),
        ]

    def each(sends, act):
        for cond, copy in sends:
            if cond is None:
                getattr(copy, act)()
            elif cond is not False:
                when(cond)(getattr(copy, act))

    def place(p):
        low = zm == 0
        sidx = jnp.where(low, p // 2, 1 - p % 2)
        own = jnp.where(low, p % 2 == 0, p < 2)
        return sidx, jnp.where(own, x, 1 - x)

    def own_sends(t):
        return w_sends(weight_in.at[fine_rows(t)], x, jown, 0, t, None, zm == 1)

    def line_sends(p, t):
        sidx, g = place(p)
        j = spot(sidx, y, c)
        src = s["w"].at[g, j, fine_rows(t)]
        up = ((sidx == 0) & (zm < 3)) | ((sidx == 1) & (zm >= 1) & (zm < 3))
        return w_sends(src, g, j, p, t, up, (sidx == 1) & (zm == 1))

    def w_wait(g, j, t):
        dst = s["w"].at[g, j, fine_rows(t)]
        remote(dst, dst, s["wx_s"].at[t], s["w_r"].at[g, j, t], c_to).wait_recv()

    def pump_line(p, t):
        def go():
            sidx, g = place(p)
            w_wait(g, spot(sidx, y, c), t)
            each(line_sends(p, t), "start")

        if p == 0:
            when(zm >= 2)(go)
        else:
            go()

    def y_pass(p, t):
        sidx, g = place(p)
        j = spot(sidx, 1 - y, c)
        at = s["w"].at[g, j, fine_rows(t)]
        return remote(at, at, s["cy_s"].at[p, t], s["w_r"].at[g, j, t], c_to)

    def pump_y(p, t):
        sidx, g = place(p)
        w_wait(g, spot(sidx, 1 - y, c), t)
        y_pass(p, t).start()

    def w_rest():
        for sidx, own in ORDER:
            for t in range(SUB):
                for yy in (0, 1):
                    w_wait(side(own), spot(sidx, yy, 1 - c), t)
        when(source)(keep_w.wait)

    def w_drain():
        def cross():
            for t in range(SUB):
                w_cross(t).wait_send()

        def owned():
            for t in range(SUB):
                each(own_sends(t), "wait_send")

        when(zm >= 2)(cross)
        when(source)(owned)
        for p in range(4):
            for t in range(SUB):
                if p == 0:
                    when(zm >= 2)(functools.partial(each, line_sends(p, t), "wait_send"))
                else:
                    each(line_sends(p, t), "wait_send")
                y_pass(p, t).wait_send()

    def start_cross():
        for t in range(SUB):
            w_cross(t).start()

    def start_owned():
        for t in range(SUB):
            each(own_sends(t), "start")

    when(zm >= 2)(start_cross)
    when(source)(start_owned)

    slab = rows // PIECES

    def og_copy(n):
        return remote(
            grad_in.at[pl.ds(n * slab, slab)], s["og"].at[x, pl.ds(n * slab, slab)],
            s["og_s"].at[n], s["og_r"].at[n], i, 1 - x,
        )

    for n in range(PIECES):
        og_copy(n).start()

    def listed(order):
        parts = 4 * SUB
        return [(pump_line if n < parts else pump_y, n % parts // SUB, n % SUB) for n in order]

    classes = (source, zm == 2, zm == 3)
    orders = [listed(order) for order in GATHER]
    done = [0] * len(classes)

    def pump(*counts):
        for n, cond in enumerate(classes):
            steps = orders[n][done[n] : counts[n]]
            done[n] = max(done[n], counts[n])

            def go(steps=steps):
                for act, p, t in steps:
                    act(p, t)

            if steps:
                when(cond)(go)

    def rate():
        return s["rate"][...]

    def near_copy(d, t):
        to = (q + t) % 4
        at = s["near"].at[d, q]
        return remote(at, at, s["near_s"].at[d, t], s["near_r"].at[d, q], ctx_at(z, to // 2, to % 2))

    def near_wait(d, t):
        frm = (q + t) % 4
        at = s["near"].at[d, frm]
        remote(at, at, s["near_s"].at[d, t], s["near_r"].at[d, frm], c_to).wait_recv()

    def far_copy(d, t):
        to = z + t if d == 0 else z - t
        at = s["far"].at[d, z]
        return remote(s["total"].at[d], at, s["far_s"].at[d, t], s["far_r"].at[d, z], ctx_at(to, y, c))

    def far_sends(d, act):
        for t in (1, 2, 3):
            cond = z + t < 4 if d == 0 else z - t >= 0
            when(cond)(getattr(far_copy(d, t), act))

    def near_start(d):
        s["near"][d, q] = s["end"][...].astype(BF16)
        for t in (1, 2, 3):
            near_copy(d, t).start()

    def near_finish(d):
        for t in (1, 2, 3):
            near_wait(d, t)
        total = jnp.zeros((groups, WIDE), F32)
        before = jnp.zeros((groups, WIDE), F32)
        mine = q if d == 0 else 3 - q
        for k in range(4):
            rank = k if d == 0 else 3 - k
            term = s["near"][d, k].astype(F32)
            total = total + jnp.exp(-rate() * float(rows * (3 - rank))) * term
            gap = mine - rank
            weight = jnp.exp(-rate() * (rows * jnp.maximum(gap - 1, 0)).astype(F32))
            before = before + jnp.where(gap > 0, weight, 0.0) * term
        s["before"][...] = before
        s["total"][d] = total.astype(BF16)
        far_sends(d, "start")

    def far_finish(d):
        for t in (1, 2, 3):
            frm = z - t if d == 0 else z + t
            at = s["far"].at[d, frm]
            copy = remote(at, at, s["far_s"].at[d, t], s["far_r"].at[d, frm], c_to)
            when(z - t >= 0 if d == 0 else z + t < 4)(copy.wait_recv)
        into = jnp.zeros((groups, WIDE), F32)
        for k in range(4):
            gap = z - k if d == 0 else k - z
            weight = jnp.exp(-rate() * (4 * rows * jnp.maximum(gap - 1, 0)).astype(F32))
            into = into + jnp.where(gap > 0, weight, 0.0) * s["far"][d, k].astype(F32)
        mine = q if d == 0 else 3 - q
        s["inc"][...] = s["before"][...] + jnp.exp(-rate() * (rows * mine).astype(F32)) * into

    def lanes(b):
        return pl.ds(pl.multiple_of(b * LANES, LANES), LANES)

    build = functools.partial(build_tables, s["par"], s["rate"], s["taps"])
    later = {1: s["rise"], 2: s["toep"]}
    regroup_filters(decay, res, skip, s["par"], s["gen"])
    loads[0].wait()
    loads[1].wait()

    def gated(b, _):
        s["u"][b] = s["inner"][:, lanes(b)].astype(F32) * s["values"][:, lanes(b)].astype(F32)
        return 0

    lax.fori_loop(0, blocks, gated, 0)
    build({0: s["tail"]}, 0, groups)
    states = (s["rate"], s["e"], s["pre"])
    ahead = conv_in(s["u"], s["z"], s["tail"], *states, s["end"], False)
    ahead(0, blocks // 2)
    pump(4, 1, 0)
    ahead(blocks // 2, blocks)
    near_start(0)
    pump(8, 2, 0)
    build({1: s["rise"]}, 0, groups)
    build({2: s["toep"]}, 0, groups)
    pump(8, 4, 1)
    near_finish(0)
    pump(10, 7, 4)
    far_finish(0)
    pump(12, 8, 6)
    onward = conv_out(s["z"], s["toep"], s["rise"], *states, s["inc"], s["y"], False)
    onward(0, blocks // 2)
    pump(14, 9, 7)
    onward(blocks // 2, blocks)
    pump(15, 12, 9)
    loads[2].wait()
    loads[3].wait()

    def modulate(b, _):
        m = (s["outer"][:, lanes(b)].astype(F32) * s["y"][b]).astype(BF16)
        s["mod"][:, lanes(b)] = m
        s["modt"][pl.ds(pl.multiple_of(b * LANES, LANES), LANES), :] = m.T
        return 0

    lax.fori_loop(0, blocks, modulate, 0)

    def wg_terms(k):
        sidx, own = ORDER[k]
        g, first = side(own), spot(sidx, 0, 0)
        height = 4 * part
        lhs = pl.ds(pl.multiple_of(first * part, height), height)

        def tile(n, _):
            cols = pl.ds(pl.multiple_of(n * 256, 256), 256)
            t = jnp.dot(s["modt"][lhs, :], s["og"][g, :, cols], preferred_element_type=F32)
            s["part"][g, pl.ds(first, 4), :, cols] = t.astype(BF16).reshape(4, part, 256)
            return 0

        lax.fori_loop(0, channels // 256, tile, 0)
        for yy in (0, 1):
            rc_copy(k, yy).start()

    def rc_copy(k, yy):
        sidx, own = ORDER[k]
        return remote(
            s["part"].at[side(own), spot(sidx, yy, 1 - c)], s["rc"].at[k, yy],
            s["rc_s"].at[k, yy], s["rc_r"].at[k, yy], c_to,
        )

    def ry_copy(k, t):
        return remote(
            s["ys"].at[k, fine_rows(t)], s["ry"].at[k, fine_rows(t)],
            s["ry_s"].at[k, t], s["ry_r"].at[k, t], y_to,
        )

    def ship_copy(t, own_row):
        r = fine_rows(t)
        if own_row:
            return rz_copy(0, t)
        return remote(s["ys"].at[0, r], s["ro"].at[r], s["ry_s"].at[0, t], s["ro_r"].at[t], down_to)

    def wg_ship():
        rc_copy(0, 0).wait_recv()
        rc_copy(0, 1).wait_recv()
        for t in range(SUB):
            r = fine_rows(t)
            for own_row, to in ((False, "ys"), (True, "zs")):
                yy = y if own_row else 1 - y
                term = s["part"][x, spot(1, yy, c), r].astype(F32) + s["rc"][0, yy, r].astype(F32)
                s[to][0, r] = term.astype(BF16)
                ship_copy(t, own_row).start()

    def wg_y(k):
        sidx, own = ORDER[k]
        rc_copy(k, 0).wait_recv()
        rc_copy(k, 1).wait_recv()
        for t in range(SUB):
            r = fine_rows(t)
            term = s["part"][side(own), spot(sidx, 1 - y, c), r].astype(F32) + s["rc"][k, 1 - y, r].astype(F32)
            s["ys"][k, r] = term.astype(BF16)
            if k == 0:

                def shipped(t=t, r=r):
                    ship_copy(t, False).wait_recv()
                    s["ys"][0, r] = (s["ys"][0, r].astype(F32) + s["ro"][r].astype(F32)).astype(BF16)

                when(zm == 2)(shipped)
            ry_copy(k, t).start()

    def rz_copy(k, t, back=False):
        r = fine_rows(t)
        if back:
            return remote(s["zs"].at[k, r], s["rb"].at[k // 2, r], s["rz_s"].at[k, t], s["rb_r"].at[k // 2, t], up_to)
        return remote(s["zs"].at[k, r], s["rz"].at[k, r], s["rz_s"].at[k, t], s["rz_r"].at[k, t], down_to)

    def fx_copy(k, t):
        r = fine_rows(t)
        return remote(s["zs"].at[k, r], s["wx"].at[r], s["rz_s"].at[k, t], s["fx_r"].at[t], i, 1 - x)

    scale = 1.0 / math.sqrt(length)

    def z_sends(k, t):
        sidx, own = ORDER[k]
        sends = [(zm > sidx, rz_copy(k, t))]
        if sidx == 1:
            sends.append((zm == 0, rz_copy(k, t, True)))
        if not own:
            sends.append((zm == sidx, fx_copy(k, t)))
        return sends

    def wg_z(k, t):
        sidx, own = ORDER[k]
        g, j = side(own), spot(sidx, y, c)
        r = fine_rows(t)
        ry_copy(k, t).wait_recv()
        s["acc"][...] = (
            s["part"][g, j, r].astype(F32) + s["rc"][k, y, r].astype(F32) + s["ry"][k, r].astype(F32)
        )

        def add_down():
            rz_copy(k, t).wait_recv()
            s["acc"][...] += s["rz"][k, r].astype(F32)

        def add_back():
            rz_copy(k, t, True).wait_recv()
            s["acc"][...] += s["rb"][k // 2, r].astype(F32)

        if sidx == 0:
            when(zm < 3)(add_down)
        else:
            when((zm == 1) | (zm == 2))(add_down)
            when(zm == 1)(add_back)

        def keep():
            s["wo"][r] = s["acc"][...] * scale

        def stage():
            s["zs"][k, r] = s["acc"][...].astype(BF16)

        if own:
            when(zm == sidx)(keep)
            when(zm != sidx)(stage)
        else:
            stage()
        each(z_sends(k, t), "start")

    def wg_last():
        def take():
            for t in range(SUB):
                fx_copy(2, t).wait_recv()
                s["wo"][fine_rows(t)] = s["wx"][fine_rows(t)].astype(F32) * scale

        when(zm >= 2)(take)
        stores[-1].start()

    def wg_drain():
        for k in range(4):
            for yy in (0, 1):
                rc_copy(k, yy).wait_send()
            for t in range(SUB):
                if k == 0:
                    when(zm < 3)(ry_copy(k, t).wait_send)
                    when(zm == 3)(ship_copy(t, False).wait_send)
                else:
                    ry_copy(k, t).wait_send()
                each(z_sends(k, t), "wait_send")

    width = channels // PIECES

    def piece(n):
        return pl.ds(n * width, width)

    stores = [
        pltpu.make_async_copy(s["bo"].at[:, piece(n)], block_out.at[:, piece(n)], s["store"].at[n])
        for n in range(PIECES)
    ] + [
        pltpu.make_async_copy(s["outer"], outer_out, s["store"].at[PIECES]),
        pltpu.make_async_copy(s["inner"], inner_out, s["store"].at[PIECES + 1]),
        pltpu.make_async_copy(s["values"], value_out, s["store"].at[PIECES + 2]),
        pltpu.make_async_copy(s["wo"], weight_out, s["store"].at[PIECES + 3]),
    ]

    def b_copy(n):
        return remote(s["bs"].at[n], s["br"].at[n], s["b_s"].at[n], s["b_r"].at[n], i, 1 - x)

    def projected(g, n):
        return jnp.dot(
            s["mod"][...], s["w"][g, :, :, piece(n)].reshape(channels, width), preferred_element_type=F32
        )

    wg_terms(0)
    pump(16, 13, 11)
    wg_terms(1)
    pump(16, 14, 12)
    when(zm < 2)(functools.partial(wg_y, 0))
    when(zm == 3)(wg_ship)
    for n in range(PIECES):
        og_copy(n).wait_recv()
    wg_terms(2)
    pump(16, 15, 13)
    wg_y(1)
    wg_terms(3)
    pump(16, 16, 16)
    w_rest()
    when(zm >= 2)(functools.partial(wg_y, 2))
    for n in range(PIECES // 2):
        s["bs"][n] = projected(1 - x, n).astype(BF16)
        b_copy(n).start()
    turns = [0] * 4

    def reduce(*counts):
        for n in range(4):
            steps = REDUCE[n][turns[n] : counts[n]]
            turns[n] = max(turns[n], counts[n])

            def go(steps=steps):
                for at in steps:
                    wg_z(at // SUB, at % SUB)

            if steps:
                when(zm == n)(go)

    reduce(0, 0, 0, 2)

    def gradient(p, _):
        cols = pl.ds(pl.multiple_of(p * 2 * LANES, 2 * LANES), 2 * LANES)
        grad = None
        for g in range(2):
            w = s["w"][g, pl.ds(p * (2 * LANES // part), 2 * LANES // part)].reshape(2 * LANES, channels)
            t = lax.dot_general(s["og"][g], w, (((1,), (1,)), ((), ())), preferred_element_type=F32)
            grad = t if grad is None else grad + t
        gate = s["outer"][:, cols].astype(F32)
        filtered_grad = grad * gate
        s["outer"][:, cols] = (
            grad * jnp.concatenate([s["y"][2 * p], s["y"][2 * p + 1]], axis=1)
        ).astype(BF16)
        s["u"][2 * p] = filtered_grad[:, :LANES]
        s["u"][2 * p + 1] = filtered_grad[:, LANES:]
        return 0

    lax.fori_loop(0, blocks // 2, gradient, 0)
    stores[PIECES].start()
    reduce(0, 0, 0, 3)
    back = conv_in(s["u"], s["z"], s["tail"], *states, s["end"], True)
    back(0, blocks)
    near_start(1)
    when(zm < 2)(functools.partial(wg_y, 2))
    wg_y(3)
    reduce(2, 0, 0, 4)
    for n in range(PIECES // 2, PIECES):
        s["bs"][n] = projected(1 - x, n).astype(BF16)
        b_copy(n).start()
    when(zm == 2)(functools.partial(wg_y, 0))
    reduce(2, 0, 0, 4)
    near_finish(1)
    for n in range(PIECES):
        s["bo"][:, piece(n)] = projected(x, n).astype(BF16)
    reduce(4, 1, 4, 5)
    far_finish(1)
    reduce(4, 3, 5, 6)
    home = conv_out(s["z"], s["toep"], s["rise"], *states, s["inc"], s["u"], True)
    quarter = blocks // 4
    home(0, quarter)
    reduce(4, 4, 6, 6)
    home(quarter, 2 * quarter)
    reduce(5, 5, 7, 6)
    home(2 * quarter, 3 * quarter)
    reduce(6, 6, 8, 6)
    home(3 * quarter, blocks)
    reduce(7, 7, 8, 6)

    def grads(b, _):
        gg = s["u"][b]
        gate, value = s["inner"][:, lanes(b)].astype(F32), s["values"][:, lanes(b)].astype(F32)
        s["inner"][:, lanes(b)] = (gg * value).astype(BF16)
        s["values"][:, lanes(b)] = (gg * gate).astype(BF16)
        return 0

    lax.fori_loop(0, blocks, grads, 0)
    stores[PIECES + 1].start()
    stores[PIECES + 2].start()
    reduce(8, 8, 8, 6)
    for n in range(PIECES):
        b_copy(n).wait_recv()
        s["bo"][:, piece(n)] = (s["bo"][:, piece(n)].astype(F32) + s["br"][n].astype(F32)).astype(BF16)
        stores[n].start()
    wg_last()

    w_drain()
    wg_drain()
    for n in range(PIECES):
        og_copy(n).wait_send()
        b_copy(n).wait_send()
    for d in (0, 1):
        for t in (1, 2, 3):
            near_copy(d, t).wait_send()
        far_sends(d, "wait_send")
    for copy in stores:
        copy.wait()


def fused(outer_gate, inner_gate, values, out_weight, skip_gain, residues, decay_rates, out_grad):
    rows, channels = values.shape
    ctx = lax.axis_size("ctx")
    scratch = fused_scratch(rows, channels)
    scratch["acc"] = pltpu.VMEM((channels // 8 // SUB, channels), F32)
    shape = jax.ShapeDtypeStruct
    small = pl.BlockSpec(memory_space=pltpu.VMEM)
    large = pl.BlockSpec(memory_space=pl.ANY)
    tile = shape((rows, channels), BF16)
    outs = pl.pallas_call(
        functools.partial(fused_kernel, tuple(scratch), rows * ctx),
        out_shape=[tile] * 4 + [shape(out_weight.shape, F32)],
        in_specs=[small] * 3 + [large] * 5,
        out_specs=[large] * 5,
        scratch_shapes=list(scratch.values()),
        compiler_params=pltpu.CompilerParams(
            collective_id=3, has_side_effects=True, vmem_limit_bytes=VMEM_BYTES
        ),
        cost_estimate=pl.CostEstimate(flops=6 * 2**30, bytes_accessed=10 * 2**20, transcendentals=0),
        name="fused",
    )(decay_rates.T, residues.T, skip_gain[None], outer_gate, inner_gate, values, out_weight, out_grad)
    return hand_over(outs)


def hand_over_kernel(*refs):
    half = len(refs) // 2
    for src, dst in zip(refs[:half], refs[half:]):
        dst[...] = src[...]


def hand_over(arrays):
    steps = 4

    def spec(x):
        return pl.BlockSpec((x.shape[0] // steps, x.shape[1]), lambda n: (n, 0))

    specs = [spec(x) for x in arrays]
    return pl.pallas_call(
        hand_over_kernel,
        grid=(steps,),
        out_shape=[jax.ShapeDtypeStruct(x.shape, x.dtype) for x in arrays],
        in_specs=specs,
        out_specs=specs,
        name="hand_over",
    )(*arrays)


def solution(mesh):
    tile = P("ctx", "fsdp")
    small = dict(mesh.shape) == {"ctx": 16, "fsdp": 2}
    return jax.shard_map(
        fused if small else shards,
        mesh=mesh,
        in_specs=(tile, tile, tile, tile, P("fsdp"), P("fsdp", None), P("fsdp", None), tile),
        out_specs=(tile,) * 5,
        check_vma=False,
    )
```

```python
import functools
import math

import jax
import jax.numpy as jnp
from jax import lax
from jax.experimental import pallas as pl
from jax.experimental.pallas import tpu as pltpu
from jax.sharding import PartitionSpec as P

F32 = jnp.float32
BF16 = jnp.bfloat16
LANES = 128
SEGS = 8
VMEM_BYTES = 62 * 2**20


def rows_at(i, steps):
    return pl.ds(i, SEGS, stride=steps)


def spread(row):
    return jnp.broadcast_to(row, (SEGS, LANES))


def segment_states(u_scr, decay_ref, pre_ref, end_ref, reverse):
    modes = decay_ref.shape[0]
    steps = u_scr.shape[0] // SEGS
    a = [spread(jnp.exp(-decay_ref[r : r + 1, :])) for r in range(modes)]

    def step(k, states):
        i = steps - 1 - k if reverse else k
        u = u_scr[rows_at(i, steps), :]
        return tuple(a[r] * states[r] + u for r in range(modes))

    zero = jnp.zeros((SEGS, LANES), F32)
    states = lax.fori_loop(0, steps, step, (zero,) * modes, unroll=4)
    seg = lax.broadcasted_iota(jnp.int32, (SEGS, LANES), 0)

    def moved(x, by):
        if reverse:
            return jnp.where(seg < SEGS - by, pltpu.roll(x, SEGS - by, 0), 0.0)
        return jnp.where(seg >= by, pltpu.roll(x, by, 0), 0.0)

    last = 0 if reverse else SEGS - 1
    for r in range(modes):
        rate = spread(decay_ref[r : r + 1, :])
        x = states[r]
        for by in (1, 2, 4):
            x = x + jnp.exp(-rate * float(steps * by)) * moved(x, by)
        end_ref[r : r + 1, :] = x[last : last + 1, :]
        pre_ref[r] = moved(x, 1)


def full_scan(u_scr, y_scr, decay_ref, res_ref, pre_ref, incoming_ref, reverse):
    modes = decay_ref.shape[0]
    rows = u_scr.shape[0]
    steps = rows // SEGS
    seg = lax.broadcasted_iota(jnp.int32, (SEGS, LANES), 0)
    ahead = ((SEGS - 1 - seg if reverse else seg) * steps).astype(F32)
    a = []
    first = []
    for r in range(modes):
        rate = spread(decay_ref[r : r + 1, :])
        a.append(jnp.exp(-rate))
        first.append(pre_ref[r] + jnp.exp(-rate * ahead) * incoming_ref[r : r + 1, :])
    res = [spread(res_ref[r : r + 1, :]) for r in range(modes)]

    def step(k, states):
        i = steps - 1 - k if reverse else k
        u = u_scr[rows_at(i, steps), :]
        states = tuple(a[r] * states[r] + u for r in range(modes))
        terms = [res[r] * states[r] for r in range(modes)]
        while len(terms) > 1:
            terms = [p + q for p, q in zip(terms[::2], terms[1::2])]
        y_scr[rows_at(i, steps), :] = terms[0]
        return states

    lax.fori_loop(0, steps, step, tuple(first), unroll=2)


def forward_ends(inner_ref, values_ref, decay_ref, pre_ref, end_ref, u_scr):
    u_scr[...] = inner_ref[...].astype(F32) * values_ref[...].astype(F32)
    segment_states(u_scr, decay_ref, pre_ref, end_ref, False)


def forward_finish(
    inner_ref, values_ref, outer_ref, decay_ref, res_ref, skip_ref, pre_ref, incoming_ref,
    filtered_ref, modulated_ref, u_scr, y_scr,
):
    u_scr[...] = inner_ref[...].astype(F32) * values_ref[...].astype(F32)
    full_scan(u_scr, y_scr, decay_ref, res_ref, pre_ref, incoming_ref, False)
    filtered = y_scr[...] + skip_ref[...] * u_scr[...]
    filtered_ref[...] = filtered
    modulated_ref[...] = (outer_ref[...].astype(F32) * filtered).astype(BF16)


def backward_ends(own_ref, other_ref, outer_ref, decay_ref, pre_ref, end_ref, u_scr):
    grad = own_ref[...].astype(F32) + other_ref[...].astype(F32)
    u_scr[...] = grad * outer_ref[...].astype(F32)
    segment_states(u_scr, decay_ref, pre_ref, end_ref, True)


def backward_finish(
    own_ref, other_ref, outer_ref, inner_ref, values_ref, filtered_ref, decay_ref, res_ref, skip_ref,
    pre_ref, incoming_ref, outer_grad_ref, inner_grad_ref, value_grad_ref, u_scr, y_scr,
):
    grad = own_ref[...].astype(F32) + other_ref[...].astype(F32)
    u_scr[...] = grad * outer_ref[...].astype(F32)
    outer_grad_ref[...] = (grad * filtered_ref[...]).astype(BF16)
    full_scan(u_scr, y_scr, decay_ref, res_ref, pre_ref, incoming_ref, True)
    gated_grad = y_scr[...] + skip_ref[...] * u_scr[...]
    inner_grad_ref[...] = (gated_grad * values_ref[...].astype(F32)).astype(BF16)
    value_grad_ref[...] = (gated_grad * inner_ref[...].astype(F32)).astype(BF16)


def by_lanes(kernel, operands, outs, rows, scans):
    channels = operands[0].shape[-1]

    def spec(x):
        lead = x.shape[:-1]
        return pl.BlockSpec(lead + (LANES,), lambda c, n=len(lead): (0,) * n + (c,))

    work = rows * channels * (24000 if scans > 1 else 16000)
    moved = sum(math.prod(x.shape) * x.dtype.itemsize for x in list(operands) + list(outs))
    return pl.pallas_call(
        kernel,
        grid=(channels // LANES,),
        out_shape=outs,
        in_specs=[spec(x) for x in operands],
        out_specs=[spec(x) for x in outs],
        scratch_shapes=[pltpu.VMEM((rows, LANES), F32)] * scans,
        cost_estimate=pl.CostEstimate(flops=work, bytes_accessed=moved, transcendentals=0),
        name=kernel.__name__,
    )(*operands)


def prefix_kernel(reverse, rows, end_ref, decay_ref, out_ref, sent, got, send_sem, recv_sem):
    me, n = lax.axis_index("ctx"), lax.axis_size("ctx")
    hops = [1 << k for k in range(sent.shape[0])]
    barrier = pltpu.get_barrier_semaphore()
    for hop in hops:
        for peer in (lax.rem(me + hop, n), lax.rem(me + n - hop, n)):
            pl.semaphore_signal(
                barrier, inc=1, device_id={"ctx": peer}, device_id_type=pl.DeviceIdType.MESH
            )
    pl.semaphore_wait(barrier, 2 * len(hops))
    decay = decay_ref[...]
    upto = end_ref[...]
    before = jnp.zeros_like(upto)
    for k, hop in enumerate(hops):
        sent[k] = upto.astype(BF16)
        copy = pltpu.make_async_remote_copy(
            src_ref=sent.at[k],
            dst_ref=got.at[k],
            send_sem=send_sem.at[k],
            recv_sem=recv_sem.at[k],
            device_id={"ctx": lax.rem(me + (n - hop if reverse else hop), n)},
            device_id_type=pl.DeviceIdType.MESH,
        )
        copy.start()
        near = jnp.exp(-decay * float(rows * (hop - 1)))
        far = jnp.exp(-decay * float(rows * hop))
        copy.wait()
        inside = (me + hop < n) if reverse else (me >= hop)
        term = got[k].astype(F32) * jnp.where(inside, 1.0, 0.0)
        before = before + near * term
        upto = upto + far * term
    out_ref[...] = before


def prefix(end, decay, rows, reverse):
    hops = max(1, (lax.axis_size("ctx") - 1).bit_length())
    whole = pl.BlockSpec(memory_space=pltpu.VMEM)
    return pl.pallas_call(
        functools.partial(prefix_kernel, reverse, rows),
        out_shape=jax.ShapeDtypeStruct(end.shape, F32),
        in_specs=[whole, whole],
        out_specs=whole,
        scratch_shapes=[
            pltpu.VMEM((hops,) + end.shape, BF16),
            pltpu.VMEM((hops,) + end.shape, BF16),
            pltpu.SemaphoreType.DMA((hops,)),
            pltpu.SemaphoreType.DMA((hops,)),
        ],
        compiler_params=pltpu.CompilerParams(
            collective_id=2 if reverse else 1, has_side_effects=True
        ),
        cost_estimate=pl.CostEstimate(flops=18 * 10**9, bytes_accessed=0, transcendentals=0),
        name="prefix_back" if reverse else "prefix_ahead",
    )(end, decay)


def shards(outer_gate, inner_gate, values, out_weight, skip_gain, residues, decay_rates, out_grad):
    rows, channels = values.shape
    modes = decay_rates.shape[1]
    ctx, fsdp = lax.axis_size("ctx"), lax.axis_size("fsdp")
    at = lax.axis_index("fsdp")
    swap = [(0, 1), (1, 0)]
    shape = jax.ShapeDtypeStruct
    panel = lax.all_gather(out_weight, "ctx", axis=0, tiled=True)
    decay = decay_rates.T
    res = residues.T
    skip = skip_gain[None]
    state_outs = [shape((modes, SEGS, channels), F32), shape((modes, channels), F32)]
    pre, end = by_lanes(forward_ends, (inner_gate, values, decay), state_outs, rows, 1)
    incoming = prefix(end, decay, rows, False)
    filtered, modulated = by_lanes(
        forward_finish,
        (inner_gate, values, outer_gate, decay, res, skip, pre, incoming),
        [shape((rows, channels), F32), shape((rows, channels), BF16)],
        rows,
        2,
    )
    if fsdp == 2:
        other = lax.ppermute(modulated, "fsdp", swap)
        first = jnp.where(at == 0, modulated, other)
        second = jnp.where(at == 0, other, modulated)
        gathered = jnp.concatenate([first, second], axis=1)
        mine = lax.dynamic_slice_in_dim(panel, at * channels, channels, 0)
        theirs = lax.dynamic_slice_in_dim(panel, (1 - at) * channels, channels, 0)
        for_them = jnp.dot(out_grad, theirs.T, preferred_element_type=F32).astype(BF16)
        from_them = lax.ppermute(for_them, "fsdp", swap)
        own = jnp.dot(out_grad, mine.T, preferred_element_type=F32).astype(BF16)
    else:
        gathered = lax.all_gather(modulated, "fsdp", axis=1, tiled=True)
        partial = jnp.dot(out_grad, panel.T, preferred_element_type=F32).astype(BF16)
        own = lax.psum_scatter(partial, "fsdp", scatter_dimension=1, tiled=True)
        from_them = jnp.zeros_like(own)
    grad_rows = lax.dot_general(
        gathered, out_grad, (((0,), (0,)), ((), ())), preferred_element_type=F32
    ).astype(BF16)
    weight_grad = lax.psum_scatter(grad_rows, "ctx", scatter_dimension=0, tiled=True)
    block_out = jnp.dot(gathered, panel, preferred_element_type=F32).astype(BF16)
    pre, end = by_lanes(
        backward_ends, (own, from_them, outer_gate, decay), state_outs, rows, 1
    )
    incoming = prefix(end, decay, rows, True)
    outer_grad, inner_grad, value_grad = by_lanes(
        backward_finish,
        (own, from_them, outer_gate, inner_gate, values, filtered, decay, res, skip, pre, incoming),
        [shape((rows, channels), BF16)] * 3,
        rows,
        2,
    )
    weight_grad, value_grad = lax.optimization_barrier((weight_grad, value_grad))
    weight_grad = weight_grad.astype(F32) * (1.0 / math.sqrt(rows * ctx))
    return (block_out, outer_grad, inner_grad, value_grad, weight_grad)


TAPS = 16
GRAN = 16
PER = LANES // GRAN
WIDE = TAPS * GRAN
SUB = 2
PIECES = 4
GATHER = (
    (0, 1, 2, 3, 4, 5, 8, 9, 6, 7, 10, 11, 12, 13, 14, 15),
    (0, 1, 2, 3, 4, 5, 8, 9, 6, 7, 10, 11, 12, 13, 14, 15),
    (0, 1, 2, 8, 3, 9, 4, 5, 6, 7, 10, 11, 12, 13, 14, 15),
    (0, 1, 2, 3, 8, 4, 5, 9, 10, 6, 11, 7, 12, 13, 14, 15),
)
RSUB = 4
SHIP = 2
SHIPPED = 2
REDUCE = (
    (8, 9, 10, 11, 0, 1, 2, 3, 12, 13, 14, 15, 4, 5, 6, 7),
    (12, 13, 14, 15, 4, 8, 5, 9, 6, 10, 7, 11, 0, 1, 2, 3),
    (12, 13, 10, 11, 14, 15, 4, 5, 6, 7, 0, 1, 2, 3),
    (12, 13, 14, 15, 4, 5, 6, 7, 0, 1, 2, 3),
)
MESH = pl.DeviceIdType.MESH
ORDER = ((1, True), (0, True), (1, False), (0, False))


def regroup(v):
    lane = lax.broadcasted_iota(jnp.int32, v[0].shape, 1) // GRAN
    v = list(v)
    for m in (1, 2, 4):
        low = (lane & m) == 0
        for i in range(PER):
            if i & m:
                continue
            p, q = v[i], v[i + m]
            v[i] = jnp.where(low, p, pltpu.roll(q, GRAN * m, 1))
            v[i + m] = jnp.where(low, pltpu.roll(p, LANES - GRAN * m, 1), q)
    return v


def row_at(k, s, steps, reverse):
    return TAPS * (steps - 1 - k) + TAPS - 1 - s if reverse else TAPS * k + s


def regroup_filters(decay_ref, res_ref, skip_ref, par_ref, gen_ref):
    row = lax.broadcasted_iota(jnp.int32, (SEGS, LANES), 0)
    lag = lax.broadcasted_iota(jnp.int32, (TAPS, LANES), 0)
    lags = lag.astype(F32)

    def block(b, _):
        cols = pl.ds(pl.multiple_of(b * LANES, LANES), LANES)
        kern = jnp.where(lag == 0, jnp.broadcast_to(skip_ref[:, cols], (TAPS, LANES)), 0.0)
        for r in range(TAPS):
            kern = kern + res_ref[r : r + 1, cols] * jnp.exp(-decay_ref[r : r + 1, cols] * lags)
        gen_ref[...] = kern
        for half in range(2):
            v = []
            for s in range(half * PER, (half + 1) * PER):
                rate = jnp.broadcast_to(decay_ref[s : s + 1, cols], (SEGS, LANES))
                res = jnp.broadcast_to(res_ref[s : s + 1, cols], (SEGS, LANES))
                tap = jnp.broadcast_to(gen_ref[s : s + 1, :], (SEGS, LANES))
                v.append(jnp.where(row == 0, rate, jnp.where(row == 1, res, tap)))
            for h, out in enumerate(regroup(v)):
                par_ref[b * PER + h, :, half * LANES : (half + 1) * LANES] = out
        return 0

    lax.fori_loop(0, decay_ref.shape[1] // LANES, block, 0)


def build_tables(par_ref, rate_ref, taps_ref, outs, first, groups):
    shape = (GRAN, WIDE)
    diagonal = lax.broadcasted_iota(jnp.int32, shape, 1) % GRAN == lax.broadcasted_iota(jnp.int32, shape, 0)
    lag = lax.broadcasted_iota(jnp.int32, (TAPS, WIDE), 0)
    lags = lag.astype(F32)
    at = lax.broadcasted_iota(jnp.int32, (TAPS, WIDE), 1) // GRAN

    def group(n, _):
        for d in range(4):
            g = first + 4 * n + d
            rate = par_ref[g, 0:1, :]
            for i in outs:
                if i == 0:
                    rate_ref[pl.ds(g, 1), :] = rate
                    taps_ref[d, i] = jnp.exp(-rate * (TAPS - 1 - lags))
                elif i == 1:
                    taps_ref[d, i] = par_ref[g, 1:2, :] * jnp.exp(-rate * (lags + 1))
                else:
                    kern = jnp.broadcast_to(par_ref[g, 2:3, :], (TAPS, WIDE))
                    taps_ref[d, i] = jnp.where(at >= lag, pltpu.roll(kern, 0, 1, stride=GRAN, stride_axis=0), 0.0)
        for d in range(4):
            g = first + 4 * n + d
            for i, out in outs.items():
                for s in range(TAPS):
                    line = jnp.broadcast_to(taps_ref[d, i, s : s + 1, :], shape)
                    out[g, s * GRAN : (s + 1) * GRAN, :] = jnp.where(diagonal, line, 0.0).astype(BF16)
        return 0

    lax.fori_loop(0, groups // 4, group, 0)


def moved(x, by, reverse):
    seg = lax.broadcasted_iota(jnp.int32, x.shape, 0)
    if reverse:
        return jnp.where(seg < SEGS - by, pltpu.roll(x, SEGS - by, 0), 0.0)
    return jnp.where(seg >= by, pltpu.roll(x, by, 0), 0.0)


def conv_in(u_ref, z_ref, tail_ref, rate_ref, e_ref, pre_ref, end_ref, reverse):
    blocks, rows, _ = u_ref.shape
    stride = rows // SEGS
    steps = stride // TAPS
    last = 0 if reverse else SEGS - 1

    def split(b):
        for half in range(2):
            for k in range(0, steps, 2):
                pair = [
                    regroup(
                        [
                            u_ref[b, pl.ds(row_at(n, half * PER + j, steps, reverse), SEGS, stride=stride), :]
                            for j in range(PER)
                        ]
                    )
                    for n in (k, k + 1)
                ]
                for h in range(PER):
                    z_ref[b * PER + h, k * SEGS : (k + 2) * SEGS, half * LANES : (half + 1) * LANES] = (
                        jnp.concatenate([pair[0][h], pair[1][h]], axis=0).astype(BF16)
                    )

    def ends(b):
        for h in range(PER):
            g = b * PER + h
            e = jnp.dot(z_ref[g], tail_ref[g], preferred_element_type=F32)
            e_ref[g] = e
            rate = jnp.broadcast_to(rate_ref[pl.ds(g, 1), :], (SEGS, WIDE))
            a = jnp.exp(-rate * float(TAPS))
            x = e[0:SEGS]
            for k in range(1, steps):
                x = a * x + e[k * SEGS : (k + 1) * SEGS]
            for by in (1, 2, 4):
                x = x + jnp.exp(-rate * float(TAPS * steps * by)) * moved(x, by, reverse)
            end_ref[pl.ds(g, 1), :] = x[last : last + 1, :]
            pre_ref[g] = moved(x, 1, reverse)

    return pipelined(split, ends, blocks)


def pipelined(first, second, blocks):
    def body(b, _):
        second(b - 1)
        first(b)
        return 0

    def run(lo, hi):
        if lo == 0:
            first(0)
        lax.fori_loop(max(lo, 1), hi, body, 0)
        if hi == blocks:
            second(blocks - 1)

    return run


def conv_out(z_ref, toep_ref, rise_ref, rate_ref, e_ref, pre_ref, inc_ref, y_ref, reverse):
    groups, chunks, _ = z_ref.shape
    steps = chunks // SEGS
    stride = y_ref.shape[1] // SEGS

    def finish(b):
        seg = lax.broadcasted_iota(jnp.int32, (SEGS, WIDE), 0)
        ahead = ((SEGS - 1 - seg if reverse else seg) * (TAPS * steps)).astype(F32)
        for h in range(PER):
            g = b * PER + h
            rate = jnp.broadcast_to(rate_ref[pl.ds(g, 1), :], (SEGS, WIDE))
            a = jnp.exp(-rate * float(TAPS))
            x = pre_ref[g] + jnp.exp(-rate * ahead) * inc_ref[pl.ds(g, 1), :]
            states = [x]
            for k in range(steps - 1):
                x = a * x + e_ref[g, k * SEGS : (k + 1) * SEGS]
                states.append(x)
            s = jnp.concatenate(states, axis=0).astype(BF16)
            y = jnp.dot(z_ref[g], toep_ref[g], preferred_element_type=F32)
            e_ref[g] = y + lax.dot_general(s, rise_ref[g], (((1,), (1,)), ((), ())), preferred_element_type=F32)

    def merge(b):
        for half in range(2):
            for k in range(steps):
                v = regroup(
                    [
                        e_ref[b * PER + h, k * SEGS : (k + 1) * SEGS, half * LANES : (half + 1) * LANES]
                        for h in range(PER)
                    ]
                )
                for j in range(PER):
                    y_ref[b, pl.ds(row_at(k, half * PER + j, steps, reverse), SEGS, stride=stride), :] = v[j]

    return pipelined(finish, merge, groups // PER)


def fused_scratch(rows, channels):
    blocks, groups = channels // LANES, channels // GRAN
    chunks = rows // TAPS
    part = channels // 8
    dma = pltpu.SemaphoreType.DMA
    v = pltpu.VMEM
    return dict(
        tail=v((groups, WIDE, WIDE), BF16),
        rise=v((groups, WIDE, WIDE), BF16),
        toep=v((groups, WIDE, WIDE), BF16),
        par=v((groups, SEGS, WIDE), F32),
        rate=v((groups, WIDE), F32),
        taps=v((4, 3, TAPS, WIDE), F32),
        gen=v((TAPS, LANES), F32),
        inner=v((rows, channels), BF16),
        values=v((rows, channels), BF16),
        outer=v((rows, channels), BF16),
        og=v((2, rows, channels), BF16),
        w=v((2, 8, part, channels), BF16),
        u=v((blocks, rows, LANES), F32),
        y=v((blocks, rows, LANES), F32),
        z=v((groups, chunks, WIDE), BF16),
        e=v((groups, chunks, WIDE), F32),
        pre=v((groups, SEGS, WIDE), F32),
        end=v((groups, WIDE), F32),
        before=v((groups, WIDE), F32),
        inc=v((groups, WIDE), F32),
        near=v((2, 4, groups, WIDE), BF16),
        total=v((2, groups, WIDE), BF16),
        far=v((2, 4, groups, WIDE), BF16),
        mod=v((rows, channels), BF16),
        modt=v((channels, rows), BF16),
        bs=v((PIECES, rows, channels // PIECES), BF16),
        br=v((PIECES, rows, channels // PIECES), BF16),
        bo=v((rows, channels), BF16),
        part=v((2, 8, part, channels), BF16),
        rc=v((4, 2, part, channels), BF16),
        ys=v((4, part, channels), BF16),
        ry=v((4, part, channels), BF16),
        zs=v((4, part, channels), BF16),
        rz=v((4, part, channels), BF16),
        rb=v((2, part, channels), BF16),
        ro=v((part, channels), BF16),
        wx=v((part, channels), BF16),
        wo=v((part, channels), F32),
        load=dma((5,)),
        store=dma((PIECES + 4,)),
        og_s=dma((PIECES,)),
        og_r=dma((PIECES,)),
        wx_s=dma((SUB,)),
        w_r=dma((2, 8, SUB)),
        up_s=dma((4, SUB)),
        down_s=dma((4, SUB)),
        y_s=dma((4, SUB)),
        c_s=dma((4, SUB)),
        cy_s=dma((4, SUB)),
        near_s=dma((2, 4)),
        near_r=dma((2, 4)),
        far_s=dma((2, 4)),
        far_r=dma((2, 4)),
        b_s=dma((PIECES,)),
        b_r=dma((PIECES,)),
        rc_s=dma((4, 2)),
        rc_r=dma((4, 2)),
        ry_s=dma((4, RSUB)),
        ry_r=dma((4, RSUB)),
        rz_s=dma((4, RSUB)),
        rz_r=dma((4, RSUB)),
        rb_r=dma((2, RSUB)),
        ro_r=dma((RSUB,)),
        fx_r=dma((RSUB,)),
    )


def fused_kernel(names, length, *refs):
    decay, res, skip, outer_in, inner_in, values_in, weight_in, grad_in = refs[:8]
    block_out, outer_out, inner_out, value_out, weight_out = refs[8:13]
    s = dict(zip(names, refs[13:]))
    rows, channels = inner_in.shape
    part = weight_in.shape[0]
    blocks = channels // LANES
    groups = channels // GRAN
    fine = part // SUB
    i, x = lax.axis_index("ctx"), lax.axis_index("fsdp")
    z, y, c = i // 4, (i // 2) % 2, i % 2
    zm = jnp.where(x == 0, z, 3 - z)
    q = i % 4

    def ctx_at(z, y, c):
        return z * 4 + y * 2 + c

    up_to = ctx_at(z + 1 - 2 * x, y, c)
    down_to = ctx_at(z - 1 + 2 * x, y, c)
    y_to = ctx_at(z, 1 - y, c)
    c_to = ctx_at(z, y, 1 - c)

    def remote(src, dst, send, recv, ctx, fsdp=x):
        return pltpu.make_async_remote_copy(
            src_ref=src, dst_ref=dst, send_sem=send, recv_sem=recv,
            device_id={"ctx": ctx, "fsdp": fsdp}, device_id_type=MESH,
        )

    def when(cond):
        return pl.when(cond)

    loads = [
        pltpu.make_async_copy(inner_in, s["inner"], s["load"].at[0]),
        pltpu.make_async_copy(values_in, s["values"], s["load"].at[1]),
        pltpu.make_async_copy(outer_in, s["outer"], s["load"].at[2]),
        pltpu.make_async_copy(grad_in, s["og"].at[x], s["load"].at[3]),
    ]
    for copy in loads:
        copy.start()
    jown = (z % 2) * 4 + q
    source = zm < 2
    keep_w = pltpu.make_async_copy(weight_in, s["w"].at[x, jown], s["load"].at[4])
    when(source)(keep_w.start)
    s["far"][...] = jnp.zeros_like(s["far"])

    barrier = pltpu.get_barrier_semaphore()
    peers = [(ctx_at(z, (q + t) % 4 // 2, (q + t) % 2), x) for t in (1, 2, 3)]
    peers += [(ctx_at((z + t) % 4, y, c), x) for t in (1, 2, 3)] + [(i, 1 - x)]
    for ctx, fsdp in peers:
        pl.semaphore_signal(barrier, inc=1, device_id={"ctx": ctx, "fsdp": fsdp}, device_id_type=MESH)
    pl.semaphore_wait(barrier, len(peers))

    def fine_rows(t):
        return pl.ds(t * fine, fine)

    def sum_rows(t):
        return pl.ds(t * (part // RSUB), part // RSUB)

    def spot(sidx, yy, cc):
        return jnp.where(x == 0, sidx, 1 - sidx) * 4 + yy * 2 + cc

    def side(own):
        return x if own else 1 - x

    def w_cross(t):
        return remote(
            weight_in.at[fine_rows(t)], s["w"].at[x, jown, fine_rows(t)], s["wx_s"].at[t],
            s["w_r"].at[x, jown, t], i, 1 - x,
        )

    def w_sends(src, g, j, k, t, up, down):
        dst = s["w"].at[g, j, fine_rows(t)]
        recv = s["w_r"].at[g, j, t]
        return [
            (up, remote(src, dst, s["up_s"].at[k, t], recv, up_to)),
            (down, remote(src, dst, s["down_s"].at[k, t], recv, down_to)),
            (None, remote(src, dst, s["y_s"].at[k, t], recv, y_to)),
            (None, remote(src, dst, s["c_s"].at[k, t], recv, c_to)),
        ]

    def each(sends, act):
        for cond, copy in sends:
            if cond is None:
                getattr(copy, act)()
            elif cond is not False:
                when(cond)(getattr(copy, act))

    def place(p, n):
        if n == 0:
            return p // 2, side(p % 2 == 0)
        return 1 - p % 2, side(p < 2)

    def own_sends(t):
        return w_sends(weight_in.at[fine_rows(t)], x, jown, 0, t, None, zm == 1)

    def line_sends(p, t, n):
        sidx, g = place(p, n)
        j = spot(sidx, y, c)
        src = s["w"].at[g, j, fine_rows(t)]
        up = None if n < 3 and (sidx == 0 or n > 0) else False
        return w_sends(src, g, j, p, t, up, None if sidx == 1 and n == 1 else False)

    def w_wait(g, j, t):
        dst = s["w"].at[g, j, fine_rows(t)]
        remote(dst, dst, s["wx_s"].at[t], s["w_r"].at[g, j, t], c_to).wait_recv()

    def pump_line(p, t, n):
        if p == 0 and n < 2:
            return
        sidx, g = place(p, n)
        w_wait(g, spot(sidx, y, c), t)
        each(line_sends(p, t, n), "start")

    def y_pass(p, t, n):
        sidx, g = place(p, n)
        j = spot(sidx, 1 - y, c)
        at = s["w"].at[g, j, fine_rows(t)]
        return remote(at, at, s["cy_s"].at[p, t], s["w_r"].at[g, j, t], c_to)

    def pump_y(p, t, n):
        sidx, g = place(p, n)
        w_wait(g, spot(sidx, 1 - y, c), t)
        y_pass(p, t, n).start()

    def w_rest():
        for sidx, own in ORDER:
            for t in range(SUB):
                for yy in (0, 1):
                    w_wait(side(own), spot(sidx, yy, 1 - c), t)
        when(source)(keep_w.wait)

    def w_drain():
        def cross():
            for t in range(SUB):
                w_cross(t).wait_send()

        def owned():
            for t in range(SUB):
                each(own_sends(t), "wait_send")

        when(zm >= 2)(cross)
        when(source)(owned)
        for n in range(4):

            def passed(n=n):
                for p in range(4):
                    for t in range(SUB):
                        if p > 0 or n >= 2:
                            each(line_sends(p, t, n), "wait_send")
                        y_pass(p, t, n).wait_send()

            when(zm == n)(passed)

    def start_cross():
        for t in range(SUB):
            w_cross(t).start()

    def start_owned():
        for t in range(SUB):
            each(own_sends(t), "start")

    when(zm >= 2)(start_cross)
    when(source)(start_owned)

    slab = rows // PIECES

    def og_copy(n):
        return remote(
            grad_in.at[pl.ds(n * slab, slab)], s["og"].at[x, pl.ds(n * slab, slab)],
            s["og_s"].at[n], s["og_r"].at[n], i, 1 - x,
        )

    for n in range(PIECES):
        og_copy(n).start()

    def listed(order):
        parts = 4 * SUB
        return [(pump_line if n < parts else pump_y, n % parts // SUB, n % SUB) for n in order]

    classes = [zm == n for n in range(4)]
    orders = [listed(order) for order in GATHER]
    done = [0] * len(classes)

    def pump(*counts):
        for n, cond in enumerate(classes):
            steps = orders[n][done[n] : counts[n]]
            done[n] = max(done[n], counts[n])

            def go(steps=steps, n=n):
                for act, p, t in steps:
                    act(p, t, n)

            if steps:
                when(cond)(go)

    def rate():
        return s["rate"][...]

    def near_copy(d, t):
        to = (q + t) % 4
        at = s["near"].at[d, q]
        return remote(at, at, s["near_s"].at[d, t], s["near_r"].at[d, q], ctx_at(z, to // 2, to % 2))

    def near_wait(d, t):
        frm = (q + t) % 4
        at = s["near"].at[d, frm]
        remote(at, at, s["near_s"].at[d, t], s["near_r"].at[d, frm], c_to).wait_recv()

    def far_copy(d, t):
        to = z + t if d == 0 else z - t
        at = s["far"].at[d, z]
        return remote(s["total"].at[d], at, s["far_s"].at[d, t], s["far_r"].at[d, z], ctx_at(to, y, c))

    def far_sends(d, act):
        for t in (1, 2, 3):
            cond = z + t < 4 if d == 0 else z - t >= 0
            when(cond)(getattr(far_copy(d, t), act))

    def near_start(d):
        s["near"][d, q] = s["end"][...].astype(BF16)
        for t in (1, 2, 3):
            near_copy(d, t).start()

    def near_finish(d):
        for t in (1, 2, 3):
            near_wait(d, t)
        total = jnp.zeros((groups, WIDE), F32)
        before = jnp.zeros((groups, WIDE), F32)
        mine = q if d == 0 else 3 - q
        for k in range(4):
            rank = k if d == 0 else 3 - k
            term = s["near"][d, k].astype(F32)
            total = total + jnp.exp(-rate() * float(rows * (3 - rank))) * term
            gap = mine - rank
            weight = jnp.exp(-rate() * (rows * jnp.maximum(gap - 1, 0)).astype(F32))
            before = before + jnp.where(gap > 0, weight, 0.0) * term
        s["before"][...] = before
        s["total"][d] = total.astype(BF16)
        far_sends(d, "start")

    def far_finish(d):
        for t in (1, 2, 3):
            frm = z - t if d == 0 else z + t
            at = s["far"].at[d, frm]
            copy = remote(at, at, s["far_s"].at[d, t], s["far_r"].at[d, frm], c_to)
            when(z - t >= 0 if d == 0 else z + t < 4)(copy.wait_recv)
        into = jnp.zeros((groups, WIDE), F32)
        for k in range(4):
            gap = z - k if d == 0 else k - z
            weight = jnp.exp(-rate() * (4 * rows * jnp.maximum(gap - 1, 0)).astype(F32))
            into = into + jnp.where(gap > 0, weight, 0.0) * s["far"][d, k].astype(F32)
        mine = q if d == 0 else 3 - q
        s["inc"][...] = s["before"][...] + jnp.exp(-rate() * (rows * mine).astype(F32)) * into

    def lanes(b):
        return pl.ds(pl.multiple_of(b * LANES, LANES), LANES)

    build = functools.partial(build_tables, s["par"], s["rate"], s["taps"])
    later = {1: s["rise"], 2: s["toep"]}
    regroup_filters(decay, res, skip, s["par"], s["gen"])
    loads[0].wait()
    loads[1].wait()

    def gated(b, _):
        s["u"][b] = s["inner"][:, lanes(b)].astype(F32) * s["values"][:, lanes(b)].astype(F32)
        return 0

    lax.fori_loop(0, blocks, gated, 0)
    build({0: s["tail"]}, 0, groups)
    states = (s["rate"], s["e"], s["pre"])
    ahead = conv_in(s["u"], s["z"], s["tail"], *states, s["end"], False)
    ahead(0, blocks // 2)
    pump(4, 4, 1, 0)
    ahead(blocks // 2, blocks)
    near_start(0)
    pump(8, 8, 2, 0)
    build({1: s["rise"]}, 0, groups)
    build({2: s["toep"]}, 0, groups)
    pump(8, 8, 4, 1)
    near_finish(0)
    pump(10, 10, 7, 4)
    far_finish(0)
    pump(12, 12, 8, 5)
    onward = conv_out(s["z"], s["toep"], s["rise"], *states, s["inc"], s["y"], False)
    quarter = blocks // 4
    onward(0, quarter)
    pump(12, 12, 8, 6)
    onward(quarter, 2 * quarter)
    pump(14, 14, 9, 6)
    onward(2 * quarter, 3 * quarter)
    pump(14, 14, 9, 7)
    onward(3 * quarter, blocks)
    pump(15, 15, 10, 9)
    loads[2].wait()
    loads[3].wait()

    def modulate(b, _):
        m = (s["outer"][:, lanes(b)].astype(F32) * s["y"][b]).astype(BF16)
        s["mod"][:, lanes(b)] = m
        s["modt"][pl.ds(pl.multiple_of(b * LANES, LANES), LANES), :] = m.T
        return 0

    lax.fori_loop(0, blocks, modulate, 0)
    pump(15, 15, 10, 10)

    def wg_terms(k):
        sidx, own = ORDER[k]
        g, first = side(own), spot(sidx, 0, 0)
        height = 4 * part
        lhs = pl.ds(pl.multiple_of(first * part, height), height)

        def tile(n, _):
            cols = pl.ds(pl.multiple_of(n * 256, 256), 256)
            t = jnp.dot(s["modt"][lhs, :], s["og"][g, :, cols], preferred_element_type=F32)
            s["part"][g, pl.ds(first, 4), :, cols] = t.astype(BF16).reshape(4, part, 256)
            return 0

        lax.fori_loop(0, channels // 256, tile, 0)
        for yy in (0, 1):
            rc_copy(k, yy).start()

    def rc_copy(k, yy):
        sidx, own = ORDER[k]
        return remote(
            s["part"].at[side(own), spot(sidx, yy, 1 - c)], s["rc"].at[k, yy],
            s["rc_s"].at[k, yy], s["rc_r"].at[k, yy], c_to,
        )

    def ry_copy(k, t):
        return remote(
            s["ys"].at[k, sum_rows(t)], s["ry"].at[k, sum_rows(t)],
            s["ry_s"].at[k, t], s["ry_r"].at[k, t], y_to,
        )

    def ship_copy(t, own_row):
        r = sum_rows(t)
        if own_row:
            return rz_copy(SHIPPED, t)
        return remote(s["ys"].at[SHIPPED, r], s["ro"].at[r], s["ry_s"].at[SHIPPED, t], s["ro_r"].at[t], down_to)

    def wg_ship(first, last, n):
        if first == 0:
            rc_copy(SHIPPED, 0).wait_recv()
            rc_copy(SHIPPED, 1).wait_recv()
        for t in range(first, last):
            r = sum_rows(t)
            for own_row, out, landed in ((False, "ys", s["ro"]), (True, "zs", s["rz"].at[SHIPPED])):
                yy = y if own_row else 1 - y
                term = s["part"][side(ORDER[SHIPPED][1]), spot(1, yy, c), r].astype(F32) + s["rc"][SHIPPED, yy, r].astype(F32)
                if n == 2:
                    ship_copy(t, own_row).wait_recv()
                    term = term + landed[r].astype(F32)
                s[out][SHIPPED, r] = term.astype(BF16)
                ship_copy(t, own_row).start()

    def wg_y(k, first=0, last=RSUB):
        sidx, own = ORDER[k]
        if first == 0:
            rc_copy(k, 0).wait_recv()
            rc_copy(k, 1).wait_recv()
        for t in range(first, last):
            r = sum_rows(t)
            term = s["part"][side(own), spot(sidx, 1 - y, c), r].astype(F32) + s["rc"][k, 1 - y, r].astype(F32)
            s["ys"][k, r] = term.astype(BF16)
            if k == SHIPPED:

                def shipped(t=t, r=r):
                    ship_copy(t, False).wait_recv()
                    s["ys"][SHIPPED, r] = (s["ys"][SHIPPED, r].astype(F32) + s["ro"][r].astype(F32)).astype(BF16)

                when(zm == (1 if t < SHIP else 2))(shipped)
            ry_copy(k, t).start()

    def rz_copy(k, t, back=False):
        r = sum_rows(t)
        if back:
            return remote(s["zs"].at[k, r], s["rb"].at[k // 2, r], s["rz_s"].at[k, t], s["rb_r"].at[k // 2, t], up_to)
        return remote(s["zs"].at[k, r], s["rz"].at[k, r], s["rz_s"].at[k, t], s["rz_r"].at[k, t], down_to)

    def fx_copy(k, t):
        r = sum_rows(t)
        return remote(s["zs"].at[k, r], s["wx"].at[r], s["rz_s"].at[k, t], s["fx_r"].at[t], i, 1 - x)

    scale = 1.0 / math.sqrt(length)

    def z_sends(k, t):
        sidx, own = ORDER[k]
        sends = [(zm > sidx, rz_copy(k, t))]
        if sidx == 1:
            sends.append((zm == 0, rz_copy(k, t, True)))
        if not own:
            sends.append((zm == sidx, fx_copy(k, t)))
        return sends

    def wg_z(k, t, n):
        sidx, own = ORDER[k]
        r = sum_rows(t)
        ry_copy(k, t).wait_recv()
        acc = (
            s["part"][side(own), spot(sidx, y, c), r].astype(F32)
            + s["rc"][k, y, r].astype(F32)
            + s["ry"][k, r].astype(F32)
        )
        if (sidx == 0 and n < 3) or (sidx == 1 and n in (1, 2)):
            rz_copy(k, t).wait_recv()
            acc = acc + s["rz"][k, r].astype(F32)
        if sidx == 1 and n == 1:
            rz_copy(k, t, True).wait_recv()
            acc = acc + s["rb"][k // 2, r].astype(F32)
        if own and n == sidx:
            s["wo"][r] = acc * scale
            return
        s["zs"][k, r] = acc.astype(BF16)
        if n > sidx:
            rz_copy(k, t).start()
        elif n < sidx:
            rz_copy(k, t, True).start()
        else:
            fx_copy(k, t).start()

    def wg_last():
        def take():
            for t in range(RSUB):
                fx_copy(2, t).wait_recv()
                s["wo"][sum_rows(t)] = s["wx"][sum_rows(t)].astype(F32) * scale

        when(zm >= 2)(take)
        stores[-1].start()

    def wg_drain():
        for k in range(4):
            for yy in (0, 1):
                rc_copy(k, yy).wait_send()
            for t in range(RSUB):
                if k == SHIPPED:
                    ships = 2 if t < SHIP else 3
                    when(zm < ships)(ry_copy(k, t).wait_send)
                    when(zm >= ships)(ship_copy(t, False).wait_send)
                else:
                    ry_copy(k, t).wait_send()
                each(z_sends(k, t), "wait_send")

    width = channels // PIECES

    def piece(n):
        return pl.ds(n * width, width)

    stores = [
        pltpu.make_async_copy(s["bo"].at[:, piece(n)], block_out.at[:, piece(n)], s["store"].at[n])
        for n in range(PIECES)
    ] + [
        pltpu.make_async_copy(s["outer"], outer_out, s["store"].at[PIECES]),
        pltpu.make_async_copy(s["inner"], inner_out, s["store"].at[PIECES + 1]),
        pltpu.make_async_copy(s["values"], value_out, s["store"].at[PIECES + 2]),
        pltpu.make_async_copy(s["wo"], weight_out, s["store"].at[PIECES + 3]),
    ]

    def b_copy(n):
        return remote(s["bs"].at[n], s["br"].at[n], s["b_s"].at[n], s["b_r"].at[n], i, 1 - x)

    def projected(g, n):
        return jnp.dot(
            s["mod"][...], s["w"][g, :, :, piece(n)].reshape(channels, width), preferred_element_type=F32
        )

    wg_terms(1)
    pump(16, 16, 13, 11)
    for n in range(PIECES):
        og_copy(n).wait_recv()
    wg_terms(SHIPPED)
    pump(16, 16, 14, 12)
    when(zm == 0)(functools.partial(wg_y, SHIPPED))
    when(zm == 3)(functools.partial(wg_ship, 0, RSUB, 3))
    wg_terms(3)
    pump(16, 16, 15, 13)
    wg_y(3)
    wg_terms(0)
    pump(16, 16, 16, 16)
    w_rest()
    when(zm == 2)(functools.partial(wg_ship, 0, 1, 2))
    when(zm == 3)(functools.partial(wg_y, 1))
    turns = [0] * 4

    sums = [[(at // RSUB, at % RSUB) for at in order] for order in REDUCE]

    def reduce(*counts):
        for n in range(4):
            steps = sums[n][turns[n] : counts[n]]
            turns[n] = max(turns[n], counts[n])

            def go(steps=steps, n=n):
                for k, t in steps:
                    wg_z(k, t, n)

            if steps:
                when(zm == n)(go)

    def gradient(p, _):
        cols = pl.ds(pl.multiple_of(p * 2 * LANES, 2 * LANES), 2 * LANES)
        grad = None
        for g in range(2):
            w = s["w"][g, pl.ds(p * (2 * LANES // part), 2 * LANES // part)].reshape(2 * LANES, channels)
            t = lax.dot_general(s["og"][g], w, (((1,), (1,)), ((), ())), preferred_element_type=F32)
            grad = t if grad is None else grad + t
        gate = s["outer"][:, cols].astype(F32)
        filtered_grad = grad * gate
        s["outer"][:, cols] = (
            grad * jnp.concatenate([s["y"][2 * p], s["y"][2 * p + 1]], axis=1)
        ).astype(BF16)
        s["u"][2 * p] = filtered_grad[:, :LANES]
        s["u"][2 * p + 1] = filtered_grad[:, LANES:]
        return 0

    lax.fori_loop(0, blocks // 2, gradient, 0)
    stores[PIECES].start()
    when(zm == 2)(functools.partial(wg_ship, 1, 2, 2))
    for n in range(PIECES // 2):
        s["bs"][n] = projected(1 - x, n).astype(BF16)
        b_copy(n).start()
    reduce(0, 0, 0, 4)
    when(zm == 2)(functools.partial(wg_y, SHIPPED, SHIP, 3))
    back = conv_in(s["u"], s["z"], s["tail"], *states, s["end"], True)
    back(0, blocks)
    near_start(1)
    when(zm == 2)(functools.partial(wg_y, SHIPPED, 3, RSUB))
    when(zm < 3)(functools.partial(wg_y, 1))
    wg_y(0)
    reduce(4, 0, 0, 6)
    for n in range(PIECES // 2, PIECES):
        s["bs"][n] = projected(1 - x, n).astype(BF16)
        b_copy(n).start()
    reduce(4, 0, 1, 6)
    near_finish(1)
    reduce(4, 0, 3, 8)
    for n in range(PIECES):
        s["bo"][:, piece(n)] = projected(x, n).astype(BF16)
    reduce(4, 0, 6, 9)
    far_finish(1)
    when(zm == 1)(functools.partial(wg_y, SHIPPED))
    reduce(8, 4, 7, 10)
    home = conv_out(s["z"], s["toep"], s["rise"], *states, s["inc"], s["u"], True)
    home(0, quarter)
    reduce(8, 6, 8, 12)
    home(quarter, 2 * quarter)
    reduce(9, 8, 9, 12)
    home(2 * quarter, 3 * quarter)
    reduce(10, 10, 11, 12)
    home(3 * quarter, blocks)
    reduce(11, 12, 13, 12)

    def grads(b, _):
        gg = s["u"][b]
        gate, value = s["inner"][:, lanes(b)].astype(F32), s["values"][:, lanes(b)].astype(F32)
        s["inner"][:, lanes(b)] = (gg * value).astype(BF16)
        s["values"][:, lanes(b)] = (gg * gate).astype(BF16)
        return 0

    lax.fori_loop(0, blocks, grads, 0)
    stores[PIECES + 1].start()
    stores[PIECES + 2].start()
    reduce(12, 12, 14, 12)
    for n in range(PIECES):
        b_copy(n).wait_recv()
        s["bo"][:, piece(n)] = (s["bo"][:, piece(n)].astype(F32) + s["br"][n].astype(F32)).astype(BF16)
        stores[n].start()
    reduce(16, 16, 14, 12)
    wg_last()

    w_drain()
    wg_drain()
    for n in range(PIECES):
        og_copy(n).wait_send()
        b_copy(n).wait_send()
    for d in (0, 1):
        for t in (1, 2, 3):
            near_copy(d, t).wait_send()
        far_sends(d, "wait_send")
    for copy in stores:
        copy.wait()


def fused(outer_gate, inner_gate, values, out_weight, skip_gain, residues, decay_rates, out_grad):
    rows, channels = values.shape
    ctx = lax.axis_size("ctx")
    scratch = fused_scratch(rows, channels)
    shape = jax.ShapeDtypeStruct
    small = pl.BlockSpec(memory_space=pltpu.VMEM)
    large = pl.BlockSpec(memory_space=pl.ANY)
    tile = shape((rows, channels), BF16)
    outs = pl.pallas_call(
        functools.partial(fused_kernel, tuple(scratch), rows * ctx),
        out_shape=[tile] * 4 + [shape(out_weight.shape, F32)],
        in_specs=[small] * 3 + [large] * 5,
        out_specs=[large] * 5,
        scratch_shapes=list(scratch.values()),
        compiler_params=pltpu.CompilerParams(
            collective_id=3, has_side_effects=True, vmem_limit_bytes=VMEM_BYTES
        ),
        cost_estimate=pl.CostEstimate(flops=6 * 2**30, bytes_accessed=10 * 2**20, transcendentals=0),
        name="fused",
    )(decay_rates.T, residues.T, skip_gain[None], outer_gate, inner_gate, values, out_weight, out_grad)
    return hand_over(outs)


def hand_over_kernel(count, *refs):
    ins, outs, held = refs[:count], refs[count : 2 * count], refs[2 * count : 3 * count]
    sems = refs[-1]
    loads = [pltpu.make_async_copy(a, b, sems.at[0, n]) for n, (a, b) in enumerate(zip(ins, held))]
    stores = [pltpu.make_async_copy(a, b, sems.at[1, n]) for n, (a, b) in enumerate(zip(held, outs))]
    for copy in loads:
        copy.start()
    for load, store in zip(loads, stores):
        load.wait()
        store.start()
    for copy in stores:
        copy.wait()


def hand_over(arrays):
    count = len(arrays)
    large = pl.BlockSpec(memory_space=pl.ANY)
    return pl.pallas_call(
        functools.partial(hand_over_kernel, count),
        out_shape=[jax.ShapeDtypeStruct(x.shape, x.dtype) for x in arrays],
        in_specs=[large] * count,
        out_specs=[large] * count,
        scratch_shapes=[pltpu.VMEM(x.shape, x.dtype) for x in arrays] + [pltpu.SemaphoreType.DMA((2, count))],
        compiler_params=pltpu.CompilerParams(vmem_limit_bytes=VMEM_BYTES),
        name="hand_over",
    )(*arrays)


def solution(mesh):
    tile = P("ctx", "fsdp")
    small = dict(mesh.shape) == {"ctx": 16, "fsdp": 2}
    return jax.shard_map(
        fused if small else shards,
        mesh=mesh,
        in_specs=(tile, tile, tile, tile, P("fsdp"), P("fsdp", None), P("fsdp", None), tile),
        out_specs=(tile,) * 5,
        check_vma=False,
    )
```

```python
import functools
import math

import jax
import jax.numpy as jnp
from jax import lax
from jax.experimental import pallas as pl
from jax.experimental.pallas import tpu as pltpu
from jax.sharding import PartitionSpec as P

F32 = jnp.float32
BF16 = jnp.bfloat16
LANES = 128
SEGS = 8
VMEM_BYTES = 62 * 2**20


def rows_at(i, steps):
    return pl.ds(i, SEGS, stride=steps)


def spread(row):
    return jnp.broadcast_to(row, (SEGS, LANES))


def segment_states(u_scr, decay_ref, pre_ref, end_ref, reverse):
    modes = decay_ref.shape[0]
    steps = u_scr.shape[0] // SEGS
    a = [spread(jnp.exp(-decay_ref[r : r + 1, :])) for r in range(modes)]

    def step(k, states):
        i = steps - 1 - k if reverse else k
        u = u_scr[rows_at(i, steps), :]
        return tuple(a[r] * states[r] + u for r in range(modes))

    zero = jnp.zeros((SEGS, LANES), F32)
    states = lax.fori_loop(0, steps, step, (zero,) * modes, unroll=4)
    seg = lax.broadcasted_iota(jnp.int32, (SEGS, LANES), 0)

    def moved(x, by):
        if reverse:
            return jnp.where(seg < SEGS - by, pltpu.roll(x, SEGS - by, 0), 0.0)
        return jnp.where(seg >= by, pltpu.roll(x, by, 0), 0.0)

    last = 0 if reverse else SEGS - 1
    for r in range(modes):
        rate = spread(decay_ref[r : r + 1, :])
        x = states[r]
        for by in (1, 2, 4):
            x = x + jnp.exp(-rate * float(steps * by)) * moved(x, by)
        end_ref[r : r + 1, :] = x[last : last + 1, :]
        pre_ref[r] = moved(x, 1)


def full_scan(u_scr, y_scr, decay_ref, res_ref, pre_ref, incoming_ref, reverse):
    modes = decay_ref.shape[0]
    rows = u_scr.shape[0]
    steps = rows // SEGS
    seg = lax.broadcasted_iota(jnp.int32, (SEGS, LANES), 0)
    ahead = ((SEGS - 1 - seg if reverse else seg) * steps).astype(F32)
    a = []
    first = []
    for r in range(modes):
        rate = spread(decay_ref[r : r + 1, :])
        a.append(jnp.exp(-rate))
        first.append(pre_ref[r] + jnp.exp(-rate * ahead) * incoming_ref[r : r + 1, :])
    res = [spread(res_ref[r : r + 1, :]) for r in range(modes)]

    def step(k, states):
        i = steps - 1 - k if reverse else k
        u = u_scr[rows_at(i, steps), :]
        states = tuple(a[r] * states[r] + u for r in range(modes))
        terms = [res[r] * states[r] for r in range(modes)]
        while len(terms) > 1:
            terms = [p + q for p, q in zip(terms[::2], terms[1::2])]
        y_scr[rows_at(i, steps), :] = terms[0]
        return states

    lax.fori_loop(0, steps, step, tuple(first), unroll=2)


def forward_ends(inner_ref, values_ref, decay_ref, pre_ref, end_ref, u_scr):
    u_scr[...] = inner_ref[...].astype(F32) * values_ref[...].astype(F32)
    segment_states(u_scr, decay_ref, pre_ref, end_ref, False)


def forward_finish(
    inner_ref, values_ref, outer_ref, decay_ref, res_ref, skip_ref, pre_ref, incoming_ref,
    filtered_ref, modulated_ref, u_scr, y_scr,
):
    u_scr[...] = inner_ref[...].astype(F32) * values_ref[...].astype(F32)
    full_scan(u_scr, y_scr, decay_ref, res_ref, pre_ref, incoming_ref, False)
    filtered = y_scr[...] + skip_ref[...] * u_scr[...]
    filtered_ref[...] = filtered
    modulated_ref[...] = (outer_ref[...].astype(F32) * filtered).astype(BF16)


def backward_ends(own_ref, other_ref, outer_ref, decay_ref, pre_ref, end_ref, u_scr):
    grad = own_ref[...].astype(F32) + other_ref[...].astype(F32)
    u_scr[...] = grad * outer_ref[...].astype(F32)
    segment_states(u_scr, decay_ref, pre_ref, end_ref, True)


def backward_finish(
    own_ref, other_ref, outer_ref, inner_ref, values_ref, filtered_ref, decay_ref, res_ref, skip_ref,
    pre_ref, incoming_ref, outer_grad_ref, inner_grad_ref, value_grad_ref, u_scr, y_scr,
):
    grad = own_ref[...].astype(F32) + other_ref[...].astype(F32)
    u_scr[...] = grad * outer_ref[...].astype(F32)
    outer_grad_ref[...] = (grad * filtered_ref[...]).astype(BF16)
    full_scan(u_scr, y_scr, decay_ref, res_ref, pre_ref, incoming_ref, True)
    gated_grad = y_scr[...] + skip_ref[...] * u_scr[...]
    inner_grad_ref[...] = (gated_grad * values_ref[...].astype(F32)).astype(BF16)
    value_grad_ref[...] = (gated_grad * inner_ref[...].astype(F32)).astype(BF16)


def by_lanes(kernel, operands, outs, rows, scans):
    channels = operands[0].shape[-1]

    def spec(x):
        lead = x.shape[:-1]
        return pl.BlockSpec(lead + (LANES,), lambda c, n=len(lead): (0,) * n + (c,))

    work = rows * channels * (24000 if scans > 1 else 16000)
    moved = sum(math.prod(x.shape) * x.dtype.itemsize for x in list(operands) + list(outs))
    return pl.pallas_call(
        kernel,
        grid=(channels // LANES,),
        out_shape=outs,
        in_specs=[spec(x) for x in operands],
        out_specs=[spec(x) for x in outs],
        scratch_shapes=[pltpu.VMEM((rows, LANES), F32)] * scans,
        cost_estimate=pl.CostEstimate(flops=work, bytes_accessed=moved, transcendentals=0),
        name=kernel.__name__,
    )(*operands)


def prefix_kernel(reverse, rows, end_ref, decay_ref, out_ref, sent, got, send_sem, recv_sem):
    me, n = lax.axis_index("ctx"), lax.axis_size("ctx")
    hops = [1 << k for k in range(sent.shape[0])]
    barrier = pltpu.get_barrier_semaphore()
    for hop in hops:
        for peer in (lax.rem(me + hop, n), lax.rem(me + n - hop, n)):
            pl.semaphore_signal(
                barrier, inc=1, device_id={"ctx": peer}, device_id_type=pl.DeviceIdType.MESH
            )
    pl.semaphore_wait(barrier, 2 * len(hops))
    decay = decay_ref[...]
    upto = end_ref[...]
    before = jnp.zeros_like(upto)
    for k, hop in enumerate(hops):
        sent[k] = upto.astype(BF16)
        copy = pltpu.make_async_remote_copy(
            src_ref=sent.at[k],
            dst_ref=got.at[k],
            send_sem=send_sem.at[k],
            recv_sem=recv_sem.at[k],
            device_id={"ctx": lax.rem(me + (n - hop if reverse else hop), n)},
            device_id_type=pl.DeviceIdType.MESH,
        )
        copy.start()
        near = jnp.exp(-decay * float(rows * (hop - 1)))
        far = jnp.exp(-decay * float(rows * hop))
        copy.wait()
        inside = (me + hop < n) if reverse else (me >= hop)
        term = got[k].astype(F32) * jnp.where(inside, 1.0, 0.0)
        before = before + near * term
        upto = upto + far * term
    out_ref[...] = before


def prefix(end, decay, rows, reverse):
    hops = max(1, (lax.axis_size("ctx") - 1).bit_length())
    whole = pl.BlockSpec(memory_space=pltpu.VMEM)
    return pl.pallas_call(
        functools.partial(prefix_kernel, reverse, rows),
        out_shape=jax.ShapeDtypeStruct(end.shape, F32),
        in_specs=[whole, whole],
        out_specs=whole,
        scratch_shapes=[
            pltpu.VMEM((hops,) + end.shape, BF16),
            pltpu.VMEM((hops,) + end.shape, BF16),
            pltpu.SemaphoreType.DMA((hops,)),
            pltpu.SemaphoreType.DMA((hops,)),
        ],
        compiler_params=pltpu.CompilerParams(
            collective_id=2 if reverse else 1, has_side_effects=True
        ),
        cost_estimate=pl.CostEstimate(flops=18 * 10**9, bytes_accessed=0, transcendentals=0),
        name="prefix_back" if reverse else "prefix_ahead",
    )(end, decay)


def shards(outer_gate, inner_gate, values, out_weight, skip_gain, residues, decay_rates, out_grad):
    rows, channels = values.shape
    modes = decay_rates.shape[1]
    ctx, fsdp = lax.axis_size("ctx"), lax.axis_size("fsdp")
    at = lax.axis_index("fsdp")
    swap = [(0, 1), (1, 0)]
    shape = jax.ShapeDtypeStruct
    panel = lax.all_gather(out_weight, "ctx", axis=0, tiled=True)
    decay = decay_rates.T
    res = residues.T
    skip = skip_gain[None]
    state_outs = [shape((modes, SEGS, channels), F32), shape((modes, channels), F32)]
    pre, end = by_lanes(forward_ends, (inner_gate, values, decay), state_outs, rows, 1)
    incoming = prefix(end, decay, rows, False)
    filtered, modulated = by_lanes(
        forward_finish,
        (inner_gate, values, outer_gate, decay, res, skip, pre, incoming),
        [shape((rows, channels), F32), shape((rows, channels), BF16)],
        rows,
        2,
    )
    if fsdp == 2:
        other = lax.ppermute(modulated, "fsdp", swap)
        first = jnp.where(at == 0, modulated, other)
        second = jnp.where(at == 0, other, modulated)
        gathered = jnp.concatenate([first, second], axis=1)
        mine = lax.dynamic_slice_in_dim(panel, at * channels, channels, 0)
        theirs = lax.dynamic_slice_in_dim(panel, (1 - at) * channels, channels, 0)
        for_them = jnp.dot(out_grad, theirs.T, preferred_element_type=F32).astype(BF16)
        from_them = lax.ppermute(for_them, "fsdp", swap)
        own = jnp.dot(out_grad, mine.T, preferred_element_type=F32).astype(BF16)
    else:
        gathered = lax.all_gather(modulated, "fsdp", axis=1, tiled=True)
        partial = jnp.dot(out_grad, panel.T, preferred_element_type=F32).astype(BF16)
        own = lax.psum_scatter(partial, "fsdp", scatter_dimension=1, tiled=True)
        from_them = jnp.zeros_like(own)
    grad_rows = lax.dot_general(
        gathered, out_grad, (((0,), (0,)), ((), ())), preferred_element_type=F32
    ).astype(BF16)
    weight_grad = lax.psum_scatter(grad_rows, "ctx", scatter_dimension=0, tiled=True)
    block_out = jnp.dot(gathered, panel, preferred_element_type=F32).astype(BF16)
    pre, end = by_lanes(
        backward_ends, (own, from_them, outer_gate, decay), state_outs, rows, 1
    )
    incoming = prefix(end, decay, rows, True)
    outer_grad, inner_grad, value_grad = by_lanes(
        backward_finish,
        (own, from_them, outer_gate, inner_gate, values, filtered, decay, res, skip, pre, incoming),
        [shape((rows, channels), BF16)] * 3,
        rows,
        2,
    )
    weight_grad, value_grad = lax.optimization_barrier((weight_grad, value_grad))
    weight_grad = weight_grad.astype(F32) * (1.0 / math.sqrt(rows * ctx))
    return (block_out, outer_grad, inner_grad, value_grad, weight_grad)


TAPS = 16
GRAN = 16
PER = LANES // GRAN
WIDE = TAPS * GRAN
SUB = 2
PIECES = 4
GATHER = (
    (0, 1, 2, 3, 4, 5, 8, 9, 6, 7, 10, 11, 12, 13, 14, 15),
    (0, 1, 2, 3, 4, 5, 8, 9, 6, 7, 10, 11, 12, 13, 14, 15),
    (0, 1, 2, 8, 3, 9, 4, 5, 6, 7, 10, 11, 12, 13, 14, 15),
    (0, 1, 2, 3, 8, 4, 5, 9, 10, 6, 11, 7, 12, 13, 14, 15),
)
RSUB = 4
SHIP = 4
SHIPPED = 2
REDUCE = (
    (8, 9, 10, 11, 0, 1, 2, 3, 12, 13, 14, 15, 4, 5, 6, 7),
    (12, 13, 14, 15, 4, 8, 5, 9, 6, 10, 7, 11, 0, 1, 2, 3),
    (12, 13, 14, 15, 4, 5, 6, 7, 0, 1, 2, 3),
    (12, 13, 14, 15, 4, 5, 6, 7, 0, 1, 2, 3),
)
MESH = pl.DeviceIdType.MESH
ORDER = ((1, True), (0, True), (1, False), (0, False))


def regroup(v):
    lane = lax.broadcasted_iota(jnp.int32, v[0].shape, 1) // GRAN
    v = list(v)
    for m in (1, 2, 4):
        low = (lane & m) == 0
        for i in range(PER):
            if i & m:
                continue
            p, q = v[i], v[i + m]
            v[i] = jnp.where(low, p, pltpu.roll(q, GRAN * m, 1))
            v[i + m] = jnp.where(low, pltpu.roll(p, LANES - GRAN * m, 1), q)
    return v


def row_at(k, s, steps, reverse):
    return TAPS * (steps - 1 - k) + TAPS - 1 - s if reverse else TAPS * k + s


def regroup_filters(decay_ref, res_ref, skip_ref, par_ref, gen_ref):
    row = lax.broadcasted_iota(jnp.int32, (SEGS, LANES), 0)
    lag = lax.broadcasted_iota(jnp.int32, (TAPS, LANES), 0)
    lags = lag.astype(F32)

    def block(b, _):
        cols = pl.ds(pl.multiple_of(b * LANES, LANES), LANES)
        kern = jnp.where(lag == 0, jnp.broadcast_to(skip_ref[:, cols], (TAPS, LANES)), 0.0)
        for r in range(TAPS):
            kern = kern + res_ref[r : r + 1, cols] * jnp.exp(-decay_ref[r : r + 1, cols] * lags)
        gen_ref[...] = kern
        for half in range(2):
            v = []
            for s in range(half * PER, (half + 1) * PER):
                rate = jnp.broadcast_to(decay_ref[s : s + 1, cols], (SEGS, LANES))
                res = jnp.broadcast_to(res_ref[s : s + 1, cols], (SEGS, LANES))
                tap = jnp.broadcast_to(gen_ref[s : s + 1, :], (SEGS, LANES))
                v.append(jnp.where(row == 0, rate, jnp.where(row == 1, res, tap)))
            for h, out in enumerate(regroup(v)):
                par_ref[b * PER + h, :, half * LANES : (half + 1) * LANES] = out
        return 0

    lax.fori_loop(0, decay_ref.shape[1] // LANES, block, 0)


def build_tables(par_ref, rate_ref, taps_ref, outs, first, groups):
    shape = (GRAN, WIDE)
    diagonal = lax.broadcasted_iota(jnp.int32, shape, 1) % GRAN == lax.broadcasted_iota(jnp.int32, shape, 0)
    lag = lax.broadcasted_iota(jnp.int32, (TAPS, WIDE), 0)
    lags = lag.astype(F32)
    at = lax.broadcasted_iota(jnp.int32, (TAPS, WIDE), 1) // GRAN

    def group(n, _):
        for d in range(4):
            g = first + 4 * n + d
            rate = par_ref[g, 0:1, :]
            for i in outs:
                if i == 0:
                    rate_ref[pl.ds(g, 1), :] = rate
                    taps_ref[d, i] = jnp.exp(-rate * (TAPS - 1 - lags))
                elif i == 1:
                    taps_ref[d, i] = par_ref[g, 1:2, :] * jnp.exp(-rate * (lags + 1))
                else:
                    kern = jnp.broadcast_to(par_ref[g, 2:3, :], (TAPS, WIDE))
                    taps_ref[d, i] = jnp.where(at >= lag, pltpu.roll(kern, 0, 1, stride=GRAN, stride_axis=0), 0.0)
        for d in range(4):
            g = first + 4 * n + d
            for i, out in outs.items():
                for s in range(TAPS):
                    line = jnp.broadcast_to(taps_ref[d, i, s : s + 1, :], shape)
                    out[g, s * GRAN : (s + 1) * GRAN, :] = jnp.where(diagonal, line, 0.0).astype(BF16)
        return 0

    lax.fori_loop(0, groups // 4, group, 0)


def moved(x, by, reverse):
    seg = lax.broadcasted_iota(jnp.int32, x.shape, 0)
    if reverse:
        return jnp.where(seg < SEGS - by, pltpu.roll(x, SEGS - by, 0), 0.0)
    return jnp.where(seg >= by, pltpu.roll(x, by, 0), 0.0)


def conv_in(u_ref, z_ref, tail_ref, rate_ref, e_ref, pre_ref, end_ref, reverse):
    blocks, rows, _ = u_ref.shape
    stride = rows // SEGS
    steps = stride // TAPS
    last = 0 if reverse else SEGS - 1

    def split(b):
        for half in range(2):
            for k in range(0, steps, 2):
                pair = [
                    regroup(
                        [
                            u_ref[b, pl.ds(row_at(n, half * PER + j, steps, reverse), SEGS, stride=stride), :]
                            for j in range(PER)
                        ]
                    )
                    for n in (k, k + 1)
                ]
                for h in range(PER):
                    z_ref[b * PER + h, k * SEGS : (k + 2) * SEGS, half * LANES : (half + 1) * LANES] = (
                        jnp.concatenate([pair[0][h], pair[1][h]], axis=0).astype(BF16)
                    )

    def ends(b):
        for h in range(PER):
            g = b * PER + h
            e = jnp.dot(z_ref[g], tail_ref[g], preferred_element_type=F32)
            e_ref[g] = e
            rate = jnp.broadcast_to(rate_ref[pl.ds(g, 1), :], (SEGS, WIDE))
            a = jnp.exp(-rate * float(TAPS))
            x = e[0:SEGS]
            for k in range(1, steps):
                x = a * x + e[k * SEGS : (k + 1) * SEGS]
            for by in (1, 2, 4):
                x = x + jnp.exp(-rate * float(TAPS * steps * by)) * moved(x, by, reverse)
            end_ref[pl.ds(g, 1), :] = x[last : last + 1, :]
            pre_ref[g] = moved(x, 1, reverse)

    return pipelined(split, ends, blocks)


def pipelined(first, second, blocks):
    def body(b, _):
        second(b - 1)
        first(b)
        return 0

    def run(lo, hi):
        if lo == 0:
            first(0)
        lax.fori_loop(max(lo, 1), hi, body, 0)
        if hi == blocks:
            second(blocks - 1)

    return run


def conv_out(z_ref, toep_ref, rise_ref, rate_ref, e_ref, pre_ref, inc_ref, y_ref, reverse):
    groups, chunks, _ = z_ref.shape
    steps = chunks // SEGS
    stride = y_ref.shape[1] // SEGS

    def finish(b):
        seg = lax.broadcasted_iota(jnp.int32, (SEGS, WIDE), 0)
        ahead = ((SEGS - 1 - seg if reverse else seg) * (TAPS * steps)).astype(F32)
        for h in range(PER):
            g = b * PER + h
            rate = jnp.broadcast_to(rate_ref[pl.ds(g, 1), :], (SEGS, WIDE))
            a = jnp.exp(-rate * float(TAPS))
            x = pre_ref[g] + jnp.exp(-rate * ahead) * inc_ref[pl.ds(g, 1), :]
            states = [x]
            for k in range(steps - 1):
                x = a * x + e_ref[g, k * SEGS : (k + 1) * SEGS]
                states.append(x)
            s = jnp.concatenate(states, axis=0).astype(BF16)
            y = jnp.dot(z_ref[g], toep_ref[g], preferred_element_type=F32)
            e_ref[g] = y + lax.dot_general(s, rise_ref[g], (((1,), (1,)), ((), ())), preferred_element_type=F32)

    def merge(b):
        for half in range(2):
            for k in range(steps):
                v = regroup(
                    [
                        e_ref[b * PER + h, k * SEGS : (k + 1) * SEGS, half * LANES : (half + 1) * LANES]
                        for h in range(PER)
                    ]
                )
                for j in range(PER):
                    y_ref[b, pl.ds(row_at(k, half * PER + j, steps, reverse), SEGS, stride=stride), :] = v[j]

    return pipelined(finish, merge, groups // PER)


def fused_scratch(rows, channels):
    blocks, groups = channels // LANES, channels // GRAN
    chunks = rows // TAPS
    part = channels // 8
    dma = pltpu.SemaphoreType.DMA
    v = pltpu.VMEM
    return dict(
        tail=v((groups, WIDE, WIDE), BF16),
        rise=v((groups, WIDE, WIDE), BF16),
        toep=v((groups, WIDE, WIDE), BF16),
        par=v((groups, SEGS, WIDE), F32),
        rate=v((groups, WIDE), F32),
        taps=v((4, 3, TAPS, WIDE), F32),
        gen=v((TAPS, LANES), F32),
        inner=v((rows, channels), BF16),
        values=v((rows, channels), BF16),
        outer=v((rows, channels), BF16),
        og=v((2, rows, channels), BF16),
        w=v((2, 8, part, channels), BF16),
        u=v((blocks, rows, LANES), F32),
        y=v((blocks, rows, LANES), F32),
        z=v((groups, chunks, WIDE), BF16),
        e=v((groups, chunks, WIDE), F32),
        pre=v((groups, SEGS, WIDE), F32),
        end=v((groups, WIDE), F32),
        before=v((groups, WIDE), F32),
        inc=v((groups, WIDE), F32),
        near=v((2, 4, groups, WIDE), BF16),
        total=v((2, groups, WIDE), BF16),
        far=v((2, 4, groups, WIDE), BF16),
        mod=v((rows, channels), BF16),
        modt=v((channels, rows), BF16),
        bs=v((PIECES, rows, channels // PIECES), BF16),
        br=v((PIECES, rows, channels // PIECES), BF16),
        bo=v((rows, channels), BF16),
        part=v((2, 8, part, channels), BF16),
        rc=v((4, 2, part, channels), BF16),
        ys=v((4, part, channels), BF16),
        ry=v((4, part, channels), BF16),
        zs=v((4, part, channels), BF16),
        rz=v((4, part, channels), BF16),
        rb=v((2, part, channels), BF16),
        ro=v((part, channels), BF16),
        wx=v((part, channels), BF16),
        wo=v((part, channels), F32),
        load=dma((5,)),
        store=dma((PIECES + 4,)),
        og_s=dma((PIECES,)),
        og_r=dma((PIECES,)),
        wx_s=dma((SUB,)),
        w_r=dma((2, 8, SUB)),
        up_s=dma((4, SUB)),
        down_s=dma((4, SUB)),
        y_s=dma((4, SUB)),
        c_s=dma((4, SUB)),
        cy_s=dma((4, SUB)),
        near_s=dma((2, 4)),
        near_r=dma((2, 4)),
        far_s=dma((2, 4)),
        far_r=dma((2, 4)),
        b_s=dma((PIECES,)),
        b_r=dma((PIECES,)),
        rc_s=dma((4, 2)),
        rc_r=dma((4, 2)),
        ry_s=dma((4, RSUB)),
        ry_r=dma((4, RSUB)),
        rz_s=dma((4, RSUB)),
        rz_r=dma((4, RSUB)),
        rb_r=dma((2, RSUB)),
        ro_r=dma((RSUB,)),
        fx_r=dma((RSUB,)),
    )


def fused_kernel(names, length, *refs):
    decay, res, skip, outer_in, inner_in, values_in, weight_in, grad_in = refs[:8]
    block_out, outer_out, inner_out, value_out, weight_out = refs[8:13]
    s = dict(zip(names, refs[13:]))
    rows, channels = inner_in.shape
    part = weight_in.shape[0]
    blocks = channels // LANES
    groups = channels // GRAN
    fine = part // SUB
    i, x = lax.axis_index("ctx"), lax.axis_index("fsdp")
    z, y, c = i // 4, (i // 2) % 2, i % 2
    zm = jnp.where(x == 0, z, 3 - z)
    q = i % 4

    def ctx_at(z, y, c):
        return z * 4 + y * 2 + c

    up_to = ctx_at(z + 1 - 2 * x, y, c)
    down_to = ctx_at(z - 1 + 2 * x, y, c)
    y_to = ctx_at(z, 1 - y, c)
    c_to = ctx_at(z, y, 1 - c)

    def remote(src, dst, send, recv, ctx, fsdp=x):
        return pltpu.make_async_remote_copy(
            src_ref=src, dst_ref=dst, send_sem=send, recv_sem=recv,
            device_id={"ctx": ctx, "fsdp": fsdp}, device_id_type=MESH,
        )

    def when(cond):
        return pl.when(cond)

    loads = [
        pltpu.make_async_copy(inner_in, s["inner"], s["load"].at[0]),
        pltpu.make_async_copy(values_in, s["values"], s["load"].at[1]),
        pltpu.make_async_copy(outer_in, s["outer"], s["load"].at[2]),
        pltpu.make_async_copy(grad_in, s["og"].at[x], s["load"].at[3]),
    ]
    for copy in loads:
        copy.start()
    jown = (z % 2) * 4 + q
    source = zm < 2
    keep_w = pltpu.make_async_copy(weight_in, s["w"].at[x, jown], s["load"].at[4])
    when(source)(keep_w.start)
    s["far"][...] = jnp.zeros_like(s["far"])

    barrier = pltpu.get_barrier_semaphore()
    peers = [(ctx_at(z, (q + t) % 4 // 2, (q + t) % 2), x) for t in (1, 2, 3)]
    peers += [(ctx_at((z + t) % 4, y, c), x) for t in (1, 2, 3)] + [(i, 1 - x)]
    for ctx, fsdp in peers:
        pl.semaphore_signal(barrier, inc=1, device_id={"ctx": ctx, "fsdp": fsdp}, device_id_type=MESH)
    pl.semaphore_wait(barrier, len(peers))

    def fine_rows(t):
        return pl.ds(t * fine, fine)

    def sum_rows(t):
        return pl.ds(t * (part // RSUB), part // RSUB)

    def spot(sidx, yy, cc):
        return jnp.where(x == 0, sidx, 1 - sidx) * 4 + yy * 2 + cc

    def side(own):
        return x if own else 1 - x

    def w_cross(t):
        return remote(
            weight_in.at[fine_rows(t)], s["w"].at[x, jown, fine_rows(t)], s["wx_s"].at[t],
            s["w_r"].at[x, jown, t], i, 1 - x,
        )

    def w_sends(src, g, j, k, t, up, down):
        dst = s["w"].at[g, j, fine_rows(t)]
        recv = s["w_r"].at[g, j, t]
        return [
            (up, remote(src, dst, s["up_s"].at[k, t], recv, up_to)),
            (down, remote(src, dst, s["down_s"].at[k, t], recv, down_to)),
            (None, remote(src, dst, s["y_s"].at[k, t], recv, y_to)),
            (None, remote(src, dst, s["c_s"].at[k, t], recv, c_to)),
        ]

    def each(sends, act):
        for cond, copy in sends:
            if cond is None:
                getattr(copy, act)()
            elif cond is not False:
                when(cond)(getattr(copy, act))

    def place(p, n):
        if n == 0:
            return p // 2, side(p % 2 == 0)
        return 1 - p % 2, side(p < 2)

    def own_sends(t):
        return w_sends(weight_in.at[fine_rows(t)], x, jown, 0, t, None, zm == 1)

    def line_sends(p, t, n):
        sidx, g = place(p, n)
        j = spot(sidx, y, c)
        src = s["w"].at[g, j, fine_rows(t)]
        up = None if n < 3 and (sidx == 0 or n > 0) else False
        return w_sends(src, g, j, p, t, up, None if sidx == 1 and n == 1 else False)

    def w_wait(g, j, t):
        dst = s["w"].at[g, j, fine_rows(t)]
        remote(dst, dst, s["wx_s"].at[t], s["w_r"].at[g, j, t], c_to).wait_recv()

    def pump_line(p, t, n):
        if p == 0 and n < 2:
            return
        sidx, g = place(p, n)
        w_wait(g, spot(sidx, y, c), t)
        each(line_sends(p, t, n), "start")

    def y_pass(p, t, n):
        sidx, g = place(p, n)
        j = spot(sidx, 1 - y, c)
        at = s["w"].at[g, j, fine_rows(t)]
        return remote(at, at, s["cy_s"].at[p, t], s["w_r"].at[g, j, t], c_to)

    def pump_y(p, t, n):
        sidx, g = place(p, n)
        w_wait(g, spot(sidx, 1 - y, c), t)
        y_pass(p, t, n).start()

    def w_rest():
        for sidx, own in ORDER:
            for t in range(SUB):
                for yy in (0, 1):
                    w_wait(side(own), spot(sidx, yy, 1 - c), t)
        when(source)(keep_w.wait)

    def w_drain():
        def cross():
            for t in range(SUB):
                w_cross(t).wait_send()

        def owned():
            for t in range(SUB):
                each(own_sends(t), "wait_send")

        when(zm >= 2)(cross)
        when(source)(owned)
        for n in range(4):

            def passed(n=n):
                for p in range(4):
                    for t in range(SUB):
                        if p > 0 or n >= 2:
                            each(line_sends(p, t, n), "wait_send")
                        y_pass(p, t, n).wait_send()

            when(zm == n)(passed)

    def start_cross():
        for t in range(SUB):
            w_cross(t).start()

    def start_owned():
        for t in range(SUB):
            each(own_sends(t), "start")

    when(zm >= 2)(start_cross)
    when(source)(start_owned)

    slab = rows // PIECES

    def og_copy(n):
        return remote(
            grad_in.at[pl.ds(n * slab, slab)], s["og"].at[x, pl.ds(n * slab, slab)],
            s["og_s"].at[n], s["og_r"].at[n], i, 1 - x,
        )

    for n in range(PIECES):
        og_copy(n).start()

    def listed(order):
        parts = 4 * SUB
        return [(pump_line if n < parts else pump_y, n % parts // SUB, n % SUB) for n in order]

    classes = [zm == n for n in range(4)]
    orders = [listed(order) for order in GATHER]
    done = [0] * len(classes)

    def pump(*counts):
        for n, cond in enumerate(classes):
            steps = orders[n][done[n] : counts[n]]
            done[n] = max(done[n], counts[n])

            def go(steps=steps, n=n):
                for act, p, t in steps:
                    act(p, t, n)

            if steps:
                when(cond)(go)

    def rate():
        return s["rate"][...]

    def near_copy(d, t):
        to = (q + t) % 4
        at = s["near"].at[d, q]
        return remote(at, at, s["near_s"].at[d, t], s["near_r"].at[d, q], ctx_at(z, to // 2, to % 2))

    def near_wait(d, t):
        frm = (q + t) % 4
        at = s["near"].at[d, frm]
        remote(at, at, s["near_s"].at[d, t], s["near_r"].at[d, frm], c_to).wait_recv()

    def far_copy(d, t):
        to = z + t if d == 0 else z - t
        at = s["far"].at[d, z]
        return remote(s["total"].at[d], at, s["far_s"].at[d, t], s["far_r"].at[d, z], ctx_at(to, y, c))

    def far_sends(d, act):
        for t in (1, 2, 3):
            cond = z + t < 4 if d == 0 else z - t >= 0
            when(cond)(getattr(far_copy(d, t), act))

    def near_start(d):
        s["near"][d, q] = s["end"][...].astype(BF16)
        for t in (1, 2, 3):
            near_copy(d, t).start()

    def near_finish(d):
        for t in (1, 2, 3):
            near_wait(d, t)
        total = jnp.zeros((groups, WIDE), F32)
        before = jnp.zeros((groups, WIDE), F32)
        mine = q if d == 0 else 3 - q
        for k in range(4):
            rank = k if d == 0 else 3 - k
            term = s["near"][d, k].astype(F32)
            total = total + jnp.exp(-rate() * float(rows * (3 - rank))) * term
            gap = mine - rank
            weight = jnp.exp(-rate() * (rows * jnp.maximum(gap - 1, 0)).astype(F32))
            before = before + jnp.where(gap > 0, weight, 0.0) * term
        s["before"][...] = before
        s["total"][d] = total.astype(BF16)
        far_sends(d, "start")

    def far_finish(d):
        for t in (1, 2, 3):
            frm = z - t if d == 0 else z + t
            at = s["far"].at[d, frm]
            copy = remote(at, at, s["far_s"].at[d, t], s["far_r"].at[d, frm], c_to)
            when(z - t >= 0 if d == 0 else z + t < 4)(copy.wait_recv)
        into = jnp.zeros((groups, WIDE), F32)
        for k in range(4):
            gap = z - k if d == 0 else k - z
            weight = jnp.exp(-rate() * (4 * rows * jnp.maximum(gap - 1, 0)).astype(F32))
            into = into + jnp.where(gap > 0, weight, 0.0) * s["far"][d, k].astype(F32)
        mine = q if d == 0 else 3 - q
        s["inc"][...] = s["before"][...] + jnp.exp(-rate() * (rows * mine).astype(F32)) * into

    def lanes(b):
        return pl.ds(pl.multiple_of(b * LANES, LANES), LANES)

    build = functools.partial(build_tables, s["par"], s["rate"], s["taps"])
    later = {1: s["rise"], 2: s["toep"]}
    regroup_filters(decay, res, skip, s["par"], s["gen"])
    loads[0].wait()
    loads[1].wait()

    def gated(b, _):
        s["u"][b] = s["inner"][:, lanes(b)].astype(F32) * s["values"][:, lanes(b)].astype(F32)
        return 0

    lax.fori_loop(0, blocks, gated, 0)
    build({0: s["tail"]}, 0, groups)
    states = (s["rate"], s["e"], s["pre"])
    ahead = conv_in(s["u"], s["z"], s["tail"], *states, s["end"], False)
    ahead(0, blocks // 2)
    pump(4, 4, 1, 0)
    ahead(blocks // 2, blocks)
    near_start(0)
    pump(8, 8, 2, 0)
    build({1: s["rise"]}, 0, groups)
    build({2: s["toep"]}, 0, groups)
    pump(8, 8, 4, 1)
    near_finish(0)
    pump(10, 10, 7, 4)
    far_finish(0)
    pump(12, 12, 8, 5)
    onward = conv_out(s["z"], s["toep"], s["rise"], *states, s["inc"], s["y"], False)
    quarter = blocks // 4
    onward(0, quarter)
    pump(12, 12, 8, 6)
    onward(quarter, 2 * quarter)
    pump(14, 14, 9, 6)
    onward(2 * quarter, 3 * quarter)
    pump(14, 14, 9, 7)
    onward(3 * quarter, blocks)
    pump(15, 15, 10, 9)
    loads[2].wait()
    loads[3].wait()

    def modulate(b, _):
        m = (s["outer"][:, lanes(b)].astype(F32) * s["y"][b]).astype(BF16)
        s["mod"][:, lanes(b)] = m
        s["modt"][pl.ds(pl.multiple_of(b * LANES, LANES), LANES), :] = m.T
        return 0

    lax.fori_loop(0, blocks, modulate, 0)
    pump(15, 15, 10, 10)

    def wg_terms(k):
        sidx, own = ORDER[k]
        g, first = side(own), spot(sidx, 0, 0)
        height = 4 * part
        lhs = pl.ds(pl.multiple_of(first * part, height), height)

        def tile(n, _):
            cols = pl.ds(pl.multiple_of(n * 256, 256), 256)
            t = jnp.dot(s["modt"][lhs, :], s["og"][g, :, cols], preferred_element_type=F32)
            s["part"][g, pl.ds(first, 4), :, cols] = t.astype(BF16).reshape(4, part, 256)
            return 0

        lax.fori_loop(0, channels // 256, tile, 0)
        for yy in (0, 1):
            rc_copy(k, yy).start()

    def rc_copy(k, yy):
        sidx, own = ORDER[k]
        return remote(
            s["part"].at[side(own), spot(sidx, yy, 1 - c)], s["rc"].at[k, yy],
            s["rc_s"].at[k, yy], s["rc_r"].at[k, yy], c_to,
        )

    def ry_copy(k, t):
        return remote(
            s["ys"].at[k, sum_rows(t)], s["ry"].at[k, sum_rows(t)],
            s["ry_s"].at[k, t], s["ry_r"].at[k, t], y_to,
        )

    def ship_copy(t, own_row):
        r = sum_rows(t)
        if own_row:
            return rz_copy(SHIPPED, t)
        return remote(s["ys"].at[SHIPPED, r], s["ro"].at[r], s["ry_s"].at[SHIPPED, t], s["ro_r"].at[t], down_to)

    def wg_ship(first, last, n):
        if first == 0:
            rc_copy(SHIPPED, 0).wait_recv()
            rc_copy(SHIPPED, 1).wait_recv()
        for t in range(first, last):
            r = sum_rows(t)
            for own_row, out, landed in ((False, "ys", s["ro"]), (True, "zs", s["rz"].at[SHIPPED])):
                yy = y if own_row else 1 - y
                term = s["part"][side(ORDER[SHIPPED][1]), spot(1, yy, c), r].astype(F32) + s["rc"][SHIPPED, yy, r].astype(F32)
                if n == 2:
                    ship_copy(t, own_row).wait_recv()
                    term = term + landed[r].astype(F32)
                s[out][SHIPPED, r] = term.astype(BF16)
                ship_copy(t, own_row).start()

    def wg_y(k, first=0, last=RSUB):
        sidx, own = ORDER[k]
        if first == 0:
            rc_copy(k, 0).wait_recv()
            rc_copy(k, 1).wait_recv()
        for t in range(first, last):
            r = sum_rows(t)
            term = s["part"][side(own), spot(sidx, 1 - y, c), r].astype(F32) + s["rc"][k, 1 - y, r].astype(F32)
            s["ys"][k, r] = term.astype(BF16)
            if k == SHIPPED:

                def shipped(t=t, r=r):
                    ship_copy(t, False).wait_recv()
                    s["ys"][SHIPPED, r] = (s["ys"][SHIPPED, r].astype(F32) + s["ro"][r].astype(F32)).astype(BF16)

                when(zm == (1 if t < SHIP else 2))(shipped)
            ry_copy(k, t).start()

    def rz_copy(k, t, back=False):
        r = sum_rows(t)
        if back:
            return remote(s["zs"].at[k, r], s["rb"].at[k // 2, r], s["rz_s"].at[k, t], s["rb_r"].at[k // 2, t], up_to)
        return remote(s["zs"].at[k, r], s["rz"].at[k, r], s["rz_s"].at[k, t], s["rz_r"].at[k, t], down_to)

    def fx_copy(k, t):
        r = sum_rows(t)
        return remote(s["zs"].at[k, r], s["wx"].at[r], s["rz_s"].at[k, t], s["fx_r"].at[t], i, 1 - x)

    scale = 1.0 / math.sqrt(length)

    def z_sends(k, t):
        sidx, own = ORDER[k]
        sends = [(zm > sidx, rz_copy(k, t))]
        if sidx == 1:
            sends.append((zm == 0, rz_copy(k, t, True)))
        if not own:
            sends.append((zm == sidx, fx_copy(k, t)))
        return sends

    def wg_z(k, t, n):
        sidx, own = ORDER[k]
        r = sum_rows(t)
        ry_copy(k, t).wait_recv()
        acc = (
            s["part"][side(own), spot(sidx, y, c), r].astype(F32)
            + s["rc"][k, y, r].astype(F32)
            + s["ry"][k, r].astype(F32)
        )
        if (sidx == 0 and n < 3) or (sidx == 1 and n in (1, 2)):
            rz_copy(k, t).wait_recv()
            acc = acc + s["rz"][k, r].astype(F32)
        if sidx == 1 and n == 1:
            rz_copy(k, t, True).wait_recv()
            acc = acc + s["rb"][k // 2, r].astype(F32)
        if own and n == sidx:
            s["wo"][r] = acc * scale
            return
        s["zs"][k, r] = acc.astype(BF16)
        if n > sidx:
            rz_copy(k, t).start()
        elif n < sidx:
            rz_copy(k, t, True).start()
        else:
            fx_copy(k, t).start()

    def wg_last():
        def take():
            for t in range(RSUB):
                fx_copy(2, t).wait_recv()
                s["wo"][sum_rows(t)] = s["wx"][sum_rows(t)].astype(F32) * scale

        when(zm >= 2)(take)
        stores[-1].start()

    def wg_drain():
        for k in range(4):
            for yy in (0, 1):
                rc_copy(k, yy).wait_send()
            for t in range(RSUB):
                if k == SHIPPED:
                    ships = 2 if t < SHIP else 3
                    when(zm < ships)(ry_copy(k, t).wait_send)
                    when(zm >= ships)(ship_copy(t, False).wait_send)
                else:
                    ry_copy(k, t).wait_send()
                each(z_sends(k, t), "wait_send")

    width = channels // PIECES

    def piece(n):
        return pl.ds(n * width, width)

    stores = [
        pltpu.make_async_copy(s["bo"].at[:, piece(n)], block_out.at[:, piece(n)], s["store"].at[n])
        for n in range(PIECES)
    ] + [
        pltpu.make_async_copy(s["outer"], outer_out, s["store"].at[PIECES]),
        pltpu.make_async_copy(s["inner"], inner_out, s["store"].at[PIECES + 1]),
        pltpu.make_async_copy(s["values"], value_out, s["store"].at[PIECES + 2]),
        pltpu.make_async_copy(s["wo"], weight_out, s["store"].at[PIECES + 3]),
    ]

    def b_copy(n):
        return remote(s["bs"].at[n], s["br"].at[n], s["b_s"].at[n], s["b_r"].at[n], i, 1 - x)

    def projected(g, n):
        return jnp.dot(
            s["mod"][...], s["w"][g, :, :, piece(n)].reshape(channels, width), preferred_element_type=F32
        )

    for n in range(PIECES):
        og_copy(n).wait_recv()
    wg_terms(SHIPPED)
    pump(16, 16, 13, 11)
    wg_terms(1)
    pump(16, 16, 14, 12)
    when(zm == 0)(functools.partial(wg_y, SHIPPED))
    when(zm == 3)(functools.partial(wg_ship, 0, RSUB, 3))
    wg_terms(3)
    pump(16, 16, 15, 13)
    wg_y(3)
    wg_terms(0)
    pump(16, 16, 16, 16)
    w_rest()
    when(zm == 2)(functools.partial(wg_ship, 0, 1, 2))
    when(zm == 3)(functools.partial(wg_y, 1))
    turns = [0] * 4

    sums = [[(at // RSUB, at % RSUB) for at in order] for order in REDUCE]

    def reduce(*counts):
        for n in range(4):
            steps = sums[n][turns[n] : counts[n]]
            turns[n] = max(turns[n], counts[n])

            def go(steps=steps, n=n):
                for k, t in steps:
                    wg_z(k, t, n)

            if steps:
                when(zm == n)(go)

    def gradient(p, _):
        cols = pl.ds(pl.multiple_of(p * 2 * LANES, 2 * LANES), 2 * LANES)
        grad = None
        for g in range(2):
            w = s["w"][g, pl.ds(p * (2 * LANES // part), 2 * LANES // part)].reshape(2 * LANES, channels)
            t = lax.dot_general(s["og"][g], w, (((1,), (1,)), ((), ())), preferred_element_type=F32)
            grad = t if grad is None else grad + t
        gate = s["outer"][:, cols].astype(F32)
        filtered_grad = grad * gate
        s["outer"][:, cols] = (
            grad * jnp.concatenate([s["y"][2 * p], s["y"][2 * p + 1]], axis=1)
        ).astype(BF16)
        s["u"][2 * p] = filtered_grad[:, :LANES]
        s["u"][2 * p + 1] = filtered_grad[:, LANES:]
        return 0

    lax.fori_loop(0, blocks // 2, gradient, 0)
    stores[PIECES].start()
    when(zm == 2)(functools.partial(wg_ship, 1, 2, 2))
    for n in range(PIECES // 2):
        s["bs"][n] = projected(1 - x, n).astype(BF16)
        b_copy(n).start()
    reduce(0, 0, 0, 4)
    when(zm == 2)(functools.partial(wg_ship, 2, 3, 2))
    back = conv_in(s["u"], s["z"], s["tail"], *states, s["end"], True)
    back(0, blocks)
    near_start(1)
    when(zm == 2)(functools.partial(wg_ship, 3, RSUB, 2))
    when(zm < 3)(functools.partial(wg_y, 1))
    wg_y(0)
    reduce(4, 0, 0, 6)
    for n in range(PIECES // 2, PIECES):
        s["bs"][n] = projected(1 - x, n).astype(BF16)
        b_copy(n).start()
    reduce(4, 0, 1, 6)
    near_finish(1)
    reduce(4, 0, 2, 8)
    for n in range(PIECES):
        s["bo"][:, piece(n)] = projected(x, n).astype(BF16)
    reduce(4, 0, 4, 9)
    far_finish(1)
    when(zm == 1)(functools.partial(wg_y, SHIPPED))
    reduce(8, 4, 5, 10)
    home = conv_out(s["z"], s["toep"], s["rise"], *states, s["inc"], s["u"], True)
    home(0, quarter)
    reduce(8, 6, 6, 12)
    home(quarter, 2 * quarter)
    reduce(9, 8, 8, 12)
    home(2 * quarter, 3 * quarter)
    reduce(10, 10, 9, 12)
    home(3 * quarter, blocks)
    reduce(11, 12, 11, 12)

    def grads(b, _):
        gg = s["u"][b]
        gate, value = s["inner"][:, lanes(b)].astype(F32), s["values"][:, lanes(b)].astype(F32)
        s["inner"][:, lanes(b)] = (gg * value).astype(BF16)
        s["values"][:, lanes(b)] = (gg * gate).astype(BF16)
        return 0

    lax.fori_loop(0, blocks, grads, 0)
    stores[PIECES + 1].start()
    stores[PIECES + 2].start()
    reduce(12, 12, 12, 12)
    for n in range(PIECES):
        b_copy(n).wait_recv()
        s["bo"][:, piece(n)] = (s["bo"][:, piece(n)].astype(F32) + s["br"][n].astype(F32)).astype(BF16)
        stores[n].start()
    reduce(16, 16, 12, 12)
    wg_last()

    w_drain()
    wg_drain()
    for n in range(PIECES):
        og_copy(n).wait_send()
        b_copy(n).wait_send()
    for d in (0, 1):
        for t in (1, 2, 3):
            near_copy(d, t).wait_send()
        far_sends(d, "wait_send")
    for copy in stores:
        copy.wait()


def fused(outer_gate, inner_gate, values, out_weight, skip_gain, residues, decay_rates, out_grad):
    rows, channels = values.shape
    ctx = lax.axis_size("ctx")
    scratch = fused_scratch(rows, channels)
    shape = jax.ShapeDtypeStruct
    small = pl.BlockSpec(memory_space=pltpu.VMEM)
    large = pl.BlockSpec(memory_space=pl.ANY)
    tile = shape((rows, channels), BF16)
    outs = pl.pallas_call(
        functools.partial(fused_kernel, tuple(scratch), rows * ctx),
        out_shape=[tile] * 4 + [shape(out_weight.shape, F32)],
        in_specs=[small] * 3 + [large] * 5,
        out_specs=[large] * 5,
        scratch_shapes=list(scratch.values()),
        compiler_params=pltpu.CompilerParams(
            collective_id=3, has_side_effects=True, vmem_limit_bytes=VMEM_BYTES
        ),
        cost_estimate=pl.CostEstimate(flops=6 * 2**30, bytes_accessed=10 * 2**20, transcendentals=0),
        name="fused",
    )(decay_rates.T, residues.T, skip_gain[None], outer_gate, inner_gate, values, out_weight, out_grad)
    return hand_over(outs)


def hand_over_kernel(count, *refs):
    ins, outs, held = refs[:count], refs[count : 2 * count], refs[2 * count : 3 * count]
    sems = refs[-1]
    loads = [pltpu.make_async_copy(a, b, sems.at[0, n]) for n, (a, b) in enumerate(zip(ins, held))]
    stores = [pltpu.make_async_copy(a, b, sems.at[1, n]) for n, (a, b) in enumerate(zip(held, outs))]
    for copy in loads:
        copy.start()
    for load, store in zip(loads, stores):
        load.wait()
        store.start()
    for copy in stores:
        copy.wait()


def hand_over(arrays):
    count = len(arrays)
    large = pl.BlockSpec(memory_space=pl.ANY)
    return pl.pallas_call(
        functools.partial(hand_over_kernel, count),
        out_shape=[jax.ShapeDtypeStruct(x.shape, x.dtype) for x in arrays],
        in_specs=[large] * count,
        out_specs=[large] * count,
        scratch_shapes=[pltpu.VMEM(x.shape, x.dtype) for x in arrays] + [pltpu.SemaphoreType.DMA((2, count))],
        compiler_params=pltpu.CompilerParams(vmem_limit_bytes=VMEM_BYTES),
        name="hand_over",
    )(*arrays)


def solution(mesh):
    tile = P("ctx", "fsdp")
    small = dict(mesh.shape) == {"ctx": 16, "fsdp": 2}
    return jax.shard_map(
        fused if small else shards,
        mesh=mesh,
        in_specs=(tile, tile, tile, tile, P("fsdp"), P("fsdp", None), P("fsdp", None), tile),
        out_specs=(tile,) * 5,
        check_vma=False,
    )
```

```python
import functools
import math

import jax
import jax.numpy as jnp
from jax import lax
from jax.experimental import pallas as pl
from jax.experimental.pallas import tpu as pltpu
from jax.sharding import PartitionSpec as P

F32 = jnp.float32
BF16 = jnp.bfloat16
LANES = 128
SEGS = 8
VMEM_BYTES = 62 * 2**20


def rows_at(i, steps):
    return pl.ds(i, SEGS, stride=steps)


def spread(row):
    return jnp.broadcast_to(row, (SEGS, LANES))


def segment_states(u_scr, decay_ref, pre_ref, end_ref, reverse):
    modes = decay_ref.shape[0]
    steps = u_scr.shape[0] // SEGS
    a = [spread(jnp.exp(-decay_ref[r : r + 1, :])) for r in range(modes)]

    def step(k, states):
        i = steps - 1 - k if reverse else k
        u = u_scr[rows_at(i, steps), :]
        return tuple(a[r] * states[r] + u for r in range(modes))

    zero = jnp.zeros((SEGS, LANES), F32)
    states = lax.fori_loop(0, steps, step, (zero,) * modes, unroll=4)
    seg = lax.broadcasted_iota(jnp.int32, (SEGS, LANES), 0)

    def moved(x, by):
        if reverse:
            return jnp.where(seg < SEGS - by, pltpu.roll(x, SEGS - by, 0), 0.0)
        return jnp.where(seg >= by, pltpu.roll(x, by, 0), 0.0)

    last = 0 if reverse else SEGS - 1
    for r in range(modes):
        rate = spread(decay_ref[r : r + 1, :])
        x = states[r]
        for by in (1, 2, 4):
            x = x + jnp.exp(-rate * float(steps * by)) * moved(x, by)
        end_ref[r : r + 1, :] = x[last : last + 1, :]
        pre_ref[r] = moved(x, 1)


def full_scan(u_scr, y_scr, decay_ref, res_ref, pre_ref, incoming_ref, reverse):
    modes = decay_ref.shape[0]
    rows = u_scr.shape[0]
    steps = rows // SEGS
    seg = lax.broadcasted_iota(jnp.int32, (SEGS, LANES), 0)
    ahead = ((SEGS - 1 - seg if reverse else seg) * steps).astype(F32)
    a = []
    first = []
    for r in range(modes):
        rate = spread(decay_ref[r : r + 1, :])
        a.append(jnp.exp(-rate))
        first.append(pre_ref[r] + jnp.exp(-rate * ahead) * incoming_ref[r : r + 1, :])
    res = [spread(res_ref[r : r + 1, :]) for r in range(modes)]

    def step(k, states):
        i = steps - 1 - k if reverse else k
        u = u_scr[rows_at(i, steps), :]
        states = tuple(a[r] * states[r] + u for r in range(modes))
        terms = [res[r] * states[r] for r in range(modes)]
        while len(terms) > 1:
            terms = [p + q for p, q in zip(terms[::2], terms[1::2])]
        y_scr[rows_at(i, steps), :] = terms[0]
        return states

    lax.fori_loop(0, steps, step, tuple(first), unroll=2)


def forward_ends(inner_ref, values_ref, decay_ref, pre_ref, end_ref, u_scr):
    u_scr[...] = inner_ref[...].astype(F32) * values_ref[...].astype(F32)
    segment_states(u_scr, decay_ref, pre_ref, end_ref, False)


def forward_finish(
    inner_ref, values_ref, outer_ref, decay_ref, res_ref, skip_ref, pre_ref, incoming_ref,
    filtered_ref, modulated_ref, u_scr, y_scr,
):
    u_scr[...] = inner_ref[...].astype(F32) * values_ref[...].astype(F32)
    full_scan(u_scr, y_scr, decay_ref, res_ref, pre_ref, incoming_ref, False)
    filtered = y_scr[...] + skip_ref[...] * u_scr[...]
    filtered_ref[...] = filtered
    modulated_ref[...] = (outer_ref[...].astype(F32) * filtered).astype(BF16)


def backward_ends(own_ref, other_ref, outer_ref, decay_ref, pre_ref, end_ref, u_scr):
    grad = own_ref[...].astype(F32) + other_ref[...].astype(F32)
    u_scr[...] = grad * outer_ref[...].astype(F32)
    segment_states(u_scr, decay_ref, pre_ref, end_ref, True)


def backward_finish(
    own_ref, other_ref, outer_ref, inner_ref, values_ref, filtered_ref, decay_ref, res_ref, skip_ref,
    pre_ref, incoming_ref, outer_grad_ref, inner_grad_ref, value_grad_ref, u_scr, y_scr,
):
    grad = own_ref[...].astype(F32) + other_ref[...].astype(F32)
    u_scr[...] = grad * outer_ref[...].astype(F32)
    outer_grad_ref[...] = (grad * filtered_ref[...]).astype(BF16)
    full_scan(u_scr, y_scr, decay_ref, res_ref, pre_ref, incoming_ref, True)
    gated_grad = y_scr[...] + skip_ref[...] * u_scr[...]
    inner_grad_ref[...] = (gated_grad * values_ref[...].astype(F32)).astype(BF16)
    value_grad_ref[...] = (gated_grad * inner_ref[...].astype(F32)).astype(BF16)


def by_lanes(kernel, operands, outs, rows, scans):
    channels = operands[0].shape[-1]

    def spec(x):
        lead = x.shape[:-1]
        return pl.BlockSpec(lead + (LANES,), lambda c, n=len(lead): (0,) * n + (c,))

    work = rows * channels * (24000 if scans > 1 else 16000)
    moved = sum(math.prod(x.shape) * x.dtype.itemsize for x in list(operands) + list(outs))
    return pl.pallas_call(
        kernel,
        grid=(channels // LANES,),
        out_shape=outs,
        in_specs=[spec(x) for x in operands],
        out_specs=[spec(x) for x in outs],
        scratch_shapes=[pltpu.VMEM((rows, LANES), F32)] * scans,
        cost_estimate=pl.CostEstimate(flops=work, bytes_accessed=moved, transcendentals=0),
        name=kernel.__name__,
    )(*operands)


def prefix_kernel(reverse, rows, end_ref, decay_ref, out_ref, sent, got, send_sem, recv_sem):
    me, n = lax.axis_index("ctx"), lax.axis_size("ctx")
    hops = [1 << k for k in range(sent.shape[0])]
    barrier = pltpu.get_barrier_semaphore()
    for hop in hops:
        for peer in (lax.rem(me + hop, n), lax.rem(me + n - hop, n)):
            pl.semaphore_signal(
                barrier, inc=1, device_id={"ctx": peer}, device_id_type=pl.DeviceIdType.MESH
            )
    pl.semaphore_wait(barrier, 2 * len(hops))
    decay = decay_ref[...]
    upto = end_ref[...]
    before = jnp.zeros_like(upto)
    for k, hop in enumerate(hops):
        sent[k] = upto.astype(BF16)
        copy = pltpu.make_async_remote_copy(
            src_ref=sent.at[k],
            dst_ref=got.at[k],
            send_sem=send_sem.at[k],
            recv_sem=recv_sem.at[k],
            device_id={"ctx": lax.rem(me + (n - hop if reverse else hop), n)},
            device_id_type=pl.DeviceIdType.MESH,
        )
        copy.start()
        near = jnp.exp(-decay * float(rows * (hop - 1)))
        far = jnp.exp(-decay * float(rows * hop))
        copy.wait()
        inside = (me + hop < n) if reverse else (me >= hop)
        term = got[k].astype(F32) * jnp.where(inside, 1.0, 0.0)
        before = before + near * term
        upto = upto + far * term
    out_ref[...] = before


def prefix(end, decay, rows, reverse):
    hops = max(1, (lax.axis_size("ctx") - 1).bit_length())
    whole = pl.BlockSpec(memory_space=pltpu.VMEM)
    return pl.pallas_call(
        functools.partial(prefix_kernel, reverse, rows),
        out_shape=jax.ShapeDtypeStruct(end.shape, F32),
        in_specs=[whole, whole],
        out_specs=whole,
        scratch_shapes=[
            pltpu.VMEM((hops,) + end.shape, BF16),
            pltpu.VMEM((hops,) + end.shape, BF16),
            pltpu.SemaphoreType.DMA((hops,)),
            pltpu.SemaphoreType.DMA((hops,)),
        ],
        compiler_params=pltpu.CompilerParams(
            collective_id=2 if reverse else 1, has_side_effects=True
        ),
        cost_estimate=pl.CostEstimate(flops=18 * 10**9, bytes_accessed=0, transcendentals=0),
        name="prefix_back" if reverse else "prefix_ahead",
    )(end, decay)


def shards(outer_gate, inner_gate, values, out_weight, skip_gain, residues, decay_rates, out_grad):
    rows, channels = values.shape
    modes = decay_rates.shape[1]
    ctx, fsdp = lax.axis_size("ctx"), lax.axis_size("fsdp")
    at = lax.axis_index("fsdp")
    swap = [(0, 1), (1, 0)]
    shape = jax.ShapeDtypeStruct
    panel = lax.all_gather(out_weight, "ctx", axis=0, tiled=True)
    decay = decay_rates.T
    res = residues.T
    skip = skip_gain[None]
    state_outs = [shape((modes, SEGS, channels), F32), shape((modes, channels), F32)]
    pre, end = by_lanes(forward_ends, (inner_gate, values, decay), state_outs, rows, 1)
    incoming = prefix(end, decay, rows, False)
    filtered, modulated = by_lanes(
        forward_finish,
        (inner_gate, values, outer_gate, decay, res, skip, pre, incoming),
        [shape((rows, channels), F32), shape((rows, channels), BF16)],
        rows,
        2,
    )
    if fsdp == 2:
        other = lax.ppermute(modulated, "fsdp", swap)
        first = jnp.where(at == 0, modulated, other)
        second = jnp.where(at == 0, other, modulated)
        gathered = jnp.concatenate([first, second], axis=1)
        mine = lax.dynamic_slice_in_dim(panel, at * channels, channels, 0)
        theirs = lax.dynamic_slice_in_dim(panel, (1 - at) * channels, channels, 0)
        for_them = jnp.dot(out_grad, theirs.T, preferred_element_type=F32).astype(BF16)
        from_them = lax.ppermute(for_them, "fsdp", swap)
        own = jnp.dot(out_grad, mine.T, preferred_element_type=F32).astype(BF16)
    else:
        gathered = lax.all_gather(modulated, "fsdp", axis=1, tiled=True)
        partial = jnp.dot(out_grad, panel.T, preferred_element_type=F32).astype(BF16)
        own = lax.psum_scatter(partial, "fsdp", scatter_dimension=1, tiled=True)
        from_them = jnp.zeros_like(own)
    grad_rows = lax.dot_general(
        gathered, out_grad, (((0,), (0,)), ((), ())), preferred_element_type=F32
    ).astype(BF16)
    weight_grad = lax.psum_scatter(grad_rows, "ctx", scatter_dimension=0, tiled=True)
    block_out = jnp.dot(gathered, panel, preferred_element_type=F32).astype(BF16)
    pre, end = by_lanes(
        backward_ends, (own, from_them, outer_gate, decay), state_outs, rows, 1
    )
    incoming = prefix(end, decay, rows, True)
    outer_grad, inner_grad, value_grad = by_lanes(
        backward_finish,
        (own, from_them, outer_gate, inner_gate, values, filtered, decay, res, skip, pre, incoming),
        [shape((rows, channels), BF16)] * 3,
        rows,
        2,
    )
    weight_grad, value_grad = lax.optimization_barrier((weight_grad, value_grad))
    weight_grad = weight_grad.astype(F32) * (1.0 / math.sqrt(rows * ctx))
    return (block_out, outer_grad, inner_grad, value_grad, weight_grad)


TAPS = 16
GRAN = 16
PER = LANES // GRAN
WIDE = TAPS * GRAN
SUB = 2
PIECES = 4
GATHER = (
    (0, 1, 2, 3, 4, 5, 8, 9, 6, 7, 10, 11, 12, 13, 14, 15),
    (0, 1, 2, 3, 4, 5, 8, 9, 6, 7, 10, 11, 12, 13, 14, 15),
    (0, 1, 2, 8, 3, 9, 4, 5, 6, 7, 10, 11, 12, 13, 14, 15),
    (0, 1, 2, 3, 8, 4, 5, 9, 10, 6, 11, 7, 12, 13, 14, 15),
)
RSUB = 4
SHIP = 4
SHIPPED = 2
REDUCE = (
    (8, 9, 10, 11, 0, 1, 2, 3, 12, 13, 14, 15, 4, 5, 6, 7),
    (12, 13, 14, 15, 4, 8, 5, 9, 6, 10, 7, 11, 0, 1, 2, 3),
    (12, 13, 14, 15, 4, 5, 6, 7, 0, 1, 2, 3),
    (12, 13, 14, 15, 4, 5, 6, 7, 0, 1, 2, 3),
)
MESH = pl.DeviceIdType.MESH
ORDER = ((1, True), (0, True), (1, False), (0, False))


def regroup(v):
    lane = lax.broadcasted_iota(jnp.int32, v[0].shape, 1) // GRAN
    v = list(v)
    for m in (1, 2, 4):
        low = (lane & m) == 0
        for i in range(PER):
            if i & m:
                continue
            p, q = v[i], v[i + m]
            v[i] = jnp.where(low, p, pltpu.roll(q, GRAN * m, 1))
            v[i + m] = jnp.where(low, pltpu.roll(p, LANES - GRAN * m, 1), q)
    return v


def row_at(k, s, steps, reverse):
    return TAPS * (steps - 1 - k) + TAPS - 1 - s if reverse else TAPS * k + s


def regroup_filters(decay_ref, res_ref, skip_ref, par_ref, gen_ref):
    row = lax.broadcasted_iota(jnp.int32, (SEGS, LANES), 0)
    lag = lax.broadcasted_iota(jnp.int32, (TAPS, LANES), 0)
    lags = lag.astype(F32)

    def block(b, _):
        cols = pl.ds(pl.multiple_of(b * LANES, LANES), LANES)
        kern = jnp.where(lag == 0, jnp.broadcast_to(skip_ref[:, cols], (TAPS, LANES)), 0.0)
        for r in range(TAPS):
            kern = kern + res_ref[r : r + 1, cols] * jnp.exp(-decay_ref[r : r + 1, cols] * lags)
        gen_ref[...] = kern
        for half in range(2):
            v = []
            for s in range(half * PER, (half + 1) * PER):
                rate = jnp.broadcast_to(decay_ref[s : s + 1, cols], (SEGS, LANES))
                res = jnp.broadcast_to(res_ref[s : s + 1, cols], (SEGS, LANES))
                tap = jnp.broadcast_to(gen_ref[s : s + 1, :], (SEGS, LANES))
                v.append(jnp.where(row == 0, rate, jnp.where(row == 1, res, tap)))
            for h, out in enumerate(regroup(v)):
                par_ref[b * PER + h, :, half * LANES : (half + 1) * LANES] = out
        return 0

    lax.fori_loop(0, decay_ref.shape[1] // LANES, block, 0)


def build_tables(par_ref, rate_ref, taps_ref, outs, first, groups):
    shape = (GRAN, WIDE)
    diagonal = lax.broadcasted_iota(jnp.int32, shape, 1) % GRAN == lax.broadcasted_iota(jnp.int32, shape, 0)
    lag = lax.broadcasted_iota(jnp.int32, (TAPS, WIDE), 0)
    lags = lag.astype(F32)
    at = lax.broadcasted_iota(jnp.int32, (TAPS, WIDE), 1) // GRAN

    def group(n, _):
        for d in range(4):
            g = first + 4 * n + d
            rate = par_ref[g, 0:1, :]
            for i in outs:
                if i == 0:
                    rate_ref[pl.ds(g, 1), :] = rate
                    taps_ref[d, i] = jnp.exp(-rate * (TAPS - 1 - lags))
                elif i == 1:
                    taps_ref[d, i] = par_ref[g, 1:2, :] * jnp.exp(-rate * (lags + 1))
                else:
                    kern = jnp.broadcast_to(par_ref[g, 2:3, :], (TAPS, WIDE))
                    taps_ref[d, i] = jnp.where(at >= lag, pltpu.roll(kern, 0, 1, stride=GRAN, stride_axis=0), 0.0)
        for d in range(4):
            g = first + 4 * n + d
            for i, out in outs.items():
                for s in range(TAPS):
                    line = jnp.broadcast_to(taps_ref[d, i, s : s + 1, :], shape)
                    out[g, s * GRAN : (s + 1) * GRAN, :] = jnp.where(diagonal, line, 0.0).astype(BF16)
        return 0

    lax.fori_loop(0, groups // 4, group, 0)


def moved(x, by, reverse):
    seg = lax.broadcasted_iota(jnp.int32, x.shape, 0)
    if reverse:
        return jnp.where(seg < SEGS - by, pltpu.roll(x, SEGS - by, 0), 0.0)
    return jnp.where(seg >= by, pltpu.roll(x, by, 0), 0.0)


def conv_in(u_ref, z_ref, tail_ref, rate_ref, e_ref, pre_ref, end_ref, reverse):
    blocks, rows, _ = u_ref.shape
    stride = rows // SEGS
    steps = stride // TAPS
    last = 0 if reverse else SEGS - 1

    def split(b):
        for half in range(2):
            for k in range(0, steps, 2):
                pair = [
                    regroup(
                        [
                            u_ref[b, pl.ds(row_at(n, half * PER + j, steps, reverse), SEGS, stride=stride), :]
                            for j in range(PER)
                        ]
                    )
                    for n in (k, k + 1)
                ]
                for h in range(PER):
                    z_ref[b * PER + h, k * SEGS : (k + 2) * SEGS, half * LANES : (half + 1) * LANES] = (
                        jnp.concatenate([pair[0][h], pair[1][h]], axis=0).astype(BF16)
                    )

    def ends(b):
        for h in range(PER):
            g = b * PER + h
            e = jnp.dot(z_ref[g], tail_ref[g], preferred_element_type=F32)
            e_ref[g] = e
            rate = jnp.broadcast_to(rate_ref[pl.ds(g, 1), :], (SEGS, WIDE))
            a = jnp.exp(-rate * float(TAPS))
            x = e[0:SEGS]
            for k in range(1, steps):
                x = a * x + e[k * SEGS : (k + 1) * SEGS]
            for by in (1, 2, 4):
                x = x + jnp.exp(-rate * float(TAPS * steps * by)) * moved(x, by, reverse)
            end_ref[pl.ds(g, 1), :] = x[last : last + 1, :]
            pre_ref[g] = moved(x, 1, reverse)

    return pipelined(split, ends, blocks)


def pipelined(first, second, blocks):
    def body(b, _):
        second(b - 1)
        first(b)
        return 0

    def run(lo, hi):
        if lo == 0:
            first(0)
        lax.fori_loop(max(lo, 1), hi, body, 0)
        if hi == blocks:
            second(blocks - 1)

    return run


def conv_out(z_ref, toep_ref, rise_ref, rate_ref, e_ref, pre_ref, inc_ref, y_ref, reverse):
    groups, chunks, _ = z_ref.shape
    steps = chunks // SEGS
    stride = y_ref.shape[1] // SEGS

    def finish(b):
        seg = lax.broadcasted_iota(jnp.int32, (SEGS, WIDE), 0)
        ahead = ((SEGS - 1 - seg if reverse else seg) * (TAPS * steps)).astype(F32)
        for h in range(PER):
            g = b * PER + h
            rate = jnp.broadcast_to(rate_ref[pl.ds(g, 1), :], (SEGS, WIDE))
            a = jnp.exp(-rate * float(TAPS))
            x = pre_ref[g] + jnp.exp(-rate * ahead) * inc_ref[pl.ds(g, 1), :]
            states = [x]
            for k in range(steps - 1):
                x = a * x + e_ref[g, k * SEGS : (k + 1) * SEGS]
                states.append(x)
            s = jnp.concatenate(states, axis=0).astype(BF16)
            y = jnp.dot(z_ref[g], toep_ref[g], preferred_element_type=F32)
            e_ref[g] = y + lax.dot_general(s, rise_ref[g], (((1,), (1,)), ((), ())), preferred_element_type=F32)

    def merge(b):
        for half in range(2):
            for k in range(steps):
                v = regroup(
                    [
                        e_ref[b * PER + h, k * SEGS : (k + 1) * SEGS, half * LANES : (half + 1) * LANES]
                        for h in range(PER)
                    ]
                )
                for j in range(PER):
                    y_ref[b, pl.ds(row_at(k, half * PER + j, steps, reverse), SEGS, stride=stride), :] = v[j]

    return pipelined(finish, merge, groups // PER)


def fused_scratch(rows, channels):
    blocks, groups = channels // LANES, channels // GRAN
    chunks = rows // TAPS
    part = channels // 8
    dma = pltpu.SemaphoreType.DMA
    v = pltpu.VMEM
    return dict(
        tail=v((groups, WIDE, WIDE), BF16),
        rise=v((groups, WIDE, WIDE), BF16),
        toep=v((groups, WIDE, WIDE), BF16),
        par=v((groups, SEGS, WIDE), F32),
        rate=v((groups, WIDE), F32),
        taps=v((4, 3, TAPS, WIDE), F32),
        gen=v((TAPS, LANES), F32),
        inner=v((rows, channels), BF16),
        values=v((rows, channels), BF16),
        outer=v((rows, channels), BF16),
        og=v((2, rows, channels), BF16),
        w=v((2, 8, part, channels), BF16),
        u=v((blocks, rows, LANES), F32),
        y=v((blocks, rows, LANES), F32),
        z=v((groups, chunks, WIDE), BF16),
        e=v((groups, chunks, WIDE), F32),
        pre=v((groups, SEGS, WIDE), F32),
        end=v((groups, WIDE), F32),
        before=v((groups, WIDE), F32),
        inc=v((groups, WIDE), F32),
        near=v((2, 4, groups, WIDE), BF16),
        total=v((2, groups, WIDE), BF16),
        far=v((2, 4, groups, WIDE), BF16),
        mod=v((rows, channels), BF16),
        modt=v((channels, rows), BF16),
        bs=v((PIECES, rows, channels // PIECES), BF16),
        br=v((PIECES, rows, channels // PIECES), BF16),
        bo=v((rows, channels), BF16),
        part=v((2, 8, part, channels), BF16),
        rc=v((4, 2, part, channels), BF16),
        ys=v((4, part, channels), BF16),
        ry=v((4, part, channels), BF16),
        zs=v((4, part, channels), BF16),
        rz=v((4, part, channels), BF16),
        rb=v((2, part, channels), BF16),
        ro=v((part, channels), BF16),
        wx=v((part, channels), BF16),
        wo=v((part, channels), F32),
        load=dma((5,)),
        store=dma((5,)),
        og_s=dma((1,)),
        og_r=dma((1,)),
        wx_s=dma((1,)),
        w_r=dma((2, 4, SUB)),
        wc_r=dma((1,)),
        up_s=dma((1,)),
        down_s=dma((1,)),
        y_s=dma((1,)),
        c_s=dma((1,)),
        cy_s=dma((1,)),
        near_s=dma((2,)),
        near_r=dma((2,)),
        far_s=dma((2,)),
        far_r=dma((2,)),
        b_s=dma((1,)),
        b_r=dma((1,)),
        rc_s=dma((1,)),
        rc_r=dma((4,)),
        ry_s=dma((1,)),
        ry_r=dma((4, RSUB)),
        rz_s=dma((1,)),
        rz_r=dma((4, RSUB)),
        rb_r=dma((2, RSUB)),
        ro_r=dma((RSUB,)),
        fx_r=dma((1,)),
    )


def fused_kernel(names, length, *refs):
    decay, res, skip, outer_in, inner_in, values_in, weight_in, grad_in = refs[:8]
    block_out, outer_out, inner_out, value_out, weight_out = refs[8:13]
    s = dict(zip(names, refs[13:]))
    rows, channels = inner_in.shape
    part = weight_in.shape[0]
    blocks = channels // LANES
    groups = channels // GRAN
    fine = part // SUB
    i, x = lax.axis_index("ctx"), lax.axis_index("fsdp")
    z, y, c = i // 4, (i // 2) % 2, i % 2
    zm = jnp.where(x == 0, z, 3 - z)
    q = i % 4

    def ctx_at(z, y, c):
        return z * 4 + y * 2 + c

    up_to = ctx_at(z + 1 - 2 * x, y, c)
    down_to = ctx_at(z - 1 + 2 * x, y, c)
    y_to = ctx_at(z, 1 - y, c)
    c_to = ctx_at(z, y, 1 - c)

    def remote(src, dst, send, recv, ctx, fsdp=x):
        return pltpu.make_async_remote_copy(
            src_ref=src, dst_ref=dst, send_sem=send, recv_sem=recv,
            device_id={"ctx": ctx, "fsdp": fsdp}, device_id_type=MESH,
        )

    def when(cond):
        return pl.when(cond)

    def sent(ref, sem):
        remote(ref, ref, sem, s["wc_r"].at[0], c_to).wait_send()

    def landed_in(ref, sem):
        remote(ref, ref, s["wx_s"].at[0], sem, c_to).wait_recv()

    loads = [
        pltpu.make_async_copy(inner_in, s["inner"], s["load"].at[0]),
        pltpu.make_async_copy(values_in, s["values"], s["load"].at[1]),
        pltpu.make_async_copy(outer_in, s["outer"], s["load"].at[2]),
        pltpu.make_async_copy(grad_in, s["og"].at[x], s["load"].at[3]),
    ]
    for copy in loads:
        copy.start()
    jown = (z % 2) * 4 + q
    source = zm < 2
    keep_w = pltpu.make_async_copy(weight_in, s["w"].at[x, jown], s["load"].at[4])
    when(source)(keep_w.start)
    s["far"][...] = jnp.zeros_like(s["far"])

    barrier = pltpu.get_barrier_semaphore()
    peers = [(ctx_at(z, (q + t) % 4 // 2, (q + t) % 2), x) for t in (1, 2, 3)]
    peers += [(ctx_at((z + t) % 4, y, c), x) for t in (1, 2, 3)] + [(i, 1 - x)]
    for ctx, fsdp in peers:
        pl.semaphore_signal(barrier, inc=1, device_id={"ctx": ctx, "fsdp": fsdp}, device_id_type=MESH)
    pl.semaphore_wait(barrier, len(peers))

    def fine_rows(t):
        return pl.ds(t * fine, fine)

    def sum_rows(t):
        return pl.ds(t * (part // RSUB), part // RSUB)

    def spot(sidx, yy, cc):
        return jnp.where(x == 0, sidx, 1 - sidx) * 4 + yy * 2 + cc

    def side(own):
        return x if own else 1 - x

    def w_cross(t):
        return remote(
            weight_in.at[fine_rows(t)], s["w"].at[x, jown, fine_rows(t)], s["wx_s"].at[0],
            s["w_r"].at[x, jown // 2, t], i, 1 - x,
        )

    def w_sends(src, g, j, t, up, down):
        dst = s["w"].at[g, j, fine_rows(t)]
        recv = s["w_r"].at[g, j // 2, t]
        return [
            (up, remote(src, dst, s["up_s"].at[0], recv, up_to)),
            (down, remote(src, dst, s["down_s"].at[0], recv, down_to)),
            (None, remote(src, dst, s["y_s"].at[0], recv, y_to)),
            (None, remote(src, dst, s["c_s"].at[0], s["wc_r"].at[0], c_to)),
        ]

    def each(sends, act):
        for cond, copy in sends:
            if cond is None:
                getattr(copy, act)()
            elif cond is not False:
                when(cond)(getattr(copy, act))

    def place(p, n):
        if n == 0:
            return p // 2, side(p % 2 == 0)
        return 1 - p % 2, side(p < 2)

    def own_sends(t):
        return w_sends(weight_in.at[fine_rows(t)], x, jown, t, None, zm == 1)

    def line_sends(p, t, n):
        sidx, g = place(p, n)
        j = spot(sidx, y, c)
        src = s["w"].at[g, j, fine_rows(t)]
        up = None if n < 3 and (sidx == 0 or n > 0) else False
        return w_sends(src, g, j, t, up, None if sidx == 1 and n == 1 else False)

    def w_wait(g, j, t):
        landed_in(s["w"].at[g, j, fine_rows(t)], s["w_r"].at[g, j // 2, t])

    def pump_line(p, t, n):
        if p == 0 and n < 2:
            return
        sidx, g = place(p, n)
        w_wait(g, spot(sidx, y, c), t)
        each(line_sends(p, t, n), "start")

    def y_pass(p, t, n):
        sidx, g = place(p, n)
        j = spot(sidx, 1 - y, c)
        at = s["w"].at[g, j, fine_rows(t)]
        return remote(at, at, s["cy_s"].at[0], s["wc_r"].at[0], c_to)

    def pump_y(p, t, n):
        sidx, g = place(p, n)
        w_wait(g, spot(sidx, 1 - y, c), t)
        y_pass(p, t, n).start()

    def w_rest():
        landed_in(s["w"].at[0], s["wc_r"].at[0])
        when(source)(keep_w.wait)

    def w_drain():
        def blocks_of(count):
            return s["w"].at[0, pl.ds(0, count)]

        when(zm >= 2)(functools.partial(sent, blocks_of(1), s["wx_s"].at[0]))
        when(zm == 0)(functools.partial(sent, blocks_of(2), s["up_s"].at[0]))
        when((zm == 1) | (zm == 2))(functools.partial(sent, blocks_of(4), s["up_s"].at[0]))
        when(zm == 1)(functools.partial(sent, blocks_of(2), s["down_s"].at[0]))
        for name in ("y_s", "c_s", "cy_s"):
            sent(blocks_of(4), s[name].at[0])

    def start_cross():
        for t in range(SUB):
            w_cross(t).start()

    def start_owned():
        for t in range(SUB):
            each(own_sends(t), "start")

    when(zm >= 2)(start_cross)
    when(source)(start_owned)

    og_copy = remote(grad_in, s["og"].at[x], s["og_s"].at[0], s["og_r"].at[0], i, 1 - x)
    og_copy.start()

    def listed(order):
        parts = 4 * SUB
        return [(pump_line if n < parts else pump_y, n % parts // SUB, n % SUB) for n in order]

    classes = [zm == n for n in range(4)]
    orders = [listed(order) for order in GATHER]
    done = [0] * len(classes)

    def pump(*counts):
        for n, cond in enumerate(classes):
            steps = orders[n][done[n] : counts[n]]
            done[n] = max(done[n], counts[n])

            def go(steps=steps, n=n):
                for act, p, t in steps:
                    act(p, t, n)

            if steps:
                when(cond)(go)

    def rate():
        return s["rate"][...]

    def near_copy(d, t):
        to = (q + t) % 4
        at = s["near"].at[d, q]
        return remote(at, at, s["near_s"].at[d], s["near_r"].at[d], ctx_at(z, to // 2, to % 2))

    def far_copy(d, t):
        to = z + t if d == 0 else z - t
        at = s["far"].at[d, z]
        return remote(s["total"].at[d], at, s["far_s"].at[d], s["far_r"].at[d], ctx_at(to, y, c))

    def far_sends(d):
        for t in (1, 2, 3):
            cond = z + t < 4 if d == 0 else z - t >= 0
            when(cond)(far_copy(d, t).start)

    def far_counted(d, count, act, name):
        for n in (1, 2, 3):
            when(count == n)(functools.partial(act, s["far"].at[d, pl.ds(0, n)], s[name].at[d]))

    def near_start(d):
        s["near"][d, q] = s["end"][...].astype(BF16)
        for t in (1, 2, 3):
            near_copy(d, t).start()

    def near_finish(d):
        landed_in(s["near"].at[d, pl.ds(0, 3)], s["near_r"].at[d])
        total = jnp.zeros((groups, WIDE), F32)
        before = jnp.zeros((groups, WIDE), F32)
        mine = q if d == 0 else 3 - q
        for k in range(4):
            rank = k if d == 0 else 3 - k
            term = s["near"][d, k].astype(F32)
            total = total + jnp.exp(-rate() * float(rows * (3 - rank))) * term
            gap = mine - rank
            weight = jnp.exp(-rate() * (rows * jnp.maximum(gap - 1, 0)).astype(F32))
            before = before + jnp.where(gap > 0, weight, 0.0) * term
        s["before"][...] = before
        s["total"][d] = total.astype(BF16)
        far_sends(d)

    def far_finish(d):
        far_counted(d, z if d == 0 else 3 - z, landed_in, "far_r")
        into = jnp.zeros((groups, WIDE), F32)
        for k in range(4):
            gap = z - k if d == 0 else k - z
            weight = jnp.exp(-rate() * (4 * rows * jnp.maximum(gap - 1, 0)).astype(F32))
            into = into + jnp.where(gap > 0, weight, 0.0) * s["far"][d, k].astype(F32)
        mine = q if d == 0 else 3 - q
        s["inc"][...] = s["before"][...] + jnp.exp(-rate() * (rows * mine).astype(F32)) * into

    def lanes(b):
        return pl.ds(pl.multiple_of(b * LANES, LANES), LANES)

    build = functools.partial(build_tables, s["par"], s["rate"], s["taps"])
    later = {1: s["rise"], 2: s["toep"]}
    regroup_filters(decay, res, skip, s["par"], s["gen"])
    loads[0].wait()
    loads[1].wait()

    def gated(b, _):
        s["u"][b] = s["inner"][:, lanes(b)].astype(F32) * s["values"][:, lanes(b)].astype(F32)
        return 0

    lax.fori_loop(0, blocks, gated, 0)
    build({0: s["tail"]}, 0, groups)
    states = (s["rate"], s["e"], s["pre"])
    ahead = conv_in(s["u"], s["z"], s["tail"], *states, s["end"], False)
    ahead(0, blocks // 2)
    pump(4, 4, 1, 0)
    ahead(blocks // 2, blocks)
    near_start(0)
    pump(8, 8, 2, 0)
    build({1: s["rise"]}, 0, groups)
    build({2: s["toep"]}, 0, groups)
    pump(8, 8, 4, 1)
    near_finish(0)
    pump(10, 10, 7, 4)
    far_finish(0)
    pump(12, 12, 8, 5)
    onward = conv_out(s["z"], s["toep"], s["rise"], *states, s["inc"], s["y"], False)
    quarter = blocks // 4
    onward(0, quarter)
    pump(12, 12, 8, 6)
    onward(quarter, 2 * quarter)
    pump(14, 14, 9, 6)
    onward(2 * quarter, 3 * quarter)
    pump(14, 14, 9, 7)
    onward(3 * quarter, blocks)
    pump(15, 15, 10, 9)
    loads[2].wait()
    loads[3].wait()

    def modulate(b, _):
        m = (s["outer"][:, lanes(b)].astype(F32) * s["y"][b]).astype(BF16)
        s["mod"][:, lanes(b)] = m
        s["modt"][pl.ds(pl.multiple_of(b * LANES, LANES), LANES), :] = m.T
        return 0

    lax.fori_loop(0, blocks, modulate, 0)
    pump(15, 15, 10, 10)

    def wg_terms(k):
        sidx, own = ORDER[k]
        g, first = side(own), spot(sidx, 0, 0)
        height = 4 * part
        lhs = pl.ds(pl.multiple_of(first * part, height), height)

        def tile(n, _):
            cols = pl.ds(pl.multiple_of(n * 256, 256), 256)
            t = jnp.dot(s["modt"][lhs, :], s["og"][g, :, cols], preferred_element_type=F32)
            s["part"][g, pl.ds(first, 4), :, cols] = t.astype(BF16).reshape(4, part, 256)
            return 0

        lax.fori_loop(0, channels // 256, tile, 0)
        for yy in (0, 1):
            rc_copy(k, yy).start()

    def rc_copy(k, yy):
        sidx, own = ORDER[k]
        return remote(
            s["part"].at[side(own), spot(sidx, yy, 1 - c)], s["rc"].at[k, yy],
            s["rc_s"].at[0], s["rc_r"].at[k], c_to,
        )

    def ry_copy(k, t):
        return remote(
            s["ys"].at[k, sum_rows(t)], s["ry"].at[k, sum_rows(t)],
            s["ry_s"].at[0], s["ry_r"].at[k, t], y_to,
        )

    def ship_copy(t, own_row):
        r = sum_rows(t)
        if own_row:
            return rz_copy(SHIPPED, t)
        return remote(s["ys"].at[SHIPPED, r], s["ro"].at[r], s["ry_s"].at[0], s["ro_r"].at[t], down_to)

    def wg_ship(first, last, n):
        if first == 0:
            landed_in(s["rc"].at[SHIPPED], s["rc_r"].at[SHIPPED])
        for t in range(first, last):
            r = sum_rows(t)
            for own_row, out, landed in ((False, "ys", s["ro"]), (True, "zs", s["rz"].at[SHIPPED])):
                yy = y if own_row else 1 - y
                term = s["part"][side(ORDER[SHIPPED][1]), spot(1, yy, c), r].astype(F32) + s["rc"][SHIPPED, yy, r].astype(F32)
                if n == 2:
                    ship_copy(t, own_row).wait_recv()
                    term = term + landed[r].astype(F32)
                s[out][SHIPPED, r] = term.astype(BF16)
                ship_copy(t, own_row).start()

    def wg_y(k, first=0, last=RSUB):
        sidx, own = ORDER[k]
        if first == 0:
            landed_in(s["rc"].at[k], s["rc_r"].at[k])
        for t in range(first, last):
            r = sum_rows(t)
            term = s["part"][side(own), spot(sidx, 1 - y, c), r].astype(F32) + s["rc"][k, 1 - y, r].astype(F32)
            s["ys"][k, r] = term.astype(BF16)
            if k == SHIPPED:

                def shipped(t=t, r=r):
                    ship_copy(t, False).wait_recv()
                    s["ys"][SHIPPED, r] = (s["ys"][SHIPPED, r].astype(F32) + s["ro"][r].astype(F32)).astype(BF16)

                when(zm == (1 if t < SHIP else 2))(shipped)
            ry_copy(k, t).start()

    def rz_copy(k, t, back=False):
        r = sum_rows(t)
        if back:
            return remote(s["zs"].at[k, r], s["rb"].at[k // 2, r], s["rz_s"].at[0], s["rb_r"].at[k // 2, t], up_to)
        return remote(s["zs"].at[k, r], s["rz"].at[k, r], s["rz_s"].at[0], s["rz_r"].at[k, t], down_to)

    def fx_copy(k, t):
        r = sum_rows(t)
        return remote(s["zs"].at[k, r], s["wx"].at[r], s["rz_s"].at[0], s["fx_r"].at[0], i, 1 - x)

    scale = 1.0 / math.sqrt(length)

    def wg_z(k, t, n):
        sidx, own = ORDER[k]
        r = sum_rows(t)
        ry_copy(k, t).wait_recv()
        acc = (
            s["part"][side(own), spot(sidx, y, c), r].astype(F32)
            + s["rc"][k, y, r].astype(F32)
            + s["ry"][k, r].astype(F32)
        )
        if (sidx == 0 and n < 3) or (sidx == 1 and n in (1, 2)):
            rz_copy(k, t).wait_recv()
            acc = acc + s["rz"][k, r].astype(F32)
        if sidx == 1 and n == 1:
            rz_copy(k, t, True).wait_recv()
            acc = acc + s["rb"][k // 2, r].astype(F32)
        if own and n == sidx:
            s["wo"][r] = acc * scale
            return
        s["zs"][k, r] = acc.astype(BF16)
        if n > sidx:
            rz_copy(k, t).start()
        elif n < sidx:
            rz_copy(k, t, True).start()
        else:
            fx_copy(k, t).start()

    def wg_last():
        def take():
            landed_in(s["wx"], s["fx_r"].at[0])
            s["wo"][...] = s["wx"][...].astype(F32) * scale

        when(zm >= 2)(take)
        stores[-1].start()

    def wg_drain():
        sent(s["rc"], s["rc_s"].at[0])
        sent(s["ys"], s["ry_s"].at[0])
        when(zm < 2)(functools.partial(sent, s["zs"].at[pl.ds(0, 3)], s["rz_s"].at[0]))
        when(zm >= 2)(functools.partial(sent, s["zs"], s["rz_s"].at[0]))

    width = channels // PIECES

    def piece(n):
        return pl.ds(n * width, width)

    stores = [
        pltpu.make_async_copy(src, dst, s["store"].at[n])
        for n, (src, dst) in enumerate(
            (
                (s["bo"], block_out),
                (s["outer"], outer_out),
                (s["inner"], inner_out),
                (s["values"], value_out),
                (s["wo"], weight_out),
            )
        )
    ]

    def b_copy(n):
        return remote(s["bs"].at[n], s["br"].at[n], s["b_s"].at[0], s["b_r"].at[0], i, 1 - x)

    def projected(g, n):
        return jnp.dot(
            s["mod"][...], s["w"][g, :, :, piece(n)].reshape(channels, width), preferred_element_type=F32
        )

    landed_in(s["og"].at[1 - x], s["og_r"].at[0])
    wg_terms(SHIPPED)
    pump(16, 16, 13, 11)
    wg_terms(1)
    pump(16, 16, 14, 12)
    when(zm == 0)(functools.partial(wg_y, SHIPPED))
    when(zm == 3)(functools.partial(wg_ship, 0, RSUB, 3))
    wg_terms(3)
    pump(16, 16, 15, 13)
    wg_y(3)
    wg_terms(0)
    pump(16, 16, 16, 16)
    w_rest()
    when(zm == 2)(functools.partial(wg_ship, 0, 1, 2))
    when(zm == 3)(functools.partial(wg_y, 1))
    turns = [0] * 4

    sums = [[(at // RSUB, at % RSUB) for at in order] for order in REDUCE]

    def reduce(*counts):
        for n in range(4):
            steps = sums[n][turns[n] : counts[n]]
            turns[n] = max(turns[n], counts[n])

            def go(steps=steps, n=n):
                for k, t in steps:
                    wg_z(k, t, n)

            if steps:
                when(zm == n)(go)

    def gradient(p, _):
        cols = pl.ds(pl.multiple_of(p * 2 * LANES, 2 * LANES), 2 * LANES)
        grad = None
        for g in range(2):
            w = s["w"][g, pl.ds(p * (2 * LANES // part), 2 * LANES // part)].reshape(2 * LANES, channels)
            t = lax.dot_general(s["og"][g], w, (((1,), (1,)), ((), ())), preferred_element_type=F32)
            grad = t if grad is None else grad + t
        gate = s["outer"][:, cols].astype(F32)
        filtered_grad = grad * gate
        s["outer"][:, cols] = (
            grad * jnp.concatenate([s["y"][2 * p], s["y"][2 * p + 1]], axis=1)
        ).astype(BF16)
        s["u"][2 * p] = filtered_grad[:, :LANES]
        s["u"][2 * p + 1] = filtered_grad[:, LANES:]
        return 0

    lax.fori_loop(0, blocks // 2, gradient, 0)
    stores[1].start()
    when(zm == 2)(functools.partial(wg_ship, 1, 2, 2))
    for n in range(PIECES // 2):
        s["bs"][n] = projected(1 - x, n).astype(BF16)
        b_copy(n).start()
    reduce(0, 0, 0, 4)
    when(zm == 2)(functools.partial(wg_ship, 2, 3, 2))
    back = conv_in(s["u"], s["z"], s["tail"], *states, s["end"], True)
    back(0, blocks)
    near_start(1)
    when(zm == 2)(functools.partial(wg_ship, 3, RSUB, 2))
    when(zm < 3)(functools.partial(wg_y, 1))
    wg_y(0)
    reduce(4, 0, 0, 6)
    for n in range(PIECES // 2, PIECES):
        s["bs"][n] = projected(1 - x, n).astype(BF16)
        b_copy(n).start()
    reduce(4, 0, 1, 6)
    near_finish(1)
    reduce(4, 0, 2, 8)
    for n in range(PIECES):
        s["bo"][:, piece(n)] = projected(x, n).astype(BF16)
    reduce(4, 0, 4, 9)
    far_finish(1)
    when(zm == 1)(functools.partial(wg_y, SHIPPED))
    reduce(8, 4, 5, 10)
    home = conv_out(s["z"], s["toep"], s["rise"], *states, s["inc"], s["u"], True)
    home(0, quarter)
    reduce(8, 6, 6, 12)
    home(quarter, 2 * quarter)
    reduce(9, 8, 8, 12)
    home(2 * quarter, 3 * quarter)
    reduce(10, 10, 9, 12)
    home(3 * quarter, blocks)
    reduce(11, 12, 11, 12)

    def grads(b, _):
        gg = s["u"][b]
        gate, value = s["inner"][:, lanes(b)].astype(F32), s["values"][:, lanes(b)].astype(F32)
        s["inner"][:, lanes(b)] = (gg * value).astype(BF16)
        s["values"][:, lanes(b)] = (gg * gate).astype(BF16)
        return 0

    lax.fori_loop(0, blocks, grads, 0)
    stores[2].start()
    stores[3].start()
    reduce(12, 12, 12, 12)
    landed_in(s["br"], s["b_r"].at[0])
    for n in range(PIECES):
        s["bo"][:, piece(n)] = (s["bo"][:, piece(n)].astype(F32) + s["br"][n].astype(F32)).astype(BF16)
    stores[0].start()
    reduce(16, 16, 12, 12)
    wg_last()

    w_drain()
    wg_drain()
    sent(s["og"].at[0], s["og_s"].at[0])
    sent(s["bs"], s["b_s"].at[0])
    for d in (0, 1):
        sent(s["near"].at[d, pl.ds(0, 3)], s["near_s"].at[d])
        far_counted(d, 3 - z if d == 0 else z, sent, "far_s")
    for copy in stores:
        copy.wait()


def fused(outer_gate, inner_gate, values, out_weight, skip_gain, residues, decay_rates, out_grad):
    rows, channels = values.shape
    ctx = lax.axis_size("ctx")
    scratch = fused_scratch(rows, channels)
    shape = jax.ShapeDtypeStruct
    small = pl.BlockSpec(memory_space=pltpu.VMEM)
    large = pl.BlockSpec(memory_space=pl.ANY)
    tile = shape((rows, channels), BF16)
    outs = pl.pallas_call(
        functools.partial(fused_kernel, tuple(scratch), rows * ctx),
        out_shape=[tile] * 4 + [shape(out_weight.shape, F32)],
        in_specs=[small] * 3 + [large] * 5,
        out_specs=[large] * 5,
        scratch_shapes=list(scratch.values()),
        compiler_params=pltpu.CompilerParams(
            collective_id=3, has_side_effects=True, vmem_limit_bytes=VMEM_BYTES
        ),
        cost_estimate=pl.CostEstimate(flops=6 * 2**30, bytes_accessed=10 * 2**20, transcendentals=0),
        name="fused",
    )(decay_rates.T, residues.T, skip_gain[None], outer_gate, inner_gate, values, out_weight, out_grad)
    return hand_over(outs)


def hand_over_kernel(count, *refs):
    ins, outs, held = refs[:count], refs[count : 2 * count], refs[2 * count : 3 * count]
    sems = refs[-1]
    loads = [pltpu.make_async_copy(a, b, sems.at[0, n]) for n, (a, b) in enumerate(zip(ins, held))]
    stores = [pltpu.make_async_copy(a, b, sems.at[1, n]) for n, (a, b) in enumerate(zip(held, outs))]
    for copy in loads:
        copy.start()
    for load, store in zip(loads, stores):
        load.wait()
        store.start()
    for copy in stores:
        copy.wait()


def hand_over(arrays):
    count = len(arrays)
    large = pl.BlockSpec(memory_space=pl.ANY)
    return pl.pallas_call(
        functools.partial(hand_over_kernel, count),
        out_shape=[jax.ShapeDtypeStruct(x.shape, x.dtype) for x in arrays],
        in_specs=[large] * count,
        out_specs=[large] * count,
        scratch_shapes=[pltpu.VMEM(x.shape, x.dtype) for x in arrays] + [pltpu.SemaphoreType.DMA((2, count))],
        compiler_params=pltpu.CompilerParams(vmem_limit_bytes=VMEM_BYTES),
        name="hand_over",
    )(*arrays)


def solution(mesh):
    tile = P("ctx", "fsdp")
    small = dict(mesh.shape) == {"ctx": 16, "fsdp": 2}
    return jax.shard_map(
        fused if small else shards,
        mesh=mesh,
        in_specs=(tile, tile, tile, tile, P("fsdp"), P("fsdp", None), P("fsdp", None), tile),
        out_specs=(tile,) * 5,
        check_vma=False,
    )
```

```python
import functools
import math

import jax
import jax.numpy as jnp
from jax import lax
from jax.experimental import pallas as pl
from jax.experimental.pallas import tpu as pltpu
from jax.sharding import PartitionSpec as P

F32 = jnp.float32
BF16 = jnp.bfloat16
LANES = 128
SEGS = 8
VMEM_BYTES = 62 * 2**20


def rows_at(i, steps):
    return pl.ds(i, SEGS, stride=steps)


def spread(row):
    return jnp.broadcast_to(row, (SEGS, LANES))


def segment_states(u_scr, decay_ref, pre_ref, end_ref, reverse):
    modes = decay_ref.shape[0]
    steps = u_scr.shape[0] // SEGS
    a = [spread(jnp.exp(-decay_ref[r : r + 1, :])) for r in range(modes)]

    def step(k, states):
        i = steps - 1 - k if reverse else k
        u = u_scr[rows_at(i, steps), :]
        return tuple(a[r] * states[r] + u for r in range(modes))

    zero = jnp.zeros((SEGS, LANES), F32)
    states = lax.fori_loop(0, steps, step, (zero,) * modes, unroll=4)
    seg = lax.broadcasted_iota(jnp.int32, (SEGS, LANES), 0)

    def moved(x, by):
        if reverse:
            return jnp.where(seg < SEGS - by, pltpu.roll(x, SEGS - by, 0), 0.0)
        return jnp.where(seg >= by, pltpu.roll(x, by, 0), 0.0)

    last = 0 if reverse else SEGS - 1
    for r in range(modes):
        rate = spread(decay_ref[r : r + 1, :])
        x = states[r]
        for by in (1, 2, 4):
            x = x + jnp.exp(-rate * float(steps * by)) * moved(x, by)
        end_ref[r : r + 1, :] = x[last : last + 1, :]
        pre_ref[r] = moved(x, 1)


def full_scan(u_scr, y_scr, decay_ref, res_ref, pre_ref, incoming_ref, reverse):
    modes = decay_ref.shape[0]
    rows = u_scr.shape[0]
    steps = rows // SEGS
    seg = lax.broadcasted_iota(jnp.int32, (SEGS, LANES), 0)
    ahead = ((SEGS - 1 - seg if reverse else seg) * steps).astype(F32)
    a = []
    first = []
    for r in range(modes):
        rate = spread(decay_ref[r : r + 1, :])
        a.append(jnp.exp(-rate))
        first.append(pre_ref[r] + jnp.exp(-rate * ahead) * incoming_ref[r : r + 1, :])
    res = [spread(res_ref[r : r + 1, :]) for r in range(modes)]

    def step(k, states):
        i = steps - 1 - k if reverse else k
        u = u_scr[rows_at(i, steps), :]
        states = tuple(a[r] * states[r] + u for r in range(modes))
        terms = [res[r] * states[r] for r in range(modes)]
        while len(terms) > 1:
            terms = [p + q for p, q in zip(terms[::2], terms[1::2])]
        y_scr[rows_at(i, steps), :] = terms[0]
        return states

    lax.fori_loop(0, steps, step, tuple(first), unroll=2)


def forward_ends(inner_ref, values_ref, decay_ref, pre_ref, end_ref, u_scr):
    u_scr[...] = inner_ref[...].astype(F32) * values_ref[...].astype(F32)
    segment_states(u_scr, decay_ref, pre_ref, end_ref, False)


def forward_finish(
    inner_ref, values_ref, outer_ref, decay_ref, res_ref, skip_ref, pre_ref, incoming_ref,
    filtered_ref, modulated_ref, u_scr, y_scr,
):
    u_scr[...] = inner_ref[...].astype(F32) * values_ref[...].astype(F32)
    full_scan(u_scr, y_scr, decay_ref, res_ref, pre_ref, incoming_ref, False)
    filtered = y_scr[...] + skip_ref[...] * u_scr[...]
    filtered_ref[...] = filtered
    modulated_ref[...] = (outer_ref[...].astype(F32) * filtered).astype(BF16)


def backward_ends(own_ref, other_ref, outer_ref, decay_ref, pre_ref, end_ref, u_scr):
    grad = own_ref[...].astype(F32) + other_ref[...].astype(F32)
    u_scr[...] = grad * outer_ref[...].astype(F32)
    segment_states(u_scr, decay_ref, pre_ref, end_ref, True)


def backward_finish(
    own_ref, other_ref, outer_ref, inner_ref, values_ref, filtered_ref, decay_ref, res_ref, skip_ref,
    pre_ref, incoming_ref, outer_grad_ref, inner_grad_ref, value_grad_ref, u_scr, y_scr,
):
    grad = own_ref[...].astype(F32) + other_ref[...].astype(F32)
    u_scr[...] = grad * outer_ref[...].astype(F32)
    outer_grad_ref[...] = (grad * filtered_ref[...]).astype(BF16)
    full_scan(u_scr, y_scr, decay_ref, res_ref, pre_ref, incoming_ref, True)
    gated_grad = y_scr[...] + skip_ref[...] * u_scr[...]
    inner_grad_ref[...] = (gated_grad * values_ref[...].astype(F32)).astype(BF16)
    value_grad_ref[...] = (gated_grad * inner_ref[...].astype(F32)).astype(BF16)


def by_lanes(kernel, operands, outs, rows, scans):
    channels = operands[0].shape[-1]

    def spec(x):
        lead = x.shape[:-1]
        return pl.BlockSpec(lead + (LANES,), lambda c, n=len(lead): (0,) * n + (c,))

    work = rows * channels * (24000 if scans > 1 else 16000)
    moved = sum(math.prod(x.shape) * x.dtype.itemsize for x in list(operands) + list(outs))
    return pl.pallas_call(
        kernel,
        grid=(channels // LANES,),
        out_shape=outs,
        in_specs=[spec(x) for x in operands],
        out_specs=[spec(x) for x in outs],
        scratch_shapes=[pltpu.VMEM((rows, LANES), F32)] * scans,
        cost_estimate=pl.CostEstimate(flops=work, bytes_accessed=moved, transcendentals=0),
        name=kernel.__name__,
    )(*operands)


def prefix_kernel(reverse, rows, end_ref, decay_ref, out_ref, sent, got, send_sem, recv_sem):
    me, n = lax.axis_index("ctx"), lax.axis_size("ctx")
    hops = [1 << k for k in range(sent.shape[0])]
    barrier = pltpu.get_barrier_semaphore()
    for hop in hops:
        for peer in (lax.rem(me + hop, n), lax.rem(me + n - hop, n)):
            pl.semaphore_signal(
                barrier, inc=1, device_id={"ctx": peer}, device_id_type=pl.DeviceIdType.MESH
            )
    pl.semaphore_wait(barrier, 2 * len(hops))
    decay = decay_ref[...]
    upto = end_ref[...]
    before = jnp.zeros_like(upto)
    for k, hop in enumerate(hops):
        sent[k] = upto.astype(BF16)
        copy = pltpu.make_async_remote_copy(
            src_ref=sent.at[k],
            dst_ref=got.at[k],
            send_sem=send_sem.at[k],
            recv_sem=recv_sem.at[k],
            device_id={"ctx": lax.rem(me + (n - hop if reverse else hop), n)},
            device_id_type=pl.DeviceIdType.MESH,
        )
        copy.start()
        near = jnp.exp(-decay * float(rows * (hop - 1)))
        far = jnp.exp(-decay * float(rows * hop))
        copy.wait()
        inside = (me + hop < n) if reverse else (me >= hop)
        term = got[k].astype(F32) * jnp.where(inside, 1.0, 0.0)
        before = before + near * term
        upto = upto + far * term
    out_ref[...] = before


def prefix(end, decay, rows, reverse):
    hops = max(1, (lax.axis_size("ctx") - 1).bit_length())
    whole = pl.BlockSpec(memory_space=pltpu.VMEM)
    return pl.pallas_call(
        functools.partial(prefix_kernel, reverse, rows),
        out_shape=jax.ShapeDtypeStruct(end.shape, F32),
        in_specs=[whole, whole],
        out_specs=whole,
        scratch_shapes=[
            pltpu.VMEM((hops,) + end.shape, BF16),
            pltpu.VMEM((hops,) + end.shape, BF16),
            pltpu.SemaphoreType.DMA((hops,)),
            pltpu.SemaphoreType.DMA((hops,)),
        ],
        compiler_params=pltpu.CompilerParams(
            collective_id=2 if reverse else 1, has_side_effects=True
        ),
        cost_estimate=pl.CostEstimate(flops=18 * 10**9, bytes_accessed=0, transcendentals=0),
        name="prefix_back" if reverse else "prefix_ahead",
    )(end, decay)


def shards(outer_gate, inner_gate, values, out_weight, skip_gain, residues, decay_rates, out_grad):
    rows, channels = values.shape
    modes = decay_rates.shape[1]
    ctx, fsdp = lax.axis_size("ctx"), lax.axis_size("fsdp")
    at = lax.axis_index("fsdp")
    swap = [(0, 1), (1, 0)]
    shape = jax.ShapeDtypeStruct
    panel = lax.all_gather(out_weight, "ctx", axis=0, tiled=True)
    decay = decay_rates.T
    res = residues.T
    skip = skip_gain[None]
    state_outs = [shape((modes, SEGS, channels), F32), shape((modes, channels), F32)]
    pre, end = by_lanes(forward_ends, (inner_gate, values, decay), state_outs, rows, 1)
    incoming = prefix(end, decay, rows, False)
    filtered, modulated = by_lanes(
        forward_finish,
        (inner_gate, values, outer_gate, decay, res, skip, pre, incoming),
        [shape((rows, channels), F32), shape((rows, channels), BF16)],
        rows,
        2,
    )
    if fsdp == 2:
        other = lax.ppermute(modulated, "fsdp", swap)
        first = jnp.where(at == 0, modulated, other)
        second = jnp.where(at == 0, other, modulated)
        gathered = jnp.concatenate([first, second], axis=1)
        mine = lax.dynamic_slice_in_dim(panel, at * channels, channels, 0)
        theirs = lax.dynamic_slice_in_dim(panel, (1 - at) * channels, channels, 0)
        for_them = jnp.dot(out_grad, theirs.T, preferred_element_type=F32).astype(BF16)
        from_them = lax.ppermute(for_them, "fsdp", swap)
        own = jnp.dot(out_grad, mine.T, preferred_element_type=F32).astype(BF16)
    else:
        gathered = lax.all_gather(modulated, "fsdp", axis=1, tiled=True)
        partial = jnp.dot(out_grad, panel.T, preferred_element_type=F32).astype(BF16)
        own = lax.psum_scatter(partial, "fsdp", scatter_dimension=1, tiled=True)
        from_them = jnp.zeros_like(own)
    grad_rows = lax.dot_general(
        gathered, out_grad, (((0,), (0,)), ((), ())), preferred_element_type=F32
    ).astype(BF16)
    weight_grad = lax.psum_scatter(grad_rows, "ctx", scatter_dimension=0, tiled=True)
    block_out = jnp.dot(gathered, panel, preferred_element_type=F32).astype(BF16)
    pre, end = by_lanes(
        backward_ends, (own, from_them, outer_gate, decay), state_outs, rows, 1
    )
    incoming = prefix(end, decay, rows, True)
    outer_grad, inner_grad, value_grad = by_lanes(
        backward_finish,
        (own, from_them, outer_gate, inner_gate, values, filtered, decay, res, skip, pre, incoming),
        [shape((rows, channels), BF16)] * 3,
        rows,
        2,
    )
    weight_grad, value_grad = lax.optimization_barrier((weight_grad, value_grad))
    weight_grad = weight_grad.astype(F32) * (1.0 / math.sqrt(rows * ctx))
    return (block_out, outer_grad, inner_grad, value_grad, weight_grad)


TAPS = 16
GRAN = 16
PER = LANES // GRAN
WIDE = TAPS * GRAN
SUB = 2
PIECES = 4
GATHER = (
    (0, 1, 2, 3, 4, 5, 8, 9, 6, 7, 10, 11, 12, 13, 14, 15),
    (0, 1, 2, 3, 4, 5, 8, 9, 6, 7, 10, 11, 12, 13, 14, 15),
    (0, 1, 2, 8, 3, 9, 4, 5, 6, 7, 10, 11, 12, 13, 14, 15),
    (0, 1, 2, 3, 8, 4, 5, 9, 10, 6, 11, 7, 12, 13, 14, 15),
)
RSUB = 4
SHIP = 4
SHIPPED = 2
REDUCE = (
    (8, 9, 10, 11, 0, 1, 2, 3, 12, 13, 14, 15, 4, 5, 6, 7),
    (12, 13, 14, 15, 4, 8, 5, 9, 6, 10, 7, 11, 0, 1, 2, 3),
    (12, 13, 14, 15, 4, 5, 6, 7, 0, 1, 2, 3),
    (12, 13, 14, 15, 4, 5, 6, 7, 0, 1, 2, 3),
)
MESH = pl.DeviceIdType.MESH
ORDER = ((1, True), (0, True), (1, False), (0, False))


def regroup(v):
    lane = lax.broadcasted_iota(jnp.int32, v[0].shape, 1) // GRAN
    v = list(v)
    for m in (1, 2, 4):
        low = (lane & m) == 0
        for i in range(PER):
            if i & m:
                continue
            p, q = v[i], v[i + m]
            v[i] = jnp.where(low, p, pltpu.roll(q, GRAN * m, 1))
            v[i + m] = jnp.where(low, pltpu.roll(p, LANES - GRAN * m, 1), q)
    return v


def row_at(k, s, steps, reverse):
    return TAPS * (steps - 1 - k) + TAPS - 1 - s if reverse else TAPS * k + s


def regroup_filters(decay_ref, res_ref, skip_ref, par_ref, gen_ref):
    row = lax.broadcasted_iota(jnp.int32, (SEGS, LANES), 0)
    lag = lax.broadcasted_iota(jnp.int32, (TAPS, LANES), 0)
    lags = lag.astype(F32)

    def block(b, _):
        cols = pl.ds(pl.multiple_of(b * LANES, LANES), LANES)
        kern = jnp.where(lag == 0, jnp.broadcast_to(skip_ref[:, cols], (TAPS, LANES)), 0.0)
        for r in range(TAPS):
            kern = kern + res_ref[r : r + 1, cols] * jnp.exp(-decay_ref[r : r + 1, cols] * lags)
        gen_ref[...] = kern
        for half in range(2):
            v = []
            for s in range(half * PER, (half + 1) * PER):
                rate = jnp.broadcast_to(decay_ref[s : s + 1, cols], (SEGS, LANES))
                res = jnp.broadcast_to(res_ref[s : s + 1, cols], (SEGS, LANES))
                tap = jnp.broadcast_to(gen_ref[s : s + 1, :], (SEGS, LANES))
                v.append(jnp.where(row == 0, rate, jnp.where(row == 1, res, tap)))
            for h, out in enumerate(regroup(v)):
                par_ref[b * PER + h, :, half * LANES : (half + 1) * LANES] = out
        return 0

    lax.fori_loop(0, decay_ref.shape[1] // LANES, block, 0)


def build_tables(par_ref, rate_ref, taps_ref, outs, first, groups):
    shape = (GRAN, WIDE)
    diagonal = lax.broadcasted_iota(jnp.int32, shape, 1) % GRAN == lax.broadcasted_iota(jnp.int32, shape, 0)
    lag = lax.broadcasted_iota(jnp.int32, (TAPS, WIDE), 0)
    lags = lag.astype(F32)
    at = lax.broadcasted_iota(jnp.int32, (TAPS, WIDE), 1) // GRAN

    def group(n, _):
        for d in range(4):
            g = first + 4 * n + d
            rate = par_ref[g, 0:1, :]
            for i in outs:
                if i == 0:
                    rate_ref[pl.ds(g, 1), :] = rate
                    taps_ref[d, i] = jnp.exp(-rate * (TAPS - 1 - lags))
                elif i == 1:
                    taps_ref[d, i] = par_ref[g, 1:2, :] * jnp.exp(-rate * (lags + 1))
                else:
                    kern = jnp.broadcast_to(par_ref[g, 2:3, :], (TAPS, WIDE))
                    taps_ref[d, i] = jnp.where(at >= lag, pltpu.roll(kern, 0, 1, stride=GRAN, stride_axis=0), 0.0)
        for d in range(4):
            g = first + 4 * n + d
            for i, out in outs.items():
                for s in range(TAPS):
                    line = jnp.broadcast_to(taps_ref[d, i, s : s + 1, :], shape)
                    out[g, s * GRAN : (s + 1) * GRAN, :] = jnp.where(diagonal, line, 0.0).astype(BF16)
        return 0

    lax.fori_loop(0, groups // 4, group, 0)


def moved(x, by, reverse):
    seg = lax.broadcasted_iota(jnp.int32, x.shape, 0)
    if reverse:
        return jnp.where(seg < SEGS - by, pltpu.roll(x, SEGS - by, 0), 0.0)
    return jnp.where(seg >= by, pltpu.roll(x, by, 0), 0.0)


def conv_in(u_ref, z_ref, tail_ref, rate_ref, e_ref, pre_ref, end_ref, reverse):
    blocks, rows, _ = u_ref.shape
    stride = rows // SEGS
    steps = stride // TAPS
    last = 0 if reverse else SEGS - 1

    def split(b):
        for half in range(2):
            for k in range(0, steps, 2):
                pair = [
                    regroup(
                        [
                            u_ref[b, pl.ds(row_at(n, half * PER + j, steps, reverse), SEGS, stride=stride), :]
                            for j in range(PER)
                        ]
                    )
                    for n in (k, k + 1)
                ]
                for h in range(PER):
                    z_ref[b * PER + h, k * SEGS : (k + 2) * SEGS, half * LANES : (half + 1) * LANES] = (
                        jnp.concatenate([pair[0][h], pair[1][h]], axis=0).astype(BF16)
                    )

    def ends(b):
        for h in range(PER):
            g = b * PER + h
            e = jnp.dot(z_ref[g], tail_ref[g], preferred_element_type=F32)
            e_ref[g] = e
            rate = jnp.broadcast_to(rate_ref[pl.ds(g, 1), :], (SEGS, WIDE))
            a = jnp.exp(-rate * float(TAPS))
            x = e[0:SEGS]
            for k in range(1, steps):
                x = a * x + e[k * SEGS : (k + 1) * SEGS]
            for by in (1, 2, 4):
                x = x + jnp.exp(-rate * float(TAPS * steps * by)) * moved(x, by, reverse)
            end_ref[pl.ds(g, 1), :] = x[last : last + 1, :]
            pre_ref[g] = moved(x, 1, reverse)

    return pipelined(split, ends, blocks)


def pipelined(first, second, blocks):
    def body(b, _):
        second(b - 1)
        first(b)
        return 0

    def run(lo, hi):
        if lo == 0:
            first(0)
        lax.fori_loop(max(lo, 1), hi, body, 0)
        if hi == blocks:
            second(blocks - 1)

    return run


def conv_out(z_ref, toep_ref, rise_ref, rate_ref, e_ref, pre_ref, inc_ref, y_ref, reverse):
    groups, chunks, _ = z_ref.shape
    steps = chunks // SEGS
    stride = y_ref.shape[1] // SEGS

    def finish(b):
        seg = lax.broadcasted_iota(jnp.int32, (SEGS, WIDE), 0)
        ahead = ((SEGS - 1 - seg if reverse else seg) * (TAPS * steps)).astype(F32)
        for h in range(PER):
            g = b * PER + h
            rate = jnp.broadcast_to(rate_ref[pl.ds(g, 1), :], (SEGS, WIDE))
            a = jnp.exp(-rate * float(TAPS))
            x = pre_ref[g] + jnp.exp(-rate * ahead) * inc_ref[pl.ds(g, 1), :]
            states = [x]
            for k in range(steps - 1):
                x = a * x + e_ref[g, k * SEGS : (k + 1) * SEGS]
                states.append(x)
            s = jnp.concatenate(states, axis=0).astype(BF16)
            y = jnp.dot(z_ref[g], toep_ref[g], preferred_element_type=F32)
            e_ref[g] = y + lax.dot_general(s, rise_ref[g], (((1,), (1,)), ((), ())), preferred_element_type=F32)

    def merge(b):
        for half in range(2):
            for k in range(steps):
                v = regroup(
                    [
                        e_ref[b * PER + h, k * SEGS : (k + 1) * SEGS, half * LANES : (half + 1) * LANES]
                        for h in range(PER)
                    ]
                )
                for j in range(PER):
                    y_ref[b, pl.ds(row_at(k, half * PER + j, steps, reverse), SEGS, stride=stride), :] = v[j]

    return pipelined(finish, merge, groups // PER)


def fused_scratch(rows, channels):
    blocks, groups = channels // LANES, channels // GRAN
    chunks = rows // TAPS
    part = channels // 8
    dma = pltpu.SemaphoreType.DMA
    v = pltpu.VMEM
    return dict(
        tail=v((groups, WIDE, WIDE), BF16),
        rise=v((groups, WIDE, WIDE), BF16),
        toep=v((groups, WIDE, WIDE), BF16),
        par=v((groups, SEGS, WIDE), F32),
        rate=v((groups, WIDE), F32),
        taps=v((4, 3, TAPS, WIDE), F32),
        gen=v((TAPS, LANES), F32),
        inner=v((rows, channels), BF16),
        values=v((rows, channels), BF16),
        outer=v((rows, channels), BF16),
        og=v((2, rows, channels), BF16),
        w=v((2, 8, part, channels), BF16),
        u=v((blocks, rows, LANES), F32),
        y=v((blocks, rows, LANES), F32),
        z=v((groups, chunks, WIDE), BF16),
        e=v((groups, chunks, WIDE), F32),
        pre=v((groups, SEGS, WIDE), F32),
        end=v((groups, WIDE), F32),
        before=v((groups, WIDE), F32),
        inc=v((groups, WIDE), F32),
        near=v((2, 4, groups, WIDE), BF16),
        total=v((2, groups, WIDE), BF16),
        far=v((2, 4, groups, WIDE), BF16),
        mod=v((rows, channels), BF16),
        modt=v((channels, rows), BF16),
        bs=v((PIECES, rows, channels // PIECES), BF16),
        br=v((PIECES, rows, channels // PIECES), BF16),
        bo=v((rows, channels), BF16),
        part=v((2, 8, part, channels), BF16),
        rc=v((4, 2, part, channels), BF16),
        ys=v((4, part, channels), BF16),
        ry=v((4, part, channels), BF16),
        zs=v((4, part, channels), BF16),
        rz=v((4, part, channels), BF16),
        rb=v((2, part, channels), BF16),
        ro=v((part, channels), BF16),
        wx=v((part, channels), BF16),
        wo=v((part, channels), F32),
        load=dma((5,)),
        store=dma((5,)),
        og_s=dma((1,)),
        og_r=dma((1,)),
        wx_s=dma((1,)),
        w_r=dma((2, 4, SUB)),
        wc_r=dma((1,)),
        up_s=dma((1,)),
        down_s=dma((1,)),
        y_s=dma((1,)),
        c_s=dma((1,)),
        cy_s=dma((1,)),
        near_s=dma((2,)),
        near_r=dma((2,)),
        far_s=dma((2,)),
        far_r=dma((2,)),
        b_s=dma((1,)),
        b_r=dma((1,)),
        rc_s=dma((1,)),
        rc_r=dma((4,)),
        ry_s=dma((1,)),
        ry_r=dma((4, RSUB)),
        rz_s=dma((1,)),
        rz_r=dma((4, RSUB)),
        rb_r=dma((2, RSUB)),
        ro_r=dma((RSUB,)),
        fx_r=dma((1,)),
    )


def fused_kernel(names, length, *refs):
    decay, res, skip, outer_in, inner_in, values_in, weight_in, grad_in = refs[:8]
    block_out, outer_out, inner_out, value_out, weight_out = refs[8:13]
    s = dict(zip(names, refs[13:]))
    rows, channels = inner_in.shape
    part = weight_in.shape[0]
    blocks = channels // LANES
    groups = channels // GRAN
    fine = part // SUB
    i, x = lax.axis_index("ctx"), lax.axis_index("fsdp")
    z, y, c = i // 4, (i // 2) % 2, i % 2
    zm = jnp.where(x == 0, z, 3 - z)
    q = i % 4

    def ctx_at(z, y, c):
        return z * 4 + y * 2 + c

    up_to = ctx_at(z + 1 - 2 * x, y, c)
    down_to = ctx_at(z - 1 + 2 * x, y, c)
    y_to = ctx_at(z, 1 - y, c)
    c_to = ctx_at(z, y, 1 - c)

    def remote(src, dst, send, recv, ctx, fsdp=x):
        return pltpu.make_async_remote_copy(
            src_ref=src, dst_ref=dst, send_sem=send, recv_sem=recv,
            device_id={"ctx": ctx, "fsdp": fsdp}, device_id_type=MESH,
        )

    def when(cond):
        return pl.when(cond)

    def sent(ref, sem):
        remote(ref, ref, sem, s["wc_r"].at[0], c_to).wait_send()

    def landed_in(ref, sem):
        remote(ref, ref, s["wx_s"].at[0], sem, c_to).wait_recv()

    loads = [
        pltpu.make_async_copy(inner_in, s["inner"], s["load"].at[0]),
        pltpu.make_async_copy(values_in, s["values"], s["load"].at[1]),
        pltpu.make_async_copy(outer_in, s["outer"], s["load"].at[2]),
        pltpu.make_async_copy(grad_in, s["og"].at[x], s["load"].at[3]),
    ]
    for copy in loads:
        copy.start()
    jown = (z % 2) * 4 + q
    source = zm < 2
    keep_w = pltpu.make_async_copy(weight_in, s["w"].at[x, jown], s["load"].at[4])
    when(source)(keep_w.start)
    s["far"][...] = jnp.zeros_like(s["far"])

    barrier = pltpu.get_barrier_semaphore()
    peers = [(ctx_at(z, (q + t) % 4 // 2, (q + t) % 2), x) for t in (1, 2, 3)]
    peers += [(ctx_at((z + t) % 4, y, c), x) for t in (1, 2, 3)] + [(i, 1 - x)]
    for ctx, fsdp in peers:
        pl.semaphore_signal(barrier, inc=1, device_id={"ctx": ctx, "fsdp": fsdp}, device_id_type=MESH)
    pl.semaphore_wait(barrier, len(peers))

    def fine_rows(t):
        return pl.ds(t * fine, fine)

    def sum_rows(t):
        return pl.ds(t * (part // RSUB), part // RSUB)

    def spot(sidx, yy, cc):
        return jnp.where(x == 0, sidx, 1 - sidx) * 4 + yy * 2 + cc

    def side(own):
        return x if own else 1 - x

    def w_cross(t):
        return remote(
            weight_in.at[fine_rows(t)], s["w"].at[x, jown, fine_rows(t)], s["wx_s"].at[0],
            s["w_r"].at[x, jown // 2, t], i, 1 - x,
        )

    def w_sends(src, g, j, t, up, down):
        dst = s["w"].at[g, j, fine_rows(t)]
        recv = s["w_r"].at[g, j // 2, t]
        return [
            (up, remote(src, dst, s["up_s"].at[0], recv, up_to)),
            (down, remote(src, dst, s["down_s"].at[0], recv, down_to)),
            (None, remote(src, dst, s["y_s"].at[0], recv, y_to)),
            (None, remote(src, dst, s["c_s"].at[0], s["wc_r"].at[0], c_to)),
        ]

    def each(sends, act):
        for cond, copy in sends:
            if cond is None:
                getattr(copy, act)()
            elif cond is not False:
                when(cond)(getattr(copy, act))

    def place(p, n):
        if n == 0:
            return p // 2, side(p % 2 == 0)
        return 1 - p % 2, side(p < 2)

    def own_sends(t):
        return w_sends(weight_in.at[fine_rows(t)], x, jown, t, None, zm == 1)

    def line_sends(p, t, n):
        sidx, g = place(p, n)
        j = spot(sidx, y, c)
        src = s["w"].at[g, j, fine_rows(t)]
        up = None if n < 3 and (sidx == 0 or n > 0) else False
        return w_sends(src, g, j, t, up, None if sidx == 1 and n == 1 else False)

    def w_wait(g, j, t):
        landed_in(s["w"].at[g, j, fine_rows(t)], s["w_r"].at[g, j // 2, t])

    def pump_line(p, t, n):
        if p == 0 and n < 2:
            return
        sidx, g = place(p, n)
        w_wait(g, spot(sidx, y, c), t)
        each(line_sends(p, t, n), "start")

    def y_pass(p, t, n):
        sidx, g = place(p, n)
        j = spot(sidx, 1 - y, c)
        at = s["w"].at[g, j, fine_rows(t)]
        return remote(at, at, s["cy_s"].at[0], s["wc_r"].at[0], c_to)

    def pump_y(p, t, n):
        sidx, g = place(p, n)
        w_wait(g, spot(sidx, 1 - y, c), t)
        y_pass(p, t, n).start()

    def w_rest():
        landed_in(s["w"].at[0], s["wc_r"].at[0])
        when(source)(keep_w.wait)

    def w_drain():
        def blocks_of(count):
            return s["w"].at[0, pl.ds(0, count)]

        when(zm >= 2)(functools.partial(sent, blocks_of(1), s["wx_s"].at[0]))
        when(zm == 0)(functools.partial(sent, blocks_of(2), s["up_s"].at[0]))
        when((zm == 1) | (zm == 2))(functools.partial(sent, blocks_of(4), s["up_s"].at[0]))
        when(zm == 1)(functools.partial(sent, blocks_of(2), s["down_s"].at[0]))
        for name in ("y_s", "c_s", "cy_s"):
            sent(blocks_of(4), s[name].at[0])

    def start_cross():
        for t in range(SUB):
            w_cross(t).start()

    def start_owned():
        for t in range(SUB):
            each(own_sends(t), "start")

    when(zm >= 2)(start_cross)
    when(source)(start_owned)

    og_copy = remote(grad_in, s["og"].at[x], s["og_s"].at[0], s["og_r"].at[0], i, 1 - x)
    og_copy.start()

    def listed(order):
        parts = 4 * SUB
        return [(pump_line if n < parts else pump_y, n % parts // SUB, n % SUB) for n in order]

    classes = [zm == n for n in range(4)]
    orders = [listed(order) for order in GATHER]
    done = [0] * len(classes)

    def pump(*counts):
        for n, cond in enumerate(classes):
            steps = orders[n][done[n] : counts[n]]
            done[n] = max(done[n], counts[n])

            def go(steps=steps, n=n):
                for act, p, t in steps:
                    act(p, t, n)

            if steps:
                when(cond)(go)

    def rate():
        return s["rate"][...]

    def near_copy(d, t):
        to = (q + t) % 4
        at = s["near"].at[d, q]
        return remote(at, at, s["near_s"].at[d], s["near_r"].at[d], ctx_at(z, to // 2, to % 2))

    def far_copy(d, t):
        to = z + t if d == 0 else z - t
        at = s["far"].at[d, z]
        return remote(s["total"].at[d], at, s["far_s"].at[d], s["far_r"].at[d], ctx_at(to, y, c))

    def far_sends(d):
        for t in (1, 2, 3):
            cond = z + t < 4 if d == 0 else z - t >= 0
            when(cond)(far_copy(d, t).start)

    def far_counted(d, count, act, name):
        for n in (1, 2, 3):
            when(count == n)(functools.partial(act, s["far"].at[d, pl.ds(0, n)], s[name].at[d]))

    def near_start(d):
        s["near"][d, q] = s["end"][...].astype(BF16)
        for t in (1, 2, 3):
            near_copy(d, t).start()

    def near_finish(d):
        landed_in(s["near"].at[d, pl.ds(0, 3)], s["near_r"].at[d])
        total = jnp.zeros((groups, WIDE), F32)
        before = jnp.zeros((groups, WIDE), F32)
        mine = q if d == 0 else 3 - q
        for k in range(4):
            rank = k if d == 0 else 3 - k
            term = s["near"][d, k].astype(F32)
            total = total + jnp.exp(-rate() * float(rows * (3 - rank))) * term
            gap = mine - rank
            weight = jnp.exp(-rate() * (rows * jnp.maximum(gap - 1, 0)).astype(F32))
            before = before + jnp.where(gap > 0, weight, 0.0) * term
        s["before"][...] = before
        s["total"][d] = total.astype(BF16)
        far_sends(d)

    def far_finish(d):
        far_counted(d, z if d == 0 else 3 - z, landed_in, "far_r")
        into = jnp.zeros((groups, WIDE), F32)
        for k in range(4):
            gap = z - k if d == 0 else k - z
            weight = jnp.exp(-rate() * (4 * rows * jnp.maximum(gap - 1, 0)).astype(F32))
            into = into + jnp.where(gap > 0, weight, 0.0) * s["far"][d, k].astype(F32)
        mine = q if d == 0 else 3 - q
        s["inc"][...] = s["before"][...] + jnp.exp(-rate() * (rows * mine).astype(F32)) * into

    def lanes(b):
        return pl.ds(pl.multiple_of(b * LANES, LANES), LANES)

    build = functools.partial(build_tables, s["par"], s["rate"], s["taps"])
    later = {1: s["rise"], 2: s["toep"]}
    regroup_filters(decay, res, skip, s["par"], s["gen"])
    loads[0].wait()
    loads[1].wait()

    def gated(b, _):
        s["u"][b] = s["inner"][:, lanes(b)].astype(F32) * s["values"][:, lanes(b)].astype(F32)
        return 0

    lax.fori_loop(0, blocks, gated, 0)
    build({0: s["tail"]}, 0, groups)
    states = (s["rate"], s["e"], s["pre"])
    ahead = conv_in(s["u"], s["z"], s["tail"], *states, s["end"], False)
    ahead(0, blocks // 2)
    pump(4, 4, 1, 0)
    ahead(blocks // 2, blocks)
    near_start(0)
    pump(8, 8, 2, 0)
    build({1: s["rise"]}, 0, groups)
    build({2: s["toep"]}, 0, groups)
    pump(8, 8, 4, 1)
    near_finish(0)
    pump(10, 10, 7, 4)
    far_finish(0)
    pump(12, 12, 8, 5)
    onward = conv_out(s["z"], s["toep"], s["rise"], *states, s["inc"], s["y"], False)
    quarter = blocks // 4
    onward(0, quarter)
    pump(12, 12, 8, 6)
    onward(quarter, 2 * quarter)
    pump(14, 14, 9, 6)
    onward(2 * quarter, 3 * quarter)
    pump(14, 14, 9, 7)
    onward(3 * quarter, blocks)
    pump(15, 15, 10, 9)
    loads[2].wait()
    loads[3].wait()

    def modulate(b, _):
        m = (s["outer"][:, lanes(b)].astype(F32) * s["y"][b]).astype(BF16)
        s["mod"][:, lanes(b)] = m
        s["modt"][pl.ds(pl.multiple_of(b * LANES, LANES), LANES), :] = m.T
        return 0

    lax.fori_loop(0, blocks, modulate, 0)
    pump(15, 15, 10, 10)

    def wg_terms(k):
        sidx, own = ORDER[k]
        g, first = side(own), spot(sidx, 0, 0)
        height = 4 * part
        lhs = pl.ds(pl.multiple_of(first * part, height), height)

        def tile(n, _):
            cols = pl.ds(pl.multiple_of(n * 256, 256), 256)
            t = jnp.dot(s["modt"][lhs, :], s["og"][g, :, cols], preferred_element_type=F32)
            s["part"][g, pl.ds(first, 4), :, cols] = t.astype(BF16).reshape(4, part, 256)
            return 0

        lax.fori_loop(0, channels // 256, tile, 0)
        for yy in (0, 1):
            rc_copy(k, yy).start()

    def rc_copy(k, yy):
        sidx, own = ORDER[k]
        return remote(
            s["part"].at[side(own), spot(sidx, yy, 1 - c)], s["rc"].at[k, yy],
            s["rc_s"].at[0], s["rc_r"].at[k], c_to,
        )

    def ry_copy(k, t):
        return remote(
            s["ys"].at[k, sum_rows(t)], s["ry"].at[k, sum_rows(t)],
            s["ry_s"].at[0], s["ry_r"].at[k, t], y_to,
        )

    def ship_copy(t, own_row):
        r = sum_rows(t)
        if own_row:
            return rz_copy(SHIPPED, t)
        return remote(s["ys"].at[SHIPPED, r], s["ro"].at[r], s["ry_s"].at[0], s["ro_r"].at[t], down_to)

    def wg_ship(first, last, n):
        if first == 0:
            landed_in(s["rc"].at[SHIPPED], s["rc_r"].at[SHIPPED])
        for t in range(first, last):
            r = sum_rows(t)
            for own_row, out, landed in ((False, "ys", s["ro"]), (True, "zs", s["rz"].at[SHIPPED])):
                yy = y if own_row else 1 - y
                term = s["part"][side(ORDER[SHIPPED][1]), spot(1, yy, c), r].astype(F32) + s["rc"][SHIPPED, yy, r].astype(F32)
                if n == 2:
                    ship_copy(t, own_row).wait_recv()
                    term = term + landed[r].astype(F32)
                s[out][SHIPPED, r] = term.astype(BF16)
                ship_copy(t, own_row).start()

    def wg_y(k, first=0, last=RSUB):
        sidx, own = ORDER[k]
        if first == 0:
            landed_in(s["rc"].at[k], s["rc_r"].at[k])
        for t in range(first, last):
            r = sum_rows(t)
            term = s["part"][side(own), spot(sidx, 1 - y, c), r].astype(F32) + s["rc"][k, 1 - y, r].astype(F32)
            s["ys"][k, r] = term.astype(BF16)
            if k == SHIPPED:

                def shipped(t=t, r=r):
                    ship_copy(t, False).wait_recv()
                    s["ys"][SHIPPED, r] = (s["ys"][SHIPPED, r].astype(F32) + s["ro"][r].astype(F32)).astype(BF16)

                when(zm == (1 if t < SHIP else 2))(shipped)
            ry_copy(k, t).start()

    def rz_copy(k, t, back=False):
        r = sum_rows(t)
        if back:
            return remote(s["zs"].at[k, r], s["rb"].at[k // 2, r], s["rz_s"].at[0], s["rb_r"].at[k // 2, t], up_to)
        return remote(s["zs"].at[k, r], s["rz"].at[k, r], s["rz_s"].at[0], s["rz_r"].at[k, t], down_to)

    def fx_copy(k, t):
        r = sum_rows(t)
        return remote(s["zs"].at[k, r], s["wx"].at[r], s["rz_s"].at[0], s["fx_r"].at[0], i, 1 - x)

    scale = 1.0 / math.sqrt(length)

    def wg_z(k, t, n):
        sidx, own = ORDER[k]
        r = sum_rows(t)
        ry_copy(k, t).wait_recv()
        acc = (
            s["part"][side(own), spot(sidx, y, c), r].astype(F32)
            + s["rc"][k, y, r].astype(F32)
            + s["ry"][k, r].astype(F32)
        )
        if (sidx == 0 and n < 3) or (sidx == 1 and n in (1, 2)):
            rz_copy(k, t).wait_recv()
            acc = acc + s["rz"][k, r].astype(F32)
        if sidx == 1 and n == 1:
            rz_copy(k, t, True).wait_recv()
            acc = acc + s["rb"][k // 2, r].astype(F32)
        if own and n == sidx:
            s["wo"][r] = acc * scale
            pltpu.make_async_copy(s["wo"].at[r], weight_out.at[r], s["store"].at[4]).start()
            return
        s["zs"][k, r] = acc.astype(BF16)
        if n > sidx:
            rz_copy(k, t).start()
        elif n < sidx:
            rz_copy(k, t, True).start()
        else:
            fx_copy(k, t).start()

    def wg_last():
        def take():
            landed_in(s["wx"], s["fx_r"].at[0])
            s["wo"][...] = s["wx"][...].astype(F32) * scale
            stores[-1].start()

        when(zm >= 2)(take)

    def wg_drain():
        sent(s["rc"], s["rc_s"].at[0])
        sent(s["ys"], s["ry_s"].at[0])
        when(zm < 2)(functools.partial(sent, s["zs"].at[pl.ds(0, 3)], s["rz_s"].at[0]))
        when(zm >= 2)(functools.partial(sent, s["zs"], s["rz_s"].at[0]))

    width = channels // PIECES

    def piece(n):
        return pl.ds(n * width, width)

    stores = [
        pltpu.make_async_copy(src, dst, s["store"].at[n])
        for n, (src, dst) in enumerate(
            (
                (s["bo"], block_out),
                (s["outer"], outer_out),
                (s["inner"], inner_out),
                (s["values"], value_out),
                (s["wo"], weight_out),
            )
        )
    ]

    def b_copy(n):
        return remote(s["bs"].at[n], s["br"].at[n], s["b_s"].at[0], s["b_r"].at[0], i, 1 - x)

    def projected(g, n):
        return jnp.dot(
            s["mod"][...], s["w"][g, :, :, piece(n)].reshape(channels, width), preferred_element_type=F32
        )

    landed_in(s["og"].at[1 - x], s["og_r"].at[0])
    wg_terms(SHIPPED)
    pump(16, 16, 13, 11)
    wg_terms(1)
    pump(16, 16, 14, 12)
    when(zm == 0)(functools.partial(wg_y, SHIPPED))
    when(zm == 3)(functools.partial(wg_ship, 0, RSUB, 3))
    wg_terms(3)
    pump(16, 16, 15, 13)
    wg_y(3)
    wg_terms(0)
    pump(16, 16, 16, 16)
    w_rest()
    when(zm == 2)(functools.partial(wg_ship, 0, 1, 2))
    when(zm == 3)(functools.partial(wg_y, 1))
    turns = [0] * 4

    sums = [[(at // RSUB, at % RSUB) for at in order] for order in REDUCE]

    def reduce(*counts):
        for n in range(4):
            steps = sums[n][turns[n] : counts[n]]
            turns[n] = max(turns[n], counts[n])

            def go(steps=steps, n=n):
                for k, t in steps:
                    wg_z(k, t, n)

            if steps:
                when(zm == n)(go)

    def gradient(p, _):
        cols = pl.ds(pl.multiple_of(p * 2 * LANES, 2 * LANES), 2 * LANES)
        grad = None
        for g in range(2):
            w = s["w"][g, pl.ds(p * (2 * LANES // part), 2 * LANES // part)].reshape(2 * LANES, channels)
            t = lax.dot_general(s["og"][g], w, (((1,), (1,)), ((), ())), preferred_element_type=F32)
            grad = t if grad is None else grad + t
        gate = s["outer"][:, cols].astype(F32)
        filtered_grad = grad * gate
        s["outer"][:, cols] = (
            grad * jnp.concatenate([s["y"][2 * p], s["y"][2 * p + 1]], axis=1)
        ).astype(BF16)
        s["u"][2 * p] = filtered_grad[:, :LANES]
        s["u"][2 * p + 1] = filtered_grad[:, LANES:]
        return 0

    lax.fori_loop(0, blocks // 2, gradient, 0)
    stores[1].start()
    when(zm == 2)(functools.partial(wg_ship, 1, 2, 2))
    for n in range(PIECES // 2):
        s["bs"][n] = projected(1 - x, n).astype(BF16)
        b_copy(n).start()
    reduce(0, 0, 0, 4)
    when(zm == 2)(functools.partial(wg_ship, 2, 3, 2))
    back = conv_in(s["u"], s["z"], s["tail"], *states, s["end"], True)
    back(0, blocks)
    near_start(1)
    when(zm == 2)(functools.partial(wg_ship, 3, RSUB, 2))
    when(zm < 3)(functools.partial(wg_y, 1))
    wg_y(0)
    reduce(4, 0, 0, 6)
    for n in range(PIECES // 2, PIECES):
        s["bs"][n] = projected(1 - x, n).astype(BF16)
        b_copy(n).start()
    reduce(4, 0, 1, 6)
    near_finish(1)
    reduce(4, 0, 2, 8)
    for n in range(PIECES):
        s["bo"][:, piece(n)] = projected(x, n).astype(BF16)
    reduce(4, 0, 4, 9)
    far_finish(1)
    when(zm == 1)(functools.partial(wg_y, SHIPPED))
    reduce(8, 4, 5, 10)
    home = conv_out(s["z"], s["toep"], s["rise"], *states, s["inc"], s["u"], True)
    home(0, quarter)
    reduce(8, 6, 6, 12)
    home(quarter, 2 * quarter)
    reduce(9, 8, 8, 12)
    home(2 * quarter, 3 * quarter)
    reduce(10, 10, 9, 12)
    home(3 * quarter, blocks)
    reduce(11, 12, 11, 12)

    def grads(b, _):
        gg = s["u"][b]
        gate, value = s["inner"][:, lanes(b)].astype(F32), s["values"][:, lanes(b)].astype(F32)
        s["inner"][:, lanes(b)] = (gg * value).astype(BF16)
        s["values"][:, lanes(b)] = (gg * gate).astype(BF16)
        return 0

    lax.fori_loop(0, blocks, grads, 0)
    stores[2].start()
    stores[3].start()
    reduce(12, 12, 12, 12)
    landed_in(s["br"], s["b_r"].at[0])
    for n in range(PIECES):
        s["bo"][:, piece(n)] = (s["bo"][:, piece(n)].astype(F32) + s["br"][n].astype(F32)).astype(BF16)
    stores[0].start()
    reduce(16, 16, 12, 12)
    wg_last()

    w_drain()
    wg_drain()
    sent(s["og"].at[0], s["og_s"].at[0])
    sent(s["bs"], s["b_s"].at[0])
    for d in (0, 1):
        sent(s["near"].at[d, pl.ds(0, 3)], s["near_s"].at[d])
        far_counted(d, 3 - z if d == 0 else z, sent, "far_s")
    for copy in stores:
        copy.wait()


def fused(outer_gate, inner_gate, values, out_weight, skip_gain, residues, decay_rates, out_grad):
    rows, channels = values.shape
    ctx = lax.axis_size("ctx")
    scratch = fused_scratch(rows, channels)
    shape = jax.ShapeDtypeStruct
    small = pl.BlockSpec(memory_space=pltpu.VMEM)
    large = pl.BlockSpec(memory_space=pl.ANY)
    tile = shape((rows, channels), BF16)
    outs = pl.pallas_call(
        functools.partial(fused_kernel, tuple(scratch), rows * ctx),
        out_shape=[tile] * 4 + [shape(out_weight.shape, F32)],
        in_specs=[small] * 3 + [large] * 5,
        out_specs=[large] * 5,
        scratch_shapes=list(scratch.values()),
        compiler_params=pltpu.CompilerParams(
            collective_id=3, has_side_effects=True, vmem_limit_bytes=VMEM_BYTES
        ),
        cost_estimate=pl.CostEstimate(flops=6 * 2**30, bytes_accessed=10 * 2**20, transcendentals=0),
        name="fused",
    )(decay_rates.T, residues.T, skip_gain[None], outer_gate, inner_gate, values, out_weight, out_grad)
    return hand_over(outs)


def hand_over_kernel(count, *refs):
    ins, outs, held = refs[:count], refs[count : 2 * count], refs[2 * count : 3 * count]
    sems = refs[-1]
    loads = [pltpu.make_async_copy(a, b, sems.at[0, n]) for n, (a, b) in enumerate(zip(ins, held))]
    stores = [pltpu.make_async_copy(a, b, sems.at[1, n]) for n, (a, b) in enumerate(zip(held, outs))]
    for copy in loads:
        copy.start()
    for load, store in zip(loads, stores):
        load.wait()
        store.start()
    for copy in stores:
        copy.wait()


def hand_over(arrays):
    count = len(arrays)
    large = pl.BlockSpec(memory_space=pl.ANY)
    return pl.pallas_call(
        functools.partial(hand_over_kernel, count),
        out_shape=[jax.ShapeDtypeStruct(x.shape, x.dtype) for x in arrays],
        in_specs=[large] * count,
        out_specs=[large] * count,
        scratch_shapes=[pltpu.VMEM(x.shape, x.dtype) for x in arrays] + [pltpu.SemaphoreType.DMA((2, count))],
        compiler_params=pltpu.CompilerParams(vmem_limit_bytes=VMEM_BYTES),
        name="hand_over",
    )(*arrays)


def solution(mesh):
    tile = P("ctx", "fsdp")
    small = dict(mesh.shape) == {"ctx": 16, "fsdp": 2}
    return jax.shard_map(
        fused if small else shards,
        mesh=mesh,
        in_specs=(tile, tile, tile, tile, P("fsdp"), P("fsdp", None), P("fsdp", None), tile),
        out_specs=(tile,) * 5,
        check_vma=False,
    )
```

```python
import functools
import math

import jax
import jax.numpy as jnp
from jax import lax
from jax.experimental import pallas as pl
from jax.experimental.pallas import tpu as pltpu
from jax.sharding import PartitionSpec as P

F32 = jnp.float32
BF16 = jnp.bfloat16
LANES = 128
SEGS = 8
VMEM_BYTES = 62 * 2**20


def rows_at(i, steps):
    return pl.ds(i, SEGS, stride=steps)


def spread(row):
    return jnp.broadcast_to(row, (SEGS, LANES))


def segment_states(u_scr, decay_ref, pre_ref, end_ref, reverse):
    modes = decay_ref.shape[0]
    steps = u_scr.shape[0] // SEGS
    a = [spread(jnp.exp(-decay_ref[r : r + 1, :])) for r in range(modes)]

    def step(k, states):
        i = steps - 1 - k if reverse else k
        u = u_scr[rows_at(i, steps), :]
        return tuple(a[r] * states[r] + u for r in range(modes))

    zero = jnp.zeros((SEGS, LANES), F32)
    states = lax.fori_loop(0, steps, step, (zero,) * modes, unroll=4)
    seg = lax.broadcasted_iota(jnp.int32, (SEGS, LANES), 0)

    def moved(x, by):
        if reverse:
            return jnp.where(seg < SEGS - by, pltpu.roll(x, SEGS - by, 0), 0.0)
        return jnp.where(seg >= by, pltpu.roll(x, by, 0), 0.0)

    last = 0 if reverse else SEGS - 1
    for r in range(modes):
        rate = spread(decay_ref[r : r + 1, :])
        x = states[r]
        for by in (1, 2, 4):
            x = x + jnp.exp(-rate * float(steps * by)) * moved(x, by)
        end_ref[r : r + 1, :] = x[last : last + 1, :]
        pre_ref[r] = moved(x, 1)


def full_scan(u_scr, y_scr, decay_ref, res_ref, pre_ref, incoming_ref, reverse):
    modes = decay_ref.shape[0]
    rows = u_scr.shape[0]
    steps = rows // SEGS
    seg = lax.broadcasted_iota(jnp.int32, (SEGS, LANES), 0)
    ahead = ((SEGS - 1 - seg if reverse else seg) * steps).astype(F32)
    a = []
    first = []
    for r in range(modes):
        rate = spread(decay_ref[r : r + 1, :])
        a.append(jnp.exp(-rate))
        first.append(pre_ref[r] + jnp.exp(-rate * ahead) * incoming_ref[r : r + 1, :])
    res = [spread(res_ref[r : r + 1, :]) for r in range(modes)]

    def step(k, states):
        i = steps - 1 - k if reverse else k
        u = u_scr[rows_at(i, steps), :]
        states = tuple(a[r] * states[r] + u for r in range(modes))
        terms = [res[r] * states[r] for r in range(modes)]
        while len(terms) > 1:
            terms = [p + q for p, q in zip(terms[::2], terms[1::2])]
        y_scr[rows_at(i, steps), :] = terms[0]
        return states

    lax.fori_loop(0, steps, step, tuple(first), unroll=2)


def forward_ends(inner_ref, values_ref, decay_ref, pre_ref, end_ref, u_scr):
    u_scr[...] = inner_ref[...].astype(F32) * values_ref[...].astype(F32)
    segment_states(u_scr, decay_ref, pre_ref, end_ref, False)


def forward_finish(
    inner_ref, values_ref, outer_ref, decay_ref, res_ref, skip_ref, pre_ref, incoming_ref,
    filtered_ref, modulated_ref, u_scr, y_scr,
):
    u_scr[...] = inner_ref[...].astype(F32) * values_ref[...].astype(F32)
    full_scan(u_scr, y_scr, decay_ref, res_ref, pre_ref, incoming_ref, False)
    filtered = y_scr[...] + skip_ref[...] * u_scr[...]
    filtered_ref[...] = filtered
    modulated_ref[...] = (outer_ref[...].astype(F32) * filtered).astype(BF16)


def backward_ends(own_ref, other_ref, outer_ref, decay_ref, pre_ref, end_ref, u_scr):
    grad = own_ref[...].astype(F32) + other_ref[...].astype(F32)
    u_scr[...] = grad * outer_ref[...].astype(F32)
    segment_states(u_scr, decay_ref, pre_ref, end_ref, True)


def backward_finish(
    own_ref, other_ref, outer_ref, inner_ref, values_ref, filtered_ref, decay_ref, res_ref, skip_ref,
    pre_ref, incoming_ref, outer_grad_ref, inner_grad_ref, value_grad_ref, u_scr, y_scr,
):
    grad = own_ref[...].astype(F32) + other_ref[...].astype(F32)
    u_scr[...] = grad * outer_ref[...].astype(F32)
    outer_grad_ref[...] = (grad * filtered_ref[...]).astype(BF16)
    full_scan(u_scr, y_scr, decay_ref, res_ref, pre_ref, incoming_ref, True)
    gated_grad = y_scr[...] + skip_ref[...] * u_scr[...]
    inner_grad_ref[...] = (gated_grad * values_ref[...].astype(F32)).astype(BF16)
    value_grad_ref[...] = (gated_grad * inner_ref[...].astype(F32)).astype(BF16)


def by_lanes(kernel, operands, outs, rows, scans):
    channels = operands[0].shape[-1]

    def spec(x):
        lead = x.shape[:-1]
        return pl.BlockSpec(lead + (LANES,), lambda c, n=len(lead): (0,) * n + (c,))

    work = rows * channels * (24000 if scans > 1 else 16000)
    moved = sum(math.prod(x.shape) * x.dtype.itemsize for x in list(operands) + list(outs))
    return pl.pallas_call(
        kernel,
        grid=(channels // LANES,),
        out_shape=outs,
        in_specs=[spec(x) for x in operands],
        out_specs=[spec(x) for x in outs],
        scratch_shapes=[pltpu.VMEM((rows, LANES), F32)] * scans,
        cost_estimate=pl.CostEstimate(flops=work, bytes_accessed=moved, transcendentals=0),
        name=kernel.__name__,
    )(*operands)


def prefix_kernel(reverse, rows, end_ref, decay_ref, out_ref, sent, got, send_sem, recv_sem):
    me, n = lax.axis_index("ctx"), lax.axis_size("ctx")
    hops = [1 << k for k in range(sent.shape[0])]
    barrier = pltpu.get_barrier_semaphore()
    for hop in hops:
        for peer in (lax.rem(me + hop, n), lax.rem(me + n - hop, n)):
            pl.semaphore_signal(
                barrier, inc=1, device_id={"ctx": peer}, device_id_type=pl.DeviceIdType.MESH
            )
    pl.semaphore_wait(barrier, 2 * len(hops))
    decay = decay_ref[...]
    upto = end_ref[...]
    before = jnp.zeros_like(upto)
    for k, hop in enumerate(hops):
        sent[k] = upto.astype(BF16)
        copy = pltpu.make_async_remote_copy(
            src_ref=sent.at[k],
            dst_ref=got.at[k],
            send_sem=send_sem.at[k],
            recv_sem=recv_sem.at[k],
            device_id={"ctx": lax.rem(me + (n - hop if reverse else hop), n)},
            device_id_type=pl.DeviceIdType.MESH,
        )
        copy.start()
        near = jnp.exp(-decay * float(rows * (hop - 1)))
        far = jnp.exp(-decay * float(rows * hop))
        copy.wait()
        inside = (me + hop < n) if reverse else (me >= hop)
        term = got[k].astype(F32) * jnp.where(inside, 1.0, 0.0)
        before = before + near * term
        upto = upto + far * term
    out_ref[...] = before


def prefix(end, decay, rows, reverse):
    hops = max(1, (lax.axis_size("ctx") - 1).bit_length())
    whole = pl.BlockSpec(memory_space=pltpu.VMEM)
    return pl.pallas_call(
        functools.partial(prefix_kernel, reverse, rows),
        out_shape=jax.ShapeDtypeStruct(end.shape, F32),
        in_specs=[whole, whole],
        out_specs=whole,
        scratch_shapes=[
            pltpu.VMEM((hops,) + end.shape, BF16),
            pltpu.VMEM((hops,) + end.shape, BF16),
            pltpu.SemaphoreType.DMA((hops,)),
            pltpu.SemaphoreType.DMA((hops,)),
        ],
        compiler_params=pltpu.CompilerParams(
            collective_id=2 if reverse else 1, has_side_effects=True
        ),
        cost_estimate=pl.CostEstimate(flops=18 * 10**9, bytes_accessed=0, transcendentals=0),
        name="prefix_back" if reverse else "prefix_ahead",
    )(end, decay)


def shards(outer_gate, inner_gate, values, out_weight, skip_gain, residues, decay_rates, out_grad):
    rows, channels = values.shape
    modes = decay_rates.shape[1]
    ctx, fsdp = lax.axis_size("ctx"), lax.axis_size("fsdp")
    at = lax.axis_index("fsdp")
    swap = [(0, 1), (1, 0)]
    shape = jax.ShapeDtypeStruct
    panel = lax.all_gather(out_weight, "ctx", axis=0, tiled=True)
    decay = decay_rates.T
    res = residues.T
    skip = skip_gain[None]
    state_outs = [shape((modes, SEGS, channels), F32), shape((modes, channels), F32)]
    pre, end = by_lanes(forward_ends, (inner_gate, values, decay), state_outs, rows, 1)
    incoming = prefix(end, decay, rows, False)
    filtered, modulated = by_lanes(
        forward_finish,
        (inner_gate, values, outer_gate, decay, res, skip, pre, incoming),
        [shape((rows, channels), F32), shape((rows, channels), BF16)],
        rows,
        2,
    )
    if fsdp == 2:
        other = lax.ppermute(modulated, "fsdp", swap)
        first = jnp.where(at == 0, modulated, other)
        second = jnp.where(at == 0, other, modulated)
        gathered = jnp.concatenate([first, second], axis=1)
        mine = lax.dynamic_slice_in_dim(panel, at * channels, channels, 0)
        theirs = lax.dynamic_slice_in_dim(panel, (1 - at) * channels, channels, 0)
        for_them = jnp.dot(out_grad, theirs.T, preferred_element_type=F32).astype(BF16)
        from_them = lax.ppermute(for_them, "fsdp", swap)
        own = jnp.dot(out_grad, mine.T, preferred_element_type=F32).astype(BF16)
    else:
        gathered = lax.all_gather(modulated, "fsdp", axis=1, tiled=True)
        partial = jnp.dot(out_grad, panel.T, preferred_element_type=F32).astype(BF16)
        own = lax.psum_scatter(partial, "fsdp", scatter_dimension=1, tiled=True)
        from_them = jnp.zeros_like(own)
    grad_rows = lax.dot_general(
        gathered, out_grad, (((0,), (0,)), ((), ())), preferred_element_type=F32
    ).astype(BF16)
    weight_grad = lax.psum_scatter(grad_rows, "ctx", scatter_dimension=0, tiled=True)
    block_out = jnp.dot(gathered, panel, preferred_element_type=F32).astype(BF16)
    pre, end = by_lanes(
        backward_ends, (own, from_them, outer_gate, decay), state_outs, rows, 1
    )
    incoming = prefix(end, decay, rows, True)
    outer_grad, inner_grad, value_grad = by_lanes(
        backward_finish,
        (own, from_them, outer_gate, inner_gate, values, filtered, decay, res, skip, pre, incoming),
        [shape((rows, channels), BF16)] * 3,
        rows,
        2,
    )
    weight_grad, value_grad = lax.optimization_barrier((weight_grad, value_grad))
    weight_grad = weight_grad.astype(F32) * (1.0 / math.sqrt(rows * ctx))
    return (block_out, outer_grad, inner_grad, value_grad, weight_grad)


TAPS = 16
GRAN = 16
PER = LANES // GRAN
WIDE = TAPS * GRAN
SUB = 2
PIECES = 4
GATHER = (
    (0, 1, 2, 3, 4, 5, 8, 9, 6, 7, 10, 11, 12, 13, 14, 15),
    (0, 1, 2, 3, 4, 5, 8, 9, 6, 7, 10, 11, 12, 13, 14, 15),
    (0, 1, 2, 8, 3, 9, 4, 5, 6, 7, 10, 11, 12, 13, 14, 15),
    (0, 1, 2, 3, 8, 4, 5, 9, 10, 6, 11, 7, 12, 13, 14, 15),
)
RSUB = 4
SHIP = 4
SHIPPED = 2
REDUCE = (
    (8, 9, 10, 11, 0, 1, 2, 3, 12, 13, 14, 15, 4, 5, 6, 7),
    (12, 13, 14, 15, 4, 8, 5, 9, 6, 10, 7, 11, 0, 1, 2, 3),
    (12, 13, 14, 15, 4, 5, 6, 7, 0, 1, 2, 3),
    (12, 13, 14, 15, 4, 5, 6, 7, 0, 1, 2, 3),
)
MESH = pl.DeviceIdType.MESH
ORDER = ((1, True), (0, True), (1, False), (0, False))


def regroup(v):
    lane = lax.broadcasted_iota(jnp.int32, v[0].shape, 1) // GRAN
    v = list(v)
    for m in (1, 2, 4):
        low = (lane & m) == 0
        for i in range(PER):
            if i & m:
                continue
            p, q = v[i], v[i + m]
            v[i] = jnp.where(low, p, pltpu.roll(q, GRAN * m, 1))
            v[i + m] = jnp.where(low, pltpu.roll(p, LANES - GRAN * m, 1), q)
    return v


def row_at(k, s, steps, reverse):
    return TAPS * (steps - 1 - k) + TAPS - 1 - s if reverse else TAPS * k + s


def regroup_filters(decay_ref, res_ref, skip_ref, par_ref, gen_ref):
    row = lax.broadcasted_iota(jnp.int32, (SEGS, LANES), 0)
    lag = lax.broadcasted_iota(jnp.int32, (TAPS, LANES), 0)
    lags = lag.astype(F32)

    def block(b, _):
        cols = pl.ds(pl.multiple_of(b * LANES, LANES), LANES)
        kern = jnp.where(lag == 0, jnp.broadcast_to(skip_ref[:, cols], (TAPS, LANES)), 0.0)
        for r in range(TAPS):
            kern = kern + res_ref[r : r + 1, cols] * jnp.exp(-decay_ref[r : r + 1, cols] * lags)
        gen_ref[...] = kern
        for half in range(2):
            v = []
            for s in range(half * PER, (half + 1) * PER):
                rate = jnp.broadcast_to(decay_ref[s : s + 1, cols], (SEGS, LANES))
                res = jnp.broadcast_to(res_ref[s : s + 1, cols], (SEGS, LANES))
                tap = jnp.broadcast_to(gen_ref[s : s + 1, :], (SEGS, LANES))
                v.append(jnp.where(row == 0, rate, jnp.where(row == 1, res, tap)))
            for h, out in enumerate(regroup(v)):
                par_ref[b * PER + h, :, half * LANES : (half + 1) * LANES] = out
        return 0

    lax.fori_loop(0, decay_ref.shape[1] // LANES, block, 0)


def build_tables(par_ref, rate_ref, taps_ref, outs, first, groups):
    shape = (GRAN, WIDE)
    diagonal = lax.broadcasted_iota(jnp.int32, shape, 1) % GRAN == lax.broadcasted_iota(jnp.int32, shape, 0)
    lag = lax.broadcasted_iota(jnp.int32, (TAPS, WIDE), 0)
    lags = lag.astype(F32)
    at = lax.broadcasted_iota(jnp.int32, (TAPS, WIDE), 1) // GRAN

    def group(n, _):
        for d in range(4):
            g = first + 4 * n + d
            rate = par_ref[g, 0:1, :]
            for i in outs:
                if i == 0:
                    rate_ref[pl.ds(g, 1), :] = rate
                    taps_ref[d, i] = jnp.exp(-rate * (TAPS - 1 - lags))
                elif i == 1:
                    taps_ref[d, i] = par_ref[g, 1:2, :] * jnp.exp(-rate * (lags + 1))
                else:
                    kern = jnp.broadcast_to(par_ref[g, 2:3, :], (TAPS, WIDE))
                    taps_ref[d, i] = jnp.where(at >= lag, pltpu.roll(kern, 0, 1, stride=GRAN, stride_axis=0), 0.0)
        for d in range(4):
            g = first + 4 * n + d
            for i, out in outs.items():
                for s in range(TAPS):
                    line = jnp.broadcast_to(taps_ref[d, i, s : s + 1, :], shape)
                    out[g, s * GRAN : (s + 1) * GRAN, :] = jnp.where(diagonal, line, 0.0).astype(BF16)
        return 0

    lax.fori_loop(0, groups // 4, group, 0)


def moved(x, by, reverse):
    seg = lax.broadcasted_iota(jnp.int32, x.shape, 0)
    if reverse:
        return jnp.where(seg < SEGS - by, pltpu.roll(x, SEGS - by, 0), 0.0)
    return jnp.where(seg >= by, pltpu.roll(x, by, 0), 0.0)


def conv_in(u_ref, z_ref, tail_ref, rate_ref, e_ref, pre_ref, end_ref, reverse):
    blocks, rows, _ = u_ref.shape
    stride = rows // SEGS
    steps = stride // TAPS
    last = 0 if reverse else SEGS - 1

    def split(b):
        for half in range(2):
            for k in range(0, steps, 2):
                pair = [
                    regroup(
                        [
                            u_ref[b, pl.ds(row_at(n, half * PER + j, steps, reverse), SEGS, stride=stride), :]
                            for j in range(PER)
                        ]
                    )
                    for n in (k, k + 1)
                ]
                for h in range(PER):
                    z_ref[b * PER + h, k * SEGS : (k + 2) * SEGS, half * LANES : (half + 1) * LANES] = (
                        jnp.concatenate([pair[0][h], pair[1][h]], axis=0).astype(BF16)
                    )

    def ends(b):
        for h in range(PER):
            g = b * PER + h
            e = jnp.dot(z_ref[g], tail_ref[g], preferred_element_type=F32)
            e_ref[g] = e
            rate = jnp.broadcast_to(rate_ref[pl.ds(g, 1), :], (SEGS, WIDE))
            a = jnp.exp(-rate * float(TAPS))
            x = e[0:SEGS]
            for k in range(1, steps):
                x = a * x + e[k * SEGS : (k + 1) * SEGS]
            for by in (1, 2, 4):
                x = x + jnp.exp(-rate * float(TAPS * steps * by)) * moved(x, by, reverse)
            end_ref[pl.ds(g, 1), :] = x[last : last + 1, :]
            pre_ref[g] = moved(x, 1, reverse)

    return pipelined(split, ends, blocks)


def pipelined(first, second, blocks):
    def body(b, _):
        second(b - 1)
        first(b)
        return 0

    def run(lo, hi):
        if lo == 0:
            first(0)
        lax.fori_loop(max(lo, 1), hi, body, 0)
        if hi == blocks:
            second(blocks - 1)

    return run


def conv_out(z_ref, toep_ref, rise_ref, rate_ref, e_ref, pre_ref, inc_ref, y_ref, reverse):
    groups, chunks, _ = z_ref.shape
    steps = chunks // SEGS
    stride = y_ref.shape[1] // SEGS

    def finish(b):
        seg = lax.broadcasted_iota(jnp.int32, (SEGS, WIDE), 0)
        ahead = ((SEGS - 1 - seg if reverse else seg) * (TAPS * steps)).astype(F32)
        for h in range(PER):
            g = b * PER + h
            rate = jnp.broadcast_to(rate_ref[pl.ds(g, 1), :], (SEGS, WIDE))
            a = jnp.exp(-rate * float(TAPS))
            x = pre_ref[g] + jnp.exp(-rate * ahead) * inc_ref[pl.ds(g, 1), :]
            states = [x]
            for k in range(steps - 1):
                x = a * x + e_ref[g, k * SEGS : (k + 1) * SEGS]
                states.append(x)
            s = jnp.concatenate(states, axis=0).astype(BF16)
            y = jnp.dot(z_ref[g], toep_ref[g], preferred_element_type=F32)
            e_ref[g] = y + lax.dot_general(s, rise_ref[g], (((1,), (1,)), ((), ())), preferred_element_type=F32)

    def merge(b):
        for half in range(2):
            for k in range(steps):
                v = regroup(
                    [
                        e_ref[b * PER + h, k * SEGS : (k + 1) * SEGS, half * LANES : (half + 1) * LANES]
                        for h in range(PER)
                    ]
                )
                for j in range(PER):
                    y_ref[b, pl.ds(row_at(k, half * PER + j, steps, reverse), SEGS, stride=stride), :] = v[j]

    return pipelined(finish, merge, groups // PER)


def fused_scratch(rows, channels):
    blocks, groups = channels // LANES, channels // GRAN
    chunks = rows // TAPS
    part = channels // 8
    dma = pltpu.SemaphoreType.DMA
    v = pltpu.VMEM
    return dict(
        tail=v((groups, WIDE, WIDE), BF16),
        rise=v((groups, WIDE, WIDE), BF16),
        toep=v((groups, WIDE, WIDE), BF16),
        par=v((groups, SEGS, WIDE), F32),
        rate=v((groups, WIDE), F32),
        taps=v((4, 3, TAPS, WIDE), F32),
        gen=v((TAPS, LANES), F32),
        inner=v((rows, channels), BF16),
        values=v((rows, channels), BF16),
        outer=v((rows, channels), BF16),
        og=v((2, rows, channels), BF16),
        w=v((2, 8, part, channels), BF16),
        u=v((blocks, rows, LANES), F32),
        y=v((blocks, rows, LANES), F32),
        z=v((groups, chunks, WIDE), BF16),
        e=v((groups, chunks, WIDE), F32),
        pre=v((groups, SEGS, WIDE), F32),
        end=v((groups, WIDE), F32),
        before=v((groups, WIDE), F32),
        inc=v((groups, WIDE), F32),
        near=v((2, 4, groups, WIDE), BF16),
        total=v((2, groups, WIDE), BF16),
        far=v((2, 4, groups, WIDE), BF16),
        mod=v((rows, channels), BF16),
        modt=v((channels, rows), BF16),
        bs=v((PIECES, rows, channels // PIECES), BF16),
        br=v((PIECES, rows, channels // PIECES), BF16),
        bo=v((rows, channels), BF16),
        part=v((2, 8, part, channels), BF16),
        rc=v((4, 2, part, channels), BF16),
        ys=v((4, part, channels), BF16),
        ry=v((4, part, channels), BF16),
        zs=v((4, part, channels), BF16),
        rz=v((4, part, channels), BF16),
        rb=v((2, part, channels), BF16),
        ro=v((part, channels), BF16),
        wx=v((part, channels), BF16),
        wo=v((part, channels), F32),
        load=dma((5,)),
        store=dma((5,)),
        og_s=dma((1,)),
        og_r=dma((1,)),
        wx_s=dma((1,)),
        w_r=dma((2, 4, SUB)),
        wc_r=dma((1,)),
        up_s=dma((1,)),
        down_s=dma((1,)),
        y_s=dma((1,)),
        c_s=dma((1,)),
        cy_s=dma((1,)),
        near_s=dma((2,)),
        near_r=dma((2,)),
        far_s=dma((2,)),
        far_r=dma((2,)),
        b_s=dma((1,)),
        b_r=dma((1,)),
        rc_s=dma((1,)),
        rc_r=dma((4,)),
        ry_s=dma((1,)),
        ry_r=dma((4, RSUB)),
        rz_s=dma((1,)),
        rz_r=dma((4, RSUB)),
        rb_r=dma((2, RSUB)),
        ro_r=dma((RSUB,)),
        fx_r=dma((1,)),
    )


def fused_kernel(names, length, *refs):
    decay, res, skip, outer_in, inner_in, values_in, weight_in, grad_in = refs[:8]
    block_out, outer_out, inner_out, value_out, weight_out = refs[8:13]
    s = dict(zip(names, refs[13:]))
    rows, channels = inner_in.shape
    part = weight_in.shape[0]
    blocks = channels // LANES
    groups = channels // GRAN
    fine = part // SUB
    i, x = lax.axis_index("ctx"), lax.axis_index("fsdp")
    z, y, c = i // 4, (i // 2) % 2, i % 2
    zm = jnp.where(x == 0, z, 3 - z)
    q = i % 4

    def ctx_at(z, y, c):
        return z * 4 + y * 2 + c

    up_to = ctx_at(z + 1 - 2 * x, y, c)
    down_to = ctx_at(z - 1 + 2 * x, y, c)
    y_to = ctx_at(z, 1 - y, c)
    c_to = ctx_at(z, y, 1 - c)

    def remote(src, dst, send, recv, ctx, fsdp=x):
        return pltpu.make_async_remote_copy(
            src_ref=src, dst_ref=dst, send_sem=send, recv_sem=recv,
            device_id={"ctx": ctx, "fsdp": fsdp}, device_id_type=MESH,
        )

    def when(cond):
        return pl.when(cond)

    def sent(ref, sem):
        remote(ref, ref, sem, s["wc_r"].at[0], c_to).wait_send()

    def landed_in(ref, sem):
        remote(ref, ref, s["wx_s"].at[0], sem, c_to).wait_recv()

    loads = [
        pltpu.make_async_copy(inner_in, s["inner"], s["load"].at[0]),
        pltpu.make_async_copy(values_in, s["values"], s["load"].at[1]),
        pltpu.make_async_copy(outer_in, s["outer"], s["load"].at[2]),
        pltpu.make_async_copy(grad_in, s["og"].at[x], s["load"].at[3]),
    ]
    for copy in loads:
        copy.start()
    jown = (z % 2) * 4 + q
    source = zm < 2
    keep_w = pltpu.make_async_copy(weight_in, s["w"].at[x, jown], s["load"].at[4])
    when(source)(keep_w.start)
    s["far"][...] = jnp.zeros_like(s["far"])

    barrier = pltpu.get_barrier_semaphore()
    peers = [(ctx_at(z, (q + t) % 4 // 2, (q + t) % 2), x) for t in (1, 2, 3)]
    peers += [(ctx_at((z + t) % 4, y, c), x) for t in (1, 2, 3)] + [(i, 1 - x)]
    for ctx, fsdp in peers:
        pl.semaphore_signal(barrier, inc=1, device_id={"ctx": ctx, "fsdp": fsdp}, device_id_type=MESH)
    pl.semaphore_wait(barrier, len(peers))

    def fine_rows(t):
        return pl.ds(t * fine, fine)

    def sum_rows(t):
        return pl.ds(t * (part // RSUB), part // RSUB)

    def spot(sidx, yy, cc):
        return jnp.where(x == 0, sidx, 1 - sidx) * 4 + yy * 2 + cc

    def side(own):
        return x if own else 1 - x

    def w_cross(t):
        return remote(
            weight_in.at[fine_rows(t)], s["w"].at[x, jown, fine_rows(t)], s["wx_s"].at[0],
            s["w_r"].at[x, jown // 2, t], i, 1 - x,
        )

    def w_sends(src, g, j, t, up, down):
        dst = s["w"].at[g, j, fine_rows(t)]
        recv = s["w_r"].at[g, j // 2, t]
        return [
            (up, remote(src, dst, s["up_s"].at[0], recv, up_to)),
            (down, remote(src, dst, s["down_s"].at[0], recv, down_to)),
            (None, remote(src, dst, s["y_s"].at[0], recv, y_to)),
            (None, remote(src, dst, s["c_s"].at[0], s["wc_r"].at[0], c_to)),
        ]

    def each(sends, act):
        for cond, copy in sends:
            if cond is None:
                getattr(copy, act)()
            elif cond is not False:
                when(cond)(getattr(copy, act))

    def place(p, n):
        if n == 0:
            return p // 2, side(p % 2 == 0)
        return 1 - p % 2, side(p < 2)

    def own_sends(t):
        return w_sends(weight_in.at[fine_rows(t)], x, jown, t, None, zm == 1)

    def line_sends(p, t, n):
        sidx, g = place(p, n)
        j = spot(sidx, y, c)
        src = s["w"].at[g, j, fine_rows(t)]
        up = None if n < 3 and (sidx == 0 or n > 0) else False
        return w_sends(src, g, j, t, up, None if sidx == 1 and n == 1 else False)

    def w_wait(g, j, t):
        landed_in(s["w"].at[g, j, fine_rows(t)], s["w_r"].at[g, j // 2, t])

    def pump_line(p, t, n):
        if p == 0 and n < 2:
            return
        sidx, g = place(p, n)
        w_wait(g, spot(sidx, y, c), t)
        each(line_sends(p, t, n), "start")

    def y_pass(p, t, n):
        sidx, g = place(p, n)
        j = spot(sidx, 1 - y, c)
        at = s["w"].at[g, j, fine_rows(t)]
        return remote(at, at, s["cy_s"].at[0], s["wc_r"].at[0], c_to)

    def pump_y(p, t, n):
        sidx, g = place(p, n)
        w_wait(g, spot(sidx, 1 - y, c), t)
        y_pass(p, t, n).start()

    def w_rest():
        landed_in(s["w"].at[0], s["wc_r"].at[0])
        when(source)(keep_w.wait)

    def w_drain():
        def blocks_of(count):
            return s["w"].at[0, pl.ds(0, count)]

        when(zm >= 2)(functools.partial(sent, blocks_of(1), s["wx_s"].at[0]))
        when(zm == 0)(functools.partial(sent, blocks_of(2), s["up_s"].at[0]))
        when((zm == 1) | (zm == 2))(functools.partial(sent, blocks_of(4), s["up_s"].at[0]))
        when(zm == 1)(functools.partial(sent, blocks_of(2), s["down_s"].at[0]))
        for name in ("y_s", "c_s", "cy_s"):
            sent(blocks_of(4), s[name].at[0])

    def start_cross():
        for t in range(SUB):
            w_cross(t).start()

    def start_owned():
        for t in range(SUB):
            each(own_sends(t), "start")

    when(zm >= 2)(start_cross)
    when(source)(start_owned)

    og_copy = remote(grad_in, s["og"].at[x], s["og_s"].at[0], s["og_r"].at[0], i, 1 - x)
    og_copy.start()

    def listed(order):
        parts = 4 * SUB
        return [(pump_line if n < parts else pump_y, n % parts // SUB, n % SUB) for n in order]

    classes = [zm == n for n in range(4)]
    orders = [listed(order) for order in GATHER]
    done = [0] * len(classes)

    def pump(*counts):
        for n, cond in enumerate(classes):
            steps = orders[n][done[n] : counts[n]]
            done[n] = max(done[n], counts[n])

            def go(steps=steps, n=n):
                for act, p, t in steps:
                    act(p, t, n)

            if steps:
                when(cond)(go)

    def rate():
        return s["rate"][...]

    def near_copy(d, t):
        to = (q + t) % 4
        at = s["near"].at[d, q]
        return remote(at, at, s["near_s"].at[d], s["near_r"].at[d], ctx_at(z, to // 2, to % 2))

    def far_copy(d, t):
        to = z + t if d == 0 else z - t
        at = s["far"].at[d, z]
        return remote(s["total"].at[d], at, s["far_s"].at[d], s["far_r"].at[d], ctx_at(to, y, c))

    def far_sends(d):
        for t in (1, 2, 3):
            cond = z + t < 4 if d == 0 else z - t >= 0
            when(cond)(far_copy(d, t).start)

    def far_counted(d, count, act, name):
        for n in (1, 2, 3):
            when(count == n)(functools.partial(act, s["far"].at[d, pl.ds(0, n)], s[name].at[d]))

    def near_start(d):
        s["near"][d, q] = s["end"][...].astype(BF16)
        for t in (1, 2, 3):
            near_copy(d, t).start()

    def near_finish(d):
        landed_in(s["near"].at[d, pl.ds(0, 3)], s["near_r"].at[d])
        total = jnp.zeros((groups, WIDE), F32)
        before = jnp.zeros((groups, WIDE), F32)
        mine = q if d == 0 else 3 - q
        for k in range(4):
            rank = k if d == 0 else 3 - k
            term = s["near"][d, k].astype(F32)
            total = total + jnp.exp(-rate() * float(rows * (3 - rank))) * term
            gap = mine - rank
            weight = jnp.exp(-rate() * (rows * jnp.maximum(gap - 1, 0)).astype(F32))
            before = before + jnp.where(gap > 0, weight, 0.0) * term
        s["before"][...] = before
        s["total"][d] = total.astype(BF16)
        far_sends(d)

    def far_finish(d):
        far_counted(d, z if d == 0 else 3 - z, landed_in, "far_r")
        into = jnp.zeros((groups, WIDE), F32)
        for k in range(4):
            gap = z - k if d == 0 else k - z
            weight = jnp.exp(-rate() * (4 * rows * jnp.maximum(gap - 1, 0)).astype(F32))
            into = into + jnp.where(gap > 0, weight, 0.0) * s["far"][d, k].astype(F32)
        mine = q if d == 0 else 3 - q
        s["inc"][...] = s["before"][...] + jnp.exp(-rate() * (rows * mine).astype(F32)) * into

    def lanes(b):
        return pl.ds(pl.multiple_of(b * LANES, LANES), LANES)

    build = functools.partial(build_tables, s["par"], s["rate"], s["taps"])
    later = {1: s["rise"], 2: s["toep"]}
    regroup_filters(decay, res, skip, s["par"], s["gen"])
    loads[0].wait()
    loads[1].wait()

    def gated(b, _):
        s["u"][b] = s["inner"][:, lanes(b)].astype(F32) * s["values"][:, lanes(b)].astype(F32)
        return 0

    lax.fori_loop(0, blocks, gated, 0)
    build({0: s["tail"]}, 0, groups)
    states = (s["rate"], s["e"], s["pre"])
    ahead = conv_in(s["u"], s["z"], s["tail"], *states, s["end"], False)
    ahead(0, blocks // 2)
    pump(4, 4, 1, 0)
    ahead(blocks // 2, blocks)
    near_start(0)
    pump(8, 8, 2, 0)
    build({1: s["rise"]}, 0, groups)
    build({2: s["toep"]}, 0, groups)
    pump(8, 8, 4, 1)
    near_finish(0)
    pump(10, 10, 7, 4)
    far_finish(0)
    pump(12, 12, 8, 5)
    onward = conv_out(s["z"], s["toep"], s["rise"], *states, s["inc"], s["y"], False)
    quarter = blocks // 4
    onward(0, quarter)
    pump(12, 12, 8, 6)
    onward(quarter, 2 * quarter)
    pump(14, 14, 9, 6)
    onward(2 * quarter, 3 * quarter)
    pump(14, 14, 9, 7)
    onward(3 * quarter, blocks)
    pump(15, 15, 10, 9)
    loads[2].wait()
    loads[3].wait()

    def modulate(b, _):
        m = (s["outer"][:, lanes(b)].astype(F32) * s["y"][b]).astype(BF16)
        s["mod"][:, lanes(b)] = m
        s["modt"][pl.ds(pl.multiple_of(b * LANES, LANES), LANES), :] = m.T
        return 0

    lax.fori_loop(0, blocks, modulate, 0)
    pump(15, 15, 10, 10)

    def wg_terms(k):
        sidx, own = ORDER[k]
        g, first = side(own), spot(sidx, 0, 0)
        height = 4 * part
        lhs = pl.ds(pl.multiple_of(first * part, height), height)

        def tile(n, _):
            cols = pl.ds(pl.multiple_of(n * 256, 256), 256)
            t = jnp.dot(s["modt"][lhs, :], s["og"][g, :, cols], preferred_element_type=F32)
            s["part"][g, pl.ds(first, 4), :, cols] = t.astype(BF16).reshape(4, part, 256)
            return 0

        lax.fori_loop(0, channels // 256, tile, 0)
        for yy in (0, 1):
            rc_copy(k, yy).start()

    def rc_copy(k, yy):
        sidx, own = ORDER[k]
        return remote(
            s["part"].at[side(own), spot(sidx, yy, 1 - c)], s["rc"].at[k, yy],
            s["rc_s"].at[0], s["rc_r"].at[k], c_to,
        )

    def ry_copy(k, t):
        return remote(
            s["ys"].at[k, sum_rows(t)], s["ry"].at[k, sum_rows(t)],
            s["ry_s"].at[0], s["ry_r"].at[k, t], y_to,
        )

    def ship_copy(t, own_row):
        r = sum_rows(t)
        if own_row:
            return rz_copy(SHIPPED, t)
        return remote(s["ys"].at[SHIPPED, r], s["ro"].at[r], s["ry_s"].at[0], s["ro_r"].at[t], down_to)

    def wg_ship(first, last, n):
        if first == 0:
            landed_in(s["rc"].at[SHIPPED], s["rc_r"].at[SHIPPED])
        for t in range(first, last):
            r = sum_rows(t)
            for own_row, out, landed in ((False, "ys", s["ro"]), (True, "zs", s["rz"].at[SHIPPED])):
                yy = y if own_row else 1 - y
                term = s["part"][side(ORDER[SHIPPED][1]), spot(1, yy, c), r].astype(F32) + s["rc"][SHIPPED, yy, r].astype(F32)
                if n == 2:
                    ship_copy(t, own_row).wait_recv()
                    term = term + landed[r].astype(F32)
                s[out][SHIPPED, r] = term.astype(BF16)
                ship_copy(t, own_row).start()

    def wg_y(k, first=0, last=RSUB):
        sidx, own = ORDER[k]
        if first == 0:
            landed_in(s["rc"].at[k], s["rc_r"].at[k])
        for t in range(first, last):
            r = sum_rows(t)
            term = s["part"][side(own), spot(sidx, 1 - y, c), r].astype(F32) + s["rc"][k, 1 - y, r].astype(F32)
            s["ys"][k, r] = term.astype(BF16)
            if k == SHIPPED:

                def shipped(t=t, r=r):
                    ship_copy(t, False).wait_recv()
                    s["ys"][SHIPPED, r] = (s["ys"][SHIPPED, r].astype(F32) + s["ro"][r].astype(F32)).astype(BF16)

                when(zm == (1 if t < SHIP else 2))(shipped)
            ry_copy(k, t).start()

    def rz_copy(k, t, back=False):
        r = sum_rows(t)
        if back:
            return remote(s["zs"].at[k, r], s["rb"].at[k // 2, r], s["rz_s"].at[0], s["rb_r"].at[k // 2, t], up_to)
        return remote(s["zs"].at[k, r], s["rz"].at[k, r], s["rz_s"].at[0], s["rz_r"].at[k, t], down_to)

    def fx_copy(k, t):
        r = sum_rows(t)
        return remote(s["zs"].at[k, r], s["wx"].at[r], s["rz_s"].at[0], s["fx_r"].at[0], i, 1 - x)

    scale = 1.0 / math.sqrt(length)

    def wg_z(k, t, n):
        sidx, own = ORDER[k]
        r = sum_rows(t)
        ry_copy(k, t).wait_recv()
        acc = (
            s["part"][side(own), spot(sidx, y, c), r].astype(F32)
            + s["rc"][k, y, r].astype(F32)
            + s["ry"][k, r].astype(F32)
        )
        if (sidx == 0 and n < 3) or (sidx == 1 and n in (1, 2)):
            rz_copy(k, t).wait_recv()
            acc = acc + s["rz"][k, r].astype(F32)
        if sidx == 1 and n == 1:
            rz_copy(k, t, True).wait_recv()
            acc = acc + s["rb"][k // 2, r].astype(F32)
        if own and n == sidx:
            s["wo"][r] = acc * scale
            return
        s["zs"][k, r] = acc.astype(BF16)
        if n > sidx:
            rz_copy(k, t).start()
        elif n < sidx:
            rz_copy(k, t, True).start()
        else:
            fx_copy(k, t).start()

    def wg_last():
        def take():
            landed_in(s["wx"], s["fx_r"].at[0])
            s["wo"][...] = s["wx"][...].astype(F32) * scale

        when(zm >= 2)(take)
        stores[-1].start()

    def wg_drain():
        sent(s["rc"], s["rc_s"].at[0])
        sent(s["ys"], s["ry_s"].at[0])
        when(zm < 2)(functools.partial(sent, s["zs"].at[pl.ds(0, 3)], s["rz_s"].at[0]))
        when(zm >= 2)(functools.partial(sent, s["zs"], s["rz_s"].at[0]))

    width = channels // PIECES

    def piece(n):
        return pl.ds(n * width, width)

    stores = [
        pltpu.make_async_copy(src, dst, s["store"].at[n])
        for n, (src, dst) in enumerate(
            (
                (s["bo"], block_out),
                (s["outer"], outer_out),
                (s["inner"], inner_out),
                (s["values"], value_out),
                (s["wo"], weight_out),
            )
        )
    ]

    def b_copy(n):
        return remote(s["bs"].at[n], s["br"].at[n], s["b_s"].at[0], s["b_r"].at[0], i, 1 - x)

    def projected(g, n):
        return jnp.dot(
            s["mod"][...], s["w"][g, :, :, piece(n)].reshape(channels, width), preferred_element_type=F32
        )

    landed_in(s["og"].at[1 - x], s["og_r"].at[0])
    wg_terms(SHIPPED)
    pump(16, 16, 13, 11)
    wg_terms(1)
    pump(16, 16, 14, 12)
    when(zm == 0)(functools.partial(wg_y, SHIPPED))
    when(zm == 3)(functools.partial(wg_ship, 0, RSUB, 3))
    wg_terms(3)
    pump(16, 16, 15, 13)
    wg_y(3)
    wg_terms(0)
    pump(16, 16, 16, 16)
    w_rest()
    when(zm == 2)(functools.partial(wg_ship, 0, 1, 2))
    when(zm == 3)(functools.partial(wg_y, 1))
    turns = [0] * 4

    sums = [[(at // RSUB, at % RSUB) for at in order] for order in REDUCE]

    def reduce(*counts):
        for n in range(4):
            steps = sums[n][turns[n] : counts[n]]
            turns[n] = max(turns[n], counts[n])

            def go(steps=steps, n=n):
                for k, t in steps:
                    wg_z(k, t, n)

            if steps:
                when(zm == n)(go)

    def gradient(p, _):
        cols = pl.ds(pl.multiple_of(p * 2 * LANES, 2 * LANES), 2 * LANES)
        grad = None
        for g in range(2):
            w = s["w"][g, pl.ds(p * (2 * LANES // part), 2 * LANES // part)].reshape(2 * LANES, channels)
            t = lax.dot_general(s["og"][g], w, (((1,), (1,)), ((), ())), preferred_element_type=F32)
            grad = t if grad is None else grad + t
        gate = s["outer"][:, cols].astype(F32)
        filtered_grad = grad * gate
        s["outer"][:, cols] = (
            grad * jnp.concatenate([s["y"][2 * p], s["y"][2 * p + 1]], axis=1)
        ).astype(BF16)
        s["u"][2 * p] = filtered_grad[:, :LANES]
        s["u"][2 * p + 1] = filtered_grad[:, LANES:]
        return 0

    lax.fori_loop(0, blocks // 2, gradient, 0)
    stores[1].start()
    when(zm == 2)(functools.partial(wg_ship, 1, 2, 2))
    for n in range(PIECES // 2):
        s["bs"][n] = projected(1 - x, n).astype(BF16)
        b_copy(n).start()
    reduce(0, 0, 0, 4)
    when(zm == 2)(functools.partial(wg_ship, 2, 3, 2))
    back = conv_in(s["u"], s["z"], s["tail"], *states, s["end"], True)
    back(0, blocks)
    near_start(1)
    when(zm == 2)(functools.partial(wg_ship, 3, RSUB, 2))
    when(zm < 3)(functools.partial(wg_y, 1))
    wg_y(0)
    reduce(4, 0, 0, 6)
    for n in range(PIECES // 2, PIECES):
        s["bs"][n] = projected(1 - x, n).astype(BF16)
        b_copy(n).start()
    reduce(4, 0, 1, 6)
    near_finish(1)
    reduce(4, 0, 2, 8)
    for n in range(PIECES):
        s["bo"][:, piece(n)] = projected(x, n).astype(BF16)
    reduce(4, 0, 4, 9)
    far_finish(1)
    when(zm == 1)(functools.partial(wg_y, SHIPPED))
    reduce(8, 4, 5, 10)
    home = conv_out(s["z"], s["toep"], s["rise"], *states, s["inc"], s["u"], True)
    home(0, quarter)
    reduce(8, 6, 6, 12)
    home(quarter, 2 * quarter)
    reduce(9, 8, 8, 12)
    home(2 * quarter, 3 * quarter)
    reduce(10, 11, 9, 12)
    home(3 * quarter, blocks)
    reduce(11, 12, 11, 12)

    def grads(b, _):
        gg = s["u"][b]
        gate, value = s["inner"][:, lanes(b)].astype(F32), s["values"][:, lanes(b)].astype(F32)
        s["inner"][:, lanes(b)] = (gg * value).astype(BF16)
        s["values"][:, lanes(b)] = (gg * gate).astype(BF16)
        return 0

    lax.fori_loop(0, blocks, grads, 0)
    stores[2].start()
    stores[3].start()
    reduce(12, 12, 12, 12)
    landed_in(s["br"], s["b_r"].at[0])
    for n in range(PIECES):
        s["bo"][:, piece(n)] = (s["bo"][:, piece(n)].astype(F32) + s["br"][n].astype(F32)).astype(BF16)
    stores[0].start()
    reduce(16, 16, 12, 12)
    wg_last()

    w_drain()
    wg_drain()
    sent(s["og"].at[0], s["og_s"].at[0])
    sent(s["bs"], s["b_s"].at[0])
    for d in (0, 1):
        sent(s["near"].at[d, pl.ds(0, 3)], s["near_s"].at[d])
        far_counted(d, 3 - z if d == 0 else z, sent, "far_s")
    for copy in stores:
        copy.wait()


def fused(outer_gate, inner_gate, values, out_weight, skip_gain, residues, decay_rates, out_grad):
    rows, channels = values.shape
    ctx = lax.axis_size("ctx")
    scratch = fused_scratch(rows, channels)
    shape = jax.ShapeDtypeStruct
    small = pl.BlockSpec(memory_space=pltpu.VMEM)
    large = pl.BlockSpec(memory_space=pl.ANY)
    tile = shape((rows, channels), BF16)
    outs = pl.pallas_call(
        functools.partial(fused_kernel, tuple(scratch), rows * ctx),
        out_shape=[tile] * 4 + [shape(out_weight.shape, F32)],
        in_specs=[small] * 3 + [large] * 5,
        out_specs=[large] * 5,
        scratch_shapes=list(scratch.values()),
        compiler_params=pltpu.CompilerParams(
            collective_id=3, has_side_effects=True, vmem_limit_bytes=VMEM_BYTES
        ),
        cost_estimate=pl.CostEstimate(flops=6 * 2**30, bytes_accessed=10 * 2**20, transcendentals=0),
        name="fused",
    )(decay_rates.T, residues.T, skip_gain[None], outer_gate, inner_gate, values, out_weight, out_grad)
    return hand_over(outs)


def hand_over_kernel(count, *refs):
    ins, outs, held = refs[:count], refs[count : 2 * count], refs[2 * count : 3 * count]
    sems = refs[-1]
    loads = [pltpu.make_async_copy(a, b, sems.at[0, n]) for n, (a, b) in enumerate(zip(ins, held))]
    stores = [pltpu.make_async_copy(a, b, sems.at[1, n]) for n, (a, b) in enumerate(zip(held, outs))]
    for copy in loads:
        copy.start()
    for load, store in zip(loads, stores):
        load.wait()
        store.start()
    for copy in stores:
        copy.wait()


def hand_over(arrays):
    count = len(arrays)
    large = pl.BlockSpec(memory_space=pl.ANY)
    return pl.pallas_call(
        functools.partial(hand_over_kernel, count),
        out_shape=[jax.ShapeDtypeStruct(x.shape, x.dtype) for x in arrays],
        in_specs=[large] * count,
        out_specs=[large] * count,
        scratch_shapes=[pltpu.VMEM(x.shape, x.dtype) for x in arrays] + [pltpu.SemaphoreType.DMA((2, count))],
        compiler_params=pltpu.CompilerParams(vmem_limit_bytes=VMEM_BYTES),
        name="hand_over",
    )(*arrays)


def solution(mesh):
    tile = P("ctx", "fsdp")
    small = dict(mesh.shape) == {"ctx": 16, "fsdp": 2}
    return jax.shard_map(
        fused if small else shards,
        mesh=mesh,
        in_specs=(tile, tile, tile, tile, P("fsdp"), P("fsdp", None), P("fsdp", None), tile),
        out_specs=(tile,) * 5,
        check_vma=False,
    )
```
